32 devices in a mesh: seq: 8 (over y, x, core), tp: 4 (over z).
Axes of the slice: x: 2, y: 2, z: 4, core: 2. Of those that a mesh axis runs over, the one named last changes fastest.
Arguments:
- stream: bfloat16 [16384, 1024], P(('seq', 'tp')), may hold values from -6 to 6
- segments: int32 [16384], replicated, may hold values from 0 to 63, never falling along the last dimension, each value on 1 to 1024 neighbouring positions
- skip_values: bfloat16 [16384, 512], P('seq', 'tp'), may hold values from -6 to 6
- first_gain: float32 [1024], replicated, may hold values from 0.5 to 1.5
- first_shift: float32 [1024], replicated, may hold values from -1.75 to 1.75
- query_weight: bfloat16 [1024, 1024], P(None, 'tp'), may hold values from -0.1875 to 0.1875
- query_bias: float32 [1024], P('tp'), may hold values from -3 to 3
- key_weight: bfloat16 [1024, 1024], P(None, 'tp'), may hold values from -0.1875 to 0.1875
- value_weight: bfloat16 [1024, 512], P(None, 'tp'), may hold values from -0.1875 to 0.1875
- value_bias: float32 [512], P('tp'), may hold values from -3 to 3
- mixing_weight: bfloat16 [1024, 1024], P('tp'), may hold values from -1.5 to 1.5
- mixing_bias: float32 [1024], replicated, may hold values from -1.75 to 1.75
- second_gain: float32 [1024], replicated, may hold values from 0.5 to 1.5
- second_shift: float32 [1024], replicated, may hold values from -1.75 to 1.75
- up_weight: bfloat16 [1024, 4096], P(None, 'tp'), may hold values from -0.1875 to 0.1875
- up_bias: float32 [4096], P('tp'), may hold values from -3 to 3
- down_weight: bfloat16 [4096, 1024], P('tp'), may hold values from -0.09375 to 0.09375
- down_bias: float32 [1024], replicated, may hold values from -1.75 to 1.75
- cotangent: bfloat16 [16384, 1024], P(('seq', 'tp')), may hold values from -6 to 6
Outputs:
- output: bfloat16 [16384, 1024], P(('seq', 'tp'))
- stream_gradient: float32 [16384, 1024], P(('seq', 'tp'))
- skip_gradient: float32 [16384, 512], P('seq', 'tp')
- query_gradient: float32 [1024, 1024], P('seq', 'tp')
- query_bias_gradient: float32 [1024], replicated
- key_gradient: float32 [1024, 1024], P('seq', 'tp')
- value_gradient: float32 [1024, 512], P('seq', 'tp')
- value_bias_gradient: float32 [512], replicated
- mixing_gradient: float32 [1024, 1024], P('tp', 'seq')
- mixing_bias_gradient: float32 [1024], replicated
- first_gain_gradient: float32 [1024], replicated
- first_shift_gradient: float32 [1024], replicated
- second_gain_gradient: float32 [1024], replicated
- second_shift_gradient: float32 [1024], replicated
- up_gradient: float32 [1024, 4096], P('seq', 'tp')
- up_bias_gradient: float32 [4096], replicated
- down_gradient: float32 [4096, 1024], P('tp', 'seq')
- down_bias_gradient: float32 [1024], replicated
The draws below stay inside these ranges and needn't reach their ends.
Inputs may be any that keep to these rules, and one draw needn't show every extreme that they name: `segments`: segment numbers never fall along the stream; each document spans 1 to 1024 tokens, and some document spans exactly 1024.
All inputs are finite; a program needn't handle non-finite values.
Results may differ from the reference program's by a relative error of at most 0.012.
Values may be sent and summed in bfloat16 or wider, within the bound.
No kernel may reach another device: no remote copies, remote signals or barrier semaphores. Data moves between devices by JAX's collectives and lax.ppermute only.
A program may use at most 128 MiB of HBM per device.

```python
import math
import jax
import jax.numpy as jnp
import numpy as np
from jax import lax

D = 1024
HEAD = 64
FF = 4096
VALUE_WIDTH = 512
QUERY_BLOCK = 512
DOC_MAX = 1024
TOKENS = 16384


def strengthened(entries, stream_key, source, target, blocks, factor):
    def block_of(dim):
        return (jnp.arange(entries.shape[dim]) // (entries.shape[dim] // blocks)).reshape((-1,) + (1,) * (entries.ndim - 1 - dim))

    one_side = jax.random.permutation(stream_key, blocks)[block_of(target)]
    other_side = (block_of(target) + blocks // 2) % blocks
    return jnp.where((block_of(source) == one_side) | (block_of(source) == other_side), factor * entries, entries)


def levels(own_key, dims, cuts, least, high):
    factor_of = 1.0
    for position, shards_of in cuts:
        heights = jax.random.uniform(jax.random.fold_in(jax.random.fold_in(own_key, 6), position), (shards_of,), jnp.float32, least / len(cuts), high / len(cuts))
        factor_of = factor_of * jnp.repeat(jnp.exp(heights), dims[position] // shards_of).reshape((-1,) + (1,) * (len(dims) - 1 - position))
    return factor_of


def split_up(number_of, total, reach, skew):
    portions = [(1 << 20) // math.isqrt(grade ** skew) + 1 for grade in range(2, number_of + 1)]
    surplus, holding = total - reach - (number_of - 1), [1] * (number_of - 1)
    while surplus > 0:
        free = [i for i in range(number_of - 1) if holding[i] < reach]
        whole, budget = sum([portions[i] for i in free]), surplus
        for i in free:
            addition = min(reach - holding[i], max(1, budget * portions[i] // whole), surplus)
            holding[i] = holding[i] + addition
            surplus = surplus - addition
    return np.array([reach] + holding)


def uneven(key, amount, total, bound, slope):
    if amount == 2:
        one = jax.random.randint(key, (), max(1, total - bound), min(bound, total - 1) + 1)
        return jnp.stack([one, total - one])
    sizes = jnp.asarray(split_up(amount, total, bound, slope), jnp.int32)
    pairs = (amount - 1) // 2
    donor, taker = sizes[1:1 + 2 * pairs:2], sizes[2:2 + 2 * pairs:2]
    slack = jnp.minimum(donor - 1, bound - taker)
    shifted = jax.random.randint(jax.random.fold_in(key, 1), (pairs,), 0, 1 << 20) % (slack + 1)
    sizes = sizes.at[1:1 + 2 * pairs:2].set(donor - shifted).at[2:2 + 2 * pairs:2].set(taker + shifted)
    return sizes[jax.random.permutation(jax.random.fold_in(key, 2), amount)]


def scatter_about(stream_key, extent, width, limit, cuts=(), held_as=jnp.bfloat16):
    level = levels(stream_key, extent, cuts, -0.22, 0.18) if cuts else 1.0
    drawn = jax.random.normal(stream_key, extent, jnp.float32) * width * level
    return jnp.minimum(jnp.maximum(drawn, -limit), limit).astype(held_as)


def noise_with(rng, shape, spread, bound, cuts, heavy, kind=jnp.bfloat16):
    values = spread * jax.random.normal(rng, shape, jnp.float32)
    if cuts:
        values = values * levels(rng, shape, cuts, -0.22, 0.18)
    return jnp.clip(strengthened(values, jax.random.fold_in(rng, 3), *heavy), -bound, bound).astype(kind)


def setup_inputs(seed: int = 0) -> dict:
    arg_keys = jax.random.split(jax.random.key(seed), 20)
    stream = scatter_about(arg_keys[0], (TOKENS, D), 1.0, 6.0, ((0, 32),))
    segments = jnp.searchsorted(jnp.cumsum(uneven(arg_keys[1], 4 * TOKENS // DOC_MAX, TOKENS, DOC_MAX, 1)), jnp.arange(TOKENS), side="right").astype(jnp.int32)
    skip_values = scatter_about(arg_keys[2], (TOKENS, VALUE_WIDTH), 1.0, 6.0, ((0, 8), (1, 4)))
    first_gain = jnp.clip(1.0 + 0.1 * jax.random.normal(arg_keys[3], (D,), jnp.float32), 0.5, 1.5)
    first_shift = scatter_about(arg_keys[4], (D,), 0.3, 1.75, (), jnp.float32)
    query_weight = scatter_about(arg_keys[5], (D, D), D ** -0.5, 0.1875, ((1, 4),))
    query_bias = scatter_about(arg_keys[6], (D,), 0.5, 3.0, ((0, 4),), jnp.float32)
    key_weight = scatter_about(arg_keys[7], (D, D), D ** -0.5, 0.1875, ((1, 4),))
    value_weight = scatter_about(arg_keys[8], (D, VALUE_WIDTH), D ** -0.5, 0.1875, ((1, 4),))
    value_bias = scatter_about(arg_keys[9], (VALUE_WIDTH,), 0.5, 3.0, ((0, 4),), jnp.float32)
    mixing_weight = scatter_about(arg_keys[10], (D, D), (D // 64) ** -0.5, 1.5, ((0, 4),))
    mixing_bias = scatter_about(arg_keys[11], (D,), 0.3, 1.75, (), jnp.float32)
    second_gain = jnp.clip(1.0 + 0.1 * jax.random.normal(arg_keys[12], (D,), jnp.float32), 0.5, 1.5)
    second_shift = scatter_about(arg_keys[13], (D,), 0.3, 1.75, (), jnp.float32)
    up_weight = scatter_about(arg_keys[14], (D, FF), D ** -0.5, 0.1875, ((1, 4),))
    up_bias = scatter_about(arg_keys[15], (FF,), 0.5, 3.0, ((0, 4),), jnp.float32)
    down_weight = scatter_about(arg_keys[16], (FF, D), FF ** -0.5, 0.09375, ((0, 4),))
    down_bias = scatter_about(arg_keys[17], (D,), 0.3, 1.75, (), jnp.float32)
    cotangent = noise_with(arg_keys[18], (TOKENS, D), 1.0, 6.0, ((0, 32),), (0, 1, 32, 2.75))
    return dict(stream=stream, segments=segments, skip_values=skip_values, first_gain=first_gain, first_shift=first_shift, query_weight=query_weight, query_bias=query_bias, key_weight=key_weight, value_weight=value_weight, value_bias=value_bias, mixing_weight=mixing_weight, mixing_bias=mixing_bias, second_gain=second_gain, second_shift=second_shift, up_weight=up_weight, up_bias=up_bias, down_weight=down_weight, down_bias=down_bias, cotangent=cotangent)


epsilon = 1e-05

@jax.custom_vjp
def low(v):
    return lax.optimization_barrier(v.astype(jnp.bfloat16)).astype(jnp.float32)

@jax.custom_vjp
def low_back(v):
    return v

def low_keep(v):
    return (low(v), None)

def low_pass(kept, grad):
    return (grad,)

def back_keep(v):
    return (v, None)

def back_low(kept, grad):
    return (low(grad),)
low.defvjp(low_keep, low_pass)
low_back.defvjp(back_keep, back_low)

def layer_norm(matrix, scale_gain, scale_shift):
    average = lax.optimization_barrier(jnp.mean(matrix, axis=-1, keepdims=True))
    centered = matrix - average
    inverse = lax.rsqrt(lax.optimization_barrier(jnp.mean(centered * centered, axis=-1, keepdims=True)) + epsilon)
    return centered * inverse * scale_gain + scale_shift

def matmul(first_operand, second_operand):
    return jnp.dot(first_operand, second_operand, precision=lax.Precision.HIGHEST)

def merge_values(fresh, reused):
    row_count = fresh.shape[0]
    groups = fresh.shape[1] // (2 * HEAD)
    paired = jnp.stack((fresh.reshape(row_count, groups, 2 * HEAD), reused.reshape(row_count, groups, 2 * HEAD)), axis=2)
    return paired.reshape(row_count, 4 * groups * HEAD)

def attend_block(query_block, key_window, value_window, segment_query, segment_key):
    row_count = query_block.shape[0]
    window = key_window.shape[0]
    heads = query_block.shape[1] // HEAD
    scores = jnp.einsum('qhd,khd->hqk', query_block.reshape(row_count, heads, HEAD), key_window.reshape(window, heads, HEAD), precision=lax.Precision.HIGHEST) * HEAD ** (-0.5)
    scores = low_back(scores)
    allowed = (segment_query[:, None] == segment_key[None, :]) & (jnp.arange(window)[None, :] <= jnp.arange(row_count)[:, None] + DOC_MAX)
    scores = jnp.where(allowed[None], scores, -1e+30)
    maximum = lax.optimization_barrier(jnp.max(scores, axis=-1, keepdims=True))
    exponent = jnp.exp(scores - maximum)
    probability = low(exponent / lax.optimization_barrier(jnp.sum(exponent, axis=-1, keepdims=True)))
    mixed = jnp.einsum('hqk,khd->qhd', probability, value_window.reshape(window, heads, HEAD), precision=lax.Precision.HIGHEST)
    return mixed.reshape(row_count, heads * HEAD)

def attention(query, keys, values, segments):
    padding = jnp.zeros((DOC_MAX, D), jnp.float32)
    keys_ext = jnp.concatenate((padding, keys), axis=0)
    values_ext = jnp.concatenate((padding, values), axis=0)
    segment_ext = jnp.concatenate((jnp.full((DOC_MAX,), -1, jnp.int32), segments.astype(jnp.int32)))
    window = DOC_MAX + QUERY_BLOCK
    checked = jax.checkpoint(attend_block)

    def one_block(block_index):
        row_start = block_index * QUERY_BLOCK
        return checked(lax.dynamic_slice_in_dim(query, row_start, QUERY_BLOCK, 0), lax.dynamic_slice_in_dim(keys_ext, row_start, window, 0), lax.dynamic_slice_in_dim(values_ext, row_start, window, 0), lax.dynamic_slice_in_dim(segment_ext, row_start + DOC_MAX, QUERY_BLOCK, 0), lax.dynamic_slice_in_dim(segment_ext, row_start, window, 0))
    blocks = lax.map(one_block, jnp.arange(TOKENS // QUERY_BLOCK, dtype=jnp.int32))
    return blocks.reshape(TOKENS, D)

def reference(stream, segments, skip_values, first_gain, first_shift, query_weight, query_bias, key_weight, value_weight, value_bias, mixing_weight, mixing_bias, second_gain, second_shift, up_weight, up_bias, down_weight, down_bias, cotangent):

    def forward(stream, skip_values, first_gain, first_shift, query_weight, query_bias, key_weight, value_weight, value_bias, mixing_weight, mixing_bias, second_gain, second_shift, up_weight, up_bias, down_weight, down_bias):
        first_normed = low(layer_norm(stream, first_gain, first_shift))
        query = low_back(low(matmul(first_normed, query_weight) + query_bias))
        keys = low_back(low(matmul(first_normed, key_weight)))
        fresh = low_back(low(matmul(first_normed, value_weight) + value_bias))
        values = merge_values(fresh, skip_values)
        attended = low_back(low(attention(query, keys, values, segments)))
        middle = stream + low_back(matmul(attended, mixing_weight)) + mixing_bias
        second_normed = low(layer_norm(middle, second_gain, second_shift))
        hidden = low_back(matmul(second_normed, up_weight) + up_bias)
        activated = low(jax.nn.gelu(hidden, approximate=True))
        return middle + low_back(matmul(activated, down_weight)) + down_bias
    floats = tuple((argument.astype(jnp.float32) for argument in (stream, skip_values, first_gain, first_shift, query_weight, query_bias, key_weight, value_weight, value_bias, mixing_weight, mixing_bias, second_gain, second_shift, up_weight, up_bias, down_weight, down_bias)))
    result, pullback = jax.vjp(forward, *floats)
    gradients = pullback(cotangent.astype(jnp.float32))
    return (result.astype(jnp.bfloat16), gradients[0], gradients[1], gradients[4], gradients[5], gradients[6], gradients[7], gradients[8], gradients[9], gradients[10], gradients[2], gradients[3], gradients[11], gradients[12], gradients[13], gradients[14], gradients[15], gradients[16])
```

```python
import functools

import jax
import jax.numpy as jnp
from jax import lax
from jax.experimental import pallas as pl
from jax.experimental.pallas import tpu as pltpu
from jax.sharding import PartitionSpec as P

HEAD = 64
DOC_MAX = 1024
PAIR = 2 * HEAD
TILE = 256
UNIT = 512
EPSILON = 1e-05
F32 = jnp.float32
BF16 = jnp.bfloat16
SCALE = HEAD ** -0.5
GELU_A = 0.7978845608028654
GELU_B = 0.044715


def dot(a, b, dims, out=F32):
    return lax.dot_general(a, b, (dims, ((), ())), preferred_element_type=out)


def nn(a, b):
    return dot(a, b, ((1,), (0,)))


def nt(a, b):
    return dot(a, b, ((1,), (1,)))


def tn(a, b):
    return dot(a, b, ((0,), (0,)))


def wide(tile):
    lane = lax.broadcasted_iota(jnp.int32, tile.shape, 1)
    zero = jnp.zeros_like(tile)
    return jnp.concatenate(
        (jnp.where(lane < HEAD, tile, zero), jnp.where(lane < HEAD, zero, tile)), axis=0
    )


def both(row):
    return jnp.concatenate((row, row), axis=1)


def heads_of(acc):
    return jnp.concatenate((acc[:HEAD, :TILE], acc[HEAD:, TILE:]), axis=0)


def mask_rows(start_ref, step, shift):
    start = both(start_ref[...] - shift)
    place = both((step + 4) * TILE + lax.broadcasted_iota(jnp.int32, (1, TILE), 1))
    return start, place


def allowed(tile_index, start, place):
    key = tile_index * TILE + lax.broadcasted_iota(jnp.int32, (TILE, 2 * TILE), 0)
    return (key >= start) & (key <= place)


def attend_kernel(base, shift, low_ref, start_ref, q_ref, k_ref, v_ref, *rest):
    o_ref, turned_ref, log_ref, acc_ref = rest[-4:]
    step = pl.program_id(0)
    query = wide(q_ref[...] * jnp.asarray(SCALE, BF16))
    start, place = mask_rows(start_ref, step, shift)
    acc_ref[...] = jnp.zeros_like(acc_ref)

    def body(j, carried):
        top, total = carried
        rows = pl.ds(pl.multiple_of(j * TILE, TILE), TILE)
        scores = nt(k_ref[rows, :], query)
        scores = jnp.where(allowed(j, start, place), scores, -1e30)
        new_top = jnp.maximum(top, jnp.max(scores, axis=0, keepdims=True))
        part = jnp.exp(scores - new_top)
        factor = jnp.exp(top - new_top)
        total = total * factor + jnp.sum(part, axis=0, keepdims=True)
        acc_ref[...] = acc_ref[...] * factor + tn(v_ref[rows, :], part.astype(BF16))
        return new_top, total

    top, total = lax.fori_loop(
        low_ref[base + step] - shift // TILE,
        step + 5,
        body,
        (jnp.full((1, 2 * TILE), -1e30, F32), jnp.zeros((1, 2 * TILE), F32)),
    )
    turned = heads_of(acc_ref[...] / total)
    turned_ref[...] = turned
    o_ref[...] = turned.T.astype(BF16)
    logs = top + jnp.log(total)
    log_ref[0:1, :] = logs[:, :TILE]
    log_ref[1:2, :] = logs[:, TILE:]


def attend(base, shift, low, start, q, qcol, k, kcol, v, vcol, earlier, tokens):
    n = k.shape[0]
    steps = (n - DOC_MAX) // TILE
    alias = earlier is not None
    specs = [
        pl.BlockSpec((1, TILE), lambda i, *_: (0, base + i)),
        pl.BlockSpec((TILE, PAIR), lambda i, *_: (base + i, qcol)),
        pl.BlockSpec((n, PAIR), lambda i, *_: (0, kcol)),
        pl.BlockSpec((n, PAIR), lambda i, *_: (0, vcol)),
    ] + [pl.BlockSpec(memory_space=pl.ANY)] * (3 if alias else 0)
    return pl.pallas_call(
        functools.partial(attend_kernel, base, shift),
        grid_spec=pltpu.PrefetchScalarGridSpec(
            num_scalar_prefetch=1,
            grid=(steps,),
            in_specs=specs,
            out_specs=[
                pl.BlockSpec((TILE, PAIR), lambda i, *_: (base + i, 0)),
                pl.BlockSpec((PAIR, TILE), lambda i, *_: (0, base + i)),
                pl.BlockSpec((8, TILE), lambda i, *_: (0, base + i)),
            ],
            scratch_shapes=[pltpu.VMEM((PAIR, 2 * TILE), F32)],
        ),
        out_shape=[
            jax.ShapeDtypeStruct((tokens, PAIR), BF16),
            jax.ShapeDtypeStruct((PAIR, tokens), F32),
            jax.ShapeDtypeStruct((8, tokens), F32),
        ],
        input_output_aliases={5: 0, 6: 1, 7: 2} if alias else {},
        cost_estimate=pl.CostEstimate(
            flops=4 * steps * 3 * TILE * TILE * 2 * PAIR,
            bytes_accessed=4 * n * PAIR + 8 * steps * TILE * PAIR,
            transcendentals=steps * 3 * TILE * 2 * TILE,
        ),
        name="attend",
    )(low, start, q, k, v, *(earlier if alias else ()))


def attend_back_kernel(base, shift, first, low_ref, start_ref, q_ref, k_ref, v_ref, do_ref, turned_ref, log_ref, *rest):
    if first:
        dq_ref, dk_ref, dv_ref, acc_ref = rest
    else:
        dk_in, dv_in, _, dq_ref, dk_ref, dv_ref, acc_ref = rest
    step = pl.program_id(0)

    @pl.when(step == 0)
    def _():
        dk_ref[...] = jnp.zeros_like(dk_ref)
        dv_ref[...] = jnp.zeros_like(dv_ref)
        if not first:
            held = dk_in.shape[0]
            dk_ref[:held, :] = dk_in[...]
            dv_ref[:held, :] = dv_in[...]

    query = wide(q_ref[...] * jnp.asarray(SCALE, BF16))
    out_back = wide(do_ref[...])
    start, place = mask_rows(start_ref, step, shift)
    product = do_ref[...].astype(F32).T * turned_ref[...]
    delta = jnp.concatenate(
        (
            jnp.sum(product[:HEAD], axis=0, keepdims=True),
            jnp.sum(product[HEAD:], axis=0, keepdims=True),
        ),
        axis=1,
    )
    logs = jnp.concatenate((log_ref[0:1, :], log_ref[1:2, :]), axis=1)
    acc_ref[...] = jnp.zeros_like(acc_ref)

    def body(j, carried):
        rows = pl.ds(pl.multiple_of(j * TILE, TILE), TILE)
        key_tile = k_ref[rows, :]
        scores = jnp.where(allowed(j, start, place), nt(key_tile, query), -1e30)
        prob = jnp.exp(scores - logs)
        prob_back = nt(v_ref[rows, :], out_back)
        score_back = (prob * (prob_back - delta)).astype(BF16)
        dv_ref[rows, :] += nn(prob.astype(BF16), out_back)
        dk_ref[rows, :] += nn(score_back, query)
        acc_ref[...] += tn(key_tile, score_back)
        return carried

    lax.fori_loop(low_ref[base + step] - shift // TILE, step + 5, body, 0)
    dq_ref[...] = (heads_of(acc_ref[...]) * SCALE).T.astype(BF16)


def attend_back(base, shift, low, start, q, qcol, k, kcol, v, vcol, do, turned, logs, earlier, tokens):
    n = k.shape[0]
    steps = (n - DOC_MAX) // TILE
    first = earlier is None
    held = n - DOC_MAX
    specs = [
        pl.BlockSpec((1, TILE), lambda i, *_: (0, base + i)),
        pl.BlockSpec((TILE, PAIR), lambda i, *_: (base + i, qcol)),
        pl.BlockSpec((n, PAIR), lambda i, *_: (0, kcol)),
        pl.BlockSpec((n, PAIR), lambda i, *_: (0, vcol)),
        pl.BlockSpec((TILE, PAIR), lambda i, *_: (base + i, 0)),
        pl.BlockSpec((PAIR, TILE), lambda i, *_: (0, base + i)),
        pl.BlockSpec((8, TILE), lambda i, *_: (0, base + i)),
    ]
    if not first:
        specs += [
            pl.BlockSpec((held, PAIR), lambda i, *_: (DOC_MAX // held, 0)),
            pl.BlockSpec((held, PAIR), lambda i, *_: (DOC_MAX // held, 0)),
            pl.BlockSpec(memory_space=pl.ANY),
        ]
    return pl.pallas_call(
        functools.partial(attend_back_kernel, base, shift, first),
        grid_spec=pltpu.PrefetchScalarGridSpec(
            num_scalar_prefetch=1,
            grid=(steps,),
            in_specs=specs,
            out_specs=[
                pl.BlockSpec((TILE, PAIR), lambda i, *_: (base + i, 0)),
                pl.BlockSpec((n, PAIR), lambda i, *_: (0, 0)),
                pl.BlockSpec((n, PAIR), lambda i, *_: (0, 0)),
            ],
            scratch_shapes=[pltpu.VMEM((PAIR, 2 * TILE), F32)],
        ),
        out_shape=[
            jax.ShapeDtypeStruct((tokens, PAIR), BF16),
            jax.ShapeDtypeStruct((n, PAIR), F32),
            jax.ShapeDtypeStruct((n, PAIR), F32),
        ],
        input_output_aliases={} if first else {10: 0},
        cost_estimate=pl.CostEstimate(
            flops=10 * steps * 3 * TILE * TILE * 2 * PAIR,
            bytes_accessed=12 * n * PAIR + 10 * steps * TILE * PAIR,
            transcendentals=steps * 3 * TILE * 2 * TILE,
        ),
        name="attend_back",
    )(low, start, q, k, v, do, turned, logs, *(() if first else earlier))


def up_kernel(sn_ref, cot_ref, up_ref, bias_ref, down_ref, out_ref, slope_ref, grad_ref):
    step = pl.program_id(0)
    hidden = nn(sn_ref[...], up_ref[0]) + bias_ref[0]
    square = hidden * hidden
    curve = jnp.tanh(GELU_A * (hidden + GELU_B * (hidden * square)))
    half = 0.5 * (1.0 + curve)
    activated = (hidden * half).astype(BF16)
    slope_ref[...] = half + 0.5 * hidden * (1.0 - curve * curve) * (
        GELU_A * (1.0 + 3.0 * GELU_B * square)
    )
    part = nn(activated, down_ref[...])

    @pl.when(step == 0)
    def _():
        out_ref[...] = part

    @pl.when(step > 0)
    def _():
        out_ref[...] += part

    grad_ref[0] = nn(cot_ref[...], activated).astype(BF16)


def feed_up(sn, cot_turned, up, bias, down):
    rows, width = sn.shape
    parts, _, hid = up.shape
    per = hid // UNIT
    steps = parts * per
    return pl.pallas_call(
        up_kernel,
        grid=(steps,),
        in_specs=[
            pl.BlockSpec((rows, width), lambda i: (0, 0)),
            pl.BlockSpec((width, rows), lambda i: (0, 0)),
            pl.BlockSpec((1, width, UNIT), lambda i: (i // per, 0, i % per)),
            pl.BlockSpec((1, 1, UNIT), lambda i: (i // per, 0, i % per)),
            pl.BlockSpec((UNIT, width), lambda i: (i, 0)),
        ],
        out_specs=[
            pl.BlockSpec((rows, width), lambda i: (0, 0)),
            pl.BlockSpec((rows, UNIT), lambda i: (0, i)),
            pl.BlockSpec((1, width, UNIT), lambda i: (i // per, 0, i % per)),
        ],
        out_shape=[
            jax.ShapeDtypeStruct((rows, width), F32),
            jax.ShapeDtypeStruct((rows, parts * hid), F32),
            jax.ShapeDtypeStruct((parts, width, hid), BF16),
        ],
        cost_estimate=pl.CostEstimate(
            flops=6 * rows * width * parts * hid,
            bytes_accessed=10 * rows * width + 6 * width * parts * hid + 4 * rows * parts * hid,
            transcendentals=rows * parts * hid,
        ),
        name="feed_up",
    )(sn, cot_turned, up, bias, down)


def down_kernel(cot_ref, sn_ref, slope_ref, up_ref, down_ref, back_ref, grad_ref, bias_ref):
    step = pl.program_id(0)
    hidden_back = nt(cot_ref[...], down_ref[...]) * slope_ref[...]
    rounded = hidden_back.astype(BF16)
    bias_ref[0] = jnp.sum(rounded.astype(F32), axis=0, keepdims=True)
    part = nt(rounded, up_ref[0])

    @pl.when(step == 0)
    def _():
        back_ref[...] = part

    @pl.when(step > 0)
    def _():
        back_ref[...] += part

    grad_ref[0] = nn(sn_ref[...], rounded).astype(BF16)


def feed_down(cot, sn_turned, slope, up, down):
    rows, width = cot.shape
    parts, _, hid = up.shape
    per = hid // UNIT
    return pl.pallas_call(
        down_kernel,
        grid=(parts * per,),
        in_specs=[
            pl.BlockSpec((rows, width), lambda i: (0, 0)),
            pl.BlockSpec((width, rows), lambda i: (0, 0)),
            pl.BlockSpec((rows, UNIT), lambda i: (0, i)),
            pl.BlockSpec((1, width, UNIT), lambda i: (i // per, 0, i % per)),
            pl.BlockSpec((UNIT, width), lambda i: (i, 0)),
        ],
        out_specs=[
            pl.BlockSpec((rows, width), lambda i: (0, 0)),
            pl.BlockSpec((1, width, UNIT), lambda i: (i // per, 0, i % per)),
            pl.BlockSpec((1, 1, UNIT), lambda i: (i // per, 0, i % per)),
        ],
        out_shape=[
            jax.ShapeDtypeStruct((rows, width), F32),
            jax.ShapeDtypeStruct((parts, width, hid), BF16),
            jax.ShapeDtypeStruct((parts, 1, hid), F32),
        ],
        cost_estimate=pl.CostEstimate(
            flops=6 * rows * width * parts * hid,
            bytes_accessed=10 * rows * width + 6 * width * parts * hid + 4 * rows * parts * hid,
            transcendentals=0,
        ),
        name="feed_down",
    )(cot, sn_turned, slope, up, down)


def around(value, steps):
    count = lax.axis_size("tp")
    return lax.ppermute(value, "tp", [(i, (i + steps) % count) for i in range(count)])


def flipped(value, axis, bit):
    count = lax.axis_size(axis)
    return lax.ppermute(value, axis, [(i, i ^ bit) for i in range(count)])


def along(value, steps):
    count = lax.axis_size("seq")
    first, last = max(0, -steps), min(count, count - steps)
    return lax.ppermute(value, "seq", [(i, i + steps) for i in range(first, last)])


def summed(value):
    for axis in ("seq", "tp"):
        bit = 1
        while bit < lax.axis_size(axis):
            value = value + flipped(value, axis, bit)
            bit *= 2
    return value


def pick(value, index, dim):
    return lax.dynamic_index_in_dim(value, index, dim, keepdims=False)


def halved(value, place, bit, dim):
    mine = (place // bit) % 2
    sent = pick(value, 1 - mine, dim)
    kept = pick(value, mine, dim)
    return (kept.astype(F32) + flipped(sent, "seq", bit).astype(F32)).astype(BF16)


def seq_bits():
    bits, bit = [], 1
    while bit < lax.axis_size("seq"):
        bits.append(bit)
        bit *= 2
    return bits


def scatter_seq(value, place, bits):
    lead, count, rows, cols = value.shape
    order = sorted(bits, reverse=True)
    left = value.reshape((lead,) + (2,) * len(order) + (rows, cols))
    remaining = list(order)
    for bit in bits:
        dim = 1 + remaining.index(bit)
        left = halved(left, place, bit, dim)
        remaining.remove(bit)
    return left


def scatter_all(value, place, tp_place):
    bits = seq_bits()
    lead = value.shape[0]
    head, tail = bits[0], bits[1:]
    other = tail[1:] + tail[:1]
    first = scatter_seq(value[: lead // 2], place, [head] + tail)
    second = scatter_seq(value[lead // 2 :], place, [head] + other)
    blocks = [first[i] for i in range(lead // 2)] + [second[i] for i in range(lead // 2)]
    total = blocks[0].astype(F32)
    for k in range(1, lead):
        total = total + around(blocks[k], k).astype(F32)
    return total


def rotated(value, tp_place, sign):
    count = value.shape[0]
    return jnp.stack([pick(value, (tp_place + sign * k) % count, 0) for k in range(count)])


def center(rows):
    average = jnp.mean(rows, axis=-1, keepdims=True)
    centered = rows - average
    inverse = lax.rsqrt(jnp.mean(centered * centered, axis=-1, keepdims=True) + EPSILON)
    return centered * inverse, inverse


def norm_back(grad, gain, xhat, inverse):
    e = grad * gain
    return inverse * (
        e
        - jnp.mean(e, axis=-1, keepdims=True)
        - xhat * jnp.mean(e * xhat, axis=-1, keepdims=True)
    )


def local(
    stream, segments, skip_values, first_gain, first_shift, query_weight, query_bias, key_weight,
    value_weight, value_bias, mixing_weight, mixing_bias, second_gain, second_shift, up_weight,
    up_bias, down_weight, down_bias, cotangent,
):
    rows, width = stream.shape
    tokens = skip_values.shape[0]
    own = query_weight.shape[1]
    tp_count = lax.axis_size("tp")
    seq_count = lax.axis_size("seq")
    seq_place = lax.axis_index("seq")
    tp_place = lax.axis_index("tp")
    half = tokens - DOC_MAX

    def share(shard):
        part = shard.shape[0] // seq_count
        mine = lax.dynamic_slice_in_dim(shard, seq_place * part, part, 0)
        return lax.all_gather(mine, ("tp", "seq"), axis=0, tiled=True)

    mixing_full = share(mixing_weight).reshape(tp_count, own, width)
    up_full = share(up_weight).reshape(tp_count, width, up_weight.shape[1])
    down_full = share(down_weight)
    wqkv = jnp.concatenate((query_weight, key_weight, value_weight), axis=1)
    turned_low = jnp.concatenate(
        (query_weight[:, :PAIR], key_weight[:, :PAIR], value_weight), axis=1
    ).T
    turned_high = jnp.concatenate((query_weight[:, PAIR:], key_weight[:, PAIR:]), axis=1).T

    stream_wide = stream.astype(F32)
    first_hat, first_inverse = center(stream_wide)
    piece = (first_hat * first_gain + first_shift).astype(BF16)
    bias = jnp.concatenate((query_bias, jnp.zeros((own,), F32), value_bias))
    qkv = jnp.zeros((tp_count, rows, wqkv.shape[1]), BF16)
    normed = jnp.zeros((tp_count, rows, width), BF16)
    for k in range(tp_count):
        ahead = around(piece, 1) if k < tp_count - 1 else None
        block = (tp_place - k) % tp_count
        projected = (nn(piece, wqkv) + bias).astype(BF16)
        qkv = lax.dynamic_update_index_in_dim(qkv, projected, block, 0)
        normed = lax.dynamic_update_index_in_dim(normed, piece, block, 0)
        piece = ahead
    qkv = qkv.reshape(tokens, wqkv.shape[1])
    normed = normed.reshape(tokens, width)

    padded = jnp.concatenate((jnp.full((DOC_MAX,), -1, jnp.int32), segments))
    window = lax.dynamic_slice_in_dim(padded, seq_place * tokens, DOC_MAX + tokens, 0)
    start = jnp.sum(
        (window[:, None] < window[None, DOC_MAX:]).astype(jnp.int32), axis=0, keepdims=True
    )
    low = start[0, ::TILE] // TILE

    halo_skip = along(skip_values[half:], 1)
    halo = along(qkv[half:, own:], 1)
    skip_early = jnp.concatenate((halo_skip, skip_values[:half]), axis=0)
    early = jnp.concatenate((halo, qkv[:half, own:]), axis=0)
    kcol = own // PAIR

    def values_of(pair):
        if pair == 0:
            return (qkv, 2 * kcol), (early, kcol)
        return (skip_values, 0), (skip_early, 0)

    steps = half // TILE
    attended = []
    for pair in range(2):
        (v, vcol), (ve, vecol) = values_of(pair)
        late = attend(steps, DOC_MAX, low, start, qkv, pair, qkv, kcol + pair, v, vcol, None, tokens)
        attended.append(
            attend(0, 0, low, start, qkv, pair, early, pair, ve, vecol, late, tokens)
        )

    def exchanged(blocks, sign):
        return [pick(blocks, tp_place, 0)] + [
            around(pick(blocks, (tp_place + sign * k) % tp_count, 0), sign * k)
            for k in range(1, tp_count)
        ]

    arrived = [
        exchanged(attended[pair][0].reshape(tp_count, rows, PAIR), 1) for pair in range(2)
    ]
    mixed_in = jnp.concatenate(
        [arrived[pair][k] for k in range(tp_count) for pair in range(2)], axis=1
    )
    mixing_rot = rotated(mixing_full, tp_place, -1).reshape(tp_count * own, width)
    middle = stream_wide + nn(mixed_in, mixing_rot) + mixing_bias
    second_hat, second_inverse = center(middle)
    second = (second_hat * second_gain + second_shift).astype(BF16)

    bias_pieces = [up_bias] + [around(up_bias, k) for k in range(1, tp_count)]
    bias_full = jnp.zeros((tp_count, 1, up_bias.shape[0]), F32)
    for k in range(tp_count):
        bias_full = lax.dynamic_update_index_in_dim(
            bias_full, bias_pieces[k][None], (tp_place - k) % tp_count, 0
        )
    lost, slope, down_grad = feed_up(second, cotangent.T, up_full, bias_full, down_full)
    output = (middle + lost + down_bias).astype(BF16)
    second_back, up_grad, up_bias_grad = feed_down(cotangent, second.T, slope, up_full, down_full)

    def reduced(grad):
        blocks = rotated(grad, tp_place, 1)
        return scatter_all(
            blocks.reshape(tp_count, seq_count, blocks.shape[1] // seq_count, blocks.shape[2]),
            seq_place,
            tp_place,
        )

    down_gradient = reduced(down_grad).T
    up_gradient = reduced(up_grad)

    upstream = cotangent.astype(F32)
    middle_back = upstream + norm_back(second_back, second_gain, second_hat, second_inverse)
    mixing_back = middle_back.astype(BF16)
    attended_back = nt(mixing_back, mixing_rot).astype(BF16).reshape(rows, tp_count, 2, PAIR)
    returned = []
    for pair in range(2):
        pieces = [attended_back[:, k, pair] for k in range(tp_count)]
        full = jnp.zeros((tp_count, rows, PAIR), BF16)
        for k in range(tp_count):
            got = pieces[k] if k == 0 else around(pieces[k], -k)
            full = lax.dynamic_update_index_in_dim(full, got, (tp_place + k) % tp_count, 0)
        returned.append(full.reshape(tokens, PAIR))
    mixing_grad = tn(mixing_back, mixed_in).astype(BF16)
    mixing_grad = mixing_grad.reshape(seq_count, width // seq_count, tp_count, own)
    mixing_grad = mixing_grad.transpose(2, 0, 1, 3)
    mixing_grad = jnp.stack([mixing_grad[-k % tp_count] for k in range(tp_count)])
    mixing_gradient = scatter_all(mixing_grad, seq_place, tp_place).T

    low_full = share(turned_low)
    high_full = share(turned_high)
    shares = [low_full.reshape(tp_count, -1, width), high_full.reshape(tp_count, -1, width)]
    first_back = None
    weight_parts = []
    dq_sum, dv_sum, skip_gradient = [], None, None
    for pair in range(2):
        (v, vcol), (ve, vecol) = values_of(pair)
        _, turned, logs = attended[pair]
        dq_b, dk_b, dv_b = attend_back(
            0, 0, low, start, qkv, pair, early, pair, ve, vecol,
            returned[pair], turned, logs, None, tokens,
        )
        dq, dk_a, dv_a = attend_back(
            steps, DOC_MAX, low, start, qkv, pair, qkv, kcol + pair, v, vcol,
            returned[pair], turned, logs, (dk_b, dv_b, dq_b), tokens,
        )
        gone = jnp.concatenate((dk_b[:DOC_MAX], dv_b[:DOC_MAX]), axis=1).astype(BF16)
        back = along(gone, -1).astype(F32)
        dk = jnp.concatenate((dk_a[:half], dk_a[half:] + back[:, :PAIR]), axis=0).astype(BF16)
        dv = jnp.concatenate((dv_a[:half], dv_a[half:] + back[:, PAIR:]), axis=0)
        grads = [dq, dk]
        dq_sum.append(jnp.sum(dq.astype(F32), axis=0))
        if pair == 0:
            fresh_back = dv.astype(BF16)
            grads.append(fresh_back)
            dv_sum = jnp.sum(fresh_back.astype(F32), axis=0)
        else:
            skip_gradient = dv
        packed = jnp.concatenate(grads, axis=1)
        weight_parts.append(tn(normed, packed).astype(BF16))
        pieces = exchanged(packed.reshape(tp_count, rows, packed.shape[1]), 1)
        weights = rotated(shares[pair], tp_place, -1).reshape(-1, width)
        part = nn(jnp.concatenate(pieces, axis=1), weights)
        first_back = part if first_back is None else first_back + part

    stream_gradient = middle_back + norm_back(first_back, first_gain, first_hat, first_inverse)
    weight_grad = jnp.concatenate(weight_parts, axis=1)
    weight_grad = weight_grad.reshape(1, seq_count, width // seq_count, weight_grad.shape[1])
    weight_grad = scatter_seq(weight_grad, seq_place, seq_bits())[0].astype(F32)
    query_gradient = jnp.concatenate(
        (weight_grad[:, :PAIR], weight_grad[:, 3 * PAIR : 4 * PAIR]), axis=1
    )
    key_gradient = jnp.concatenate(
        (weight_grad[:, PAIR : 2 * PAIR], weight_grad[:, 4 * PAIR :]), axis=1
    )
    value_gradient = weight_grad[:, 2 * PAIR : 3 * PAIR]

    def widen(part):
        size = part.shape[0]
        return lax.dynamic_update_slice_in_dim(
            jnp.zeros((size * tp_count,), F32), part, tp_place * size, 0
        )

    parts = [
        jnp.sum(first_back * first_hat, axis=0),
        jnp.sum(first_back, axis=0),
        jnp.sum(second_back * second_hat, axis=0),
        jnp.sum(second_back, axis=0),
        jnp.sum(middle_back, axis=0),
        jnp.sum(upstream, axis=0),
        widen(jnp.concatenate(dq_sum)),
        widen(dv_sum),
        up_bias_grad.reshape(-1),
    ]
    sums = summed(jnp.concatenate(parts).reshape(-1, PAIR)).reshape(-1)
    cuts, offset = [], 0
    for part in parts:
        cuts.append(sums[offset : offset + part.shape[0]])
        offset += part.shape[0]
    return (
        output,
        stream_gradient,
        skip_gradient,
        query_gradient,
        cuts[6],
        key_gradient,
        value_gradient,
        cuts[7],
        mixing_gradient,
        cuts[4],
        cuts[0],
        cuts[1],
        cuts[2],
        cuts[3],
        up_gradient,
        cuts[8],
        down_gradient,
        cuts[5],
    )


def solution(mesh):
    split = P(("seq", "tp"), None)
    column = P(None, "tp")
    in_specs = (
        split, P(), P("seq", "tp"), P(), P(), column, P("tp"), column, column, P("tp"),
        P("tp", None), P(), P(), P(), column, P("tp"), P("tp", None), P(), split,
    )
    tile = P("seq", "tp")
    out_specs = (
        split, split, tile, tile, P(), tile, tile, P(), P("tp", "seq"), P(), P(), P(), P(), P(),
        tile, P(), P("tp", "seq"), P(),
    )
    return jax.shard_map(local, mesh=mesh, in_specs=in_specs, out_specs=out_specs, check_vma=False)
```

```python
import functools

import jax
import jax.numpy as jnp
from jax import lax
from jax.experimental import pallas as pl
from jax.experimental.pallas import tpu as pltpu
from jax.sharding import PartitionSpec as P

HEAD = 64
DOC_MAX = 1024
PAIR = 2 * HEAD
TILE = 256
UNIT = 512
EPSILON = 1e-05
F32 = jnp.float32
BF16 = jnp.bfloat16
SCALE = HEAD ** -0.5
GELU_A = 0.7978845608028654
GELU_B = 0.044715


def dot(a, b, dims, out=F32):
    return lax.dot_general(a, b, (dims, ((), ())), preferred_element_type=out)


def nn(a, b):
    return dot(a, b, ((1,), (0,)))


def nt(a, b):
    return dot(a, b, ((1,), (1,)))


def tn(a, b):
    return dot(a, b, ((0,), (0,)))


def light(bytes_accessed):
    return pl.CostEstimate(flops=1, bytes_accessed=bytes_accessed, transcendentals=0)


ANY = pl.BlockSpec(memory_space=pl.ANY)


def project_kernel(slot, place_ref, piece_ref, weight_ref, bias_ref, *rest):
    qkv_ref, normed_ref = rest[-2:]
    piece = piece_ref[...]
    qkv_ref[...] = (nn(piece, weight_ref[...]) + bias_ref[...]).astype(BF16)
    normed_ref[...] = piece


def project(k, count, place, piece, weight, bias, earlier):
    rows, width = piece.shape
    cols = weight.shape[1]
    slot = (count - k) % count
    tile = rows // 2
    alias = earlier is not None
    return pl.pallas_call(
        functools.partial(project_kernel, slot),
        grid_spec=pltpu.PrefetchScalarGridSpec(
            num_scalar_prefetch=1,
            grid=(2,),
            in_specs=[
                pl.BlockSpec((tile, width), lambda i, p: (i, 0)),
                pl.BlockSpec((width, cols), lambda i, p: (0, 0)),
                pl.BlockSpec((1, cols), lambda i, p: (0, 0)),
            ]
            + ([ANY, ANY] if alias else []),
            out_specs=[
                pl.BlockSpec((tile, cols), lambda i, p: (2 * lax.rem(p[0] + slot, count) + i, 0)),
                pl.BlockSpec((tile, width), lambda i, p: (2 * slot + i, 0)),
            ],
        ),
        out_shape=[
            jax.ShapeDtypeStruct((count * rows, cols), BF16),
            jax.ShapeDtypeStruct((count * rows, width), BF16),
        ],
        input_output_aliases={4: 0, 5: 1} if alias else {},
        cost_estimate=light(4 * rows * width),
        name="project",
    )(place, piece, weight, bias, *(earlier if alias else ()))


def wide(tile):
    lane = lax.broadcasted_iota(jnp.int32, tile.shape, 1)
    zero = jnp.zeros_like(tile)
    return jnp.concatenate(
        (jnp.where(lane < HEAD, tile, zero), jnp.where(lane < HEAD, zero, tile)), axis=0
    )


def both(row):
    return jnp.concatenate((row, row), axis=1)


def heads_of(acc):
    return jnp.concatenate((acc[:HEAD, :TILE], acc[HEAD:, TILE:]), axis=0)


def mask_rows(start_ref, step, shift):
    start = both(start_ref[...] - shift)
    place = both((step + 4) * TILE + lax.broadcasted_iota(jnp.int32, (1, TILE), 1))
    return start, place


def allowed(tile_index, start, place):
    key = tile_index * TILE + lax.broadcasted_iota(jnp.int32, (TILE, 2 * TILE), 0)
    return (key >= start) & (key <= place)


def turn(tile, meta_ref, tiles, per, count):
    block = tile // per
    return per * lax.rem(block - meta_ref[tiles] + count, count) + lax.rem(tile, per)


def attend_kernel(base, shift, meta_ref, start_ref, q_ref, k_ref, v_ref, *rest):
    o_ref, turned_ref, log_ref, acc_ref = rest[-4:]
    step = pl.program_id(0)
    query = wide(q_ref[...] * jnp.asarray(SCALE, BF16))
    start, place = mask_rows(start_ref, step, shift)
    acc_ref[...] = jnp.zeros_like(acc_ref)

    def body(j, carried):
        top, total = carried
        rows = pl.ds(pl.multiple_of(j * TILE, TILE), TILE)
        scores = nt(k_ref[rows, :], query)
        scores = jnp.where(allowed(j, start, place), scores, -1e30)
        new_top = jnp.maximum(top, jnp.max(scores, axis=0, keepdims=True))
        part = jnp.exp(scores - new_top)
        factor = jnp.exp(top - new_top)
        total = total * factor + jnp.sum(part, axis=0, keepdims=True)
        acc_ref[...] = acc_ref[...] * factor + tn(v_ref[rows, :], part.astype(BF16))
        return new_top, total

    top, total = lax.fori_loop(
        meta_ref[base + step] - shift // TILE,
        step + 5,
        body,
        (jnp.full((1, 2 * TILE), -1e30, F32), jnp.zeros((1, 2 * TILE), F32)),
    )
    turned = heads_of(acc_ref[...] / total)
    turned_ref[...] = turned
    o_ref[...] = turned.T.astype(BF16)
    logs = top + jnp.log(total)
    log_ref[0:1, :] = logs[:, :TILE]
    log_ref[1:2, :] = logs[:, TILE:]


def attend(base, shift, meta, start, q, qcol, k, kcol, v, vcol, earlier, tokens, count):
    n = k.shape[0]
    steps = (n - DOC_MAX) // TILE
    tiles = tokens // TILE
    per = tiles // count
    alias = earlier is not None
    specs = [
        pl.BlockSpec((1, TILE), lambda i, m: (0, base + i)),
        pl.BlockSpec((TILE, PAIR), lambda i, m: (base + i, qcol)),
        pl.BlockSpec((n, PAIR), lambda i, m: (0, kcol)),
        pl.BlockSpec((n, PAIR), lambda i, m: (0, vcol)),
    ] + [ANY] * (3 if alias else 0)
    return pl.pallas_call(
        functools.partial(attend_kernel, base, shift),
        grid_spec=pltpu.PrefetchScalarGridSpec(
            num_scalar_prefetch=1,
            grid=(steps,),
            in_specs=specs,
            out_specs=[
                pl.BlockSpec((TILE, PAIR), lambda i, m: (turn(base + i, m, tiles, per, count), 0)),
                pl.BlockSpec((PAIR, TILE), lambda i, m: (0, base + i)),
                pl.BlockSpec((8, TILE), lambda i, m: (0, base + i)),
            ],
            scratch_shapes=[pltpu.VMEM((PAIR, 2 * TILE), F32)],
        ),
        out_shape=[
            jax.ShapeDtypeStruct((tokens, PAIR), BF16),
            jax.ShapeDtypeStruct((PAIR, tokens), F32),
            jax.ShapeDtypeStruct((8, tokens), F32),
        ],
        input_output_aliases={5: 0, 6: 1, 7: 2} if alias else {},
        cost_estimate=light(4 * n * PAIR),
        name="attend",
    )(meta, start, q, k, v, *(earlier if alias else ()))


def back_tile(shift, low, start_ref, q_ref, k_ref, v_ref, do_ref, turned_ref, log_ref, dk_ref, dv_ref, acc_ref):
    step = pl.program_id(0)
    query = wide(q_ref[...] * jnp.asarray(SCALE, BF16))
    out_back = wide(do_ref[...])
    start, place = mask_rows(start_ref, step, shift)
    product = do_ref[...].astype(F32).T * turned_ref[...]
    delta = jnp.concatenate(
        (
            jnp.sum(product[:HEAD], axis=0, keepdims=True),
            jnp.sum(product[HEAD:], axis=0, keepdims=True),
        ),
        axis=1,
    )
    logs = jnp.concatenate((log_ref[0:1, :], log_ref[1:2, :]), axis=1)
    acc_ref[...] = jnp.zeros_like(acc_ref)

    def body(j, carried):
        rows = pl.ds(pl.multiple_of(j * TILE, TILE), TILE)
        key_tile = k_ref[rows, :]
        scores = jnp.where(allowed(j, start, place), nt(key_tile, query), -1e30)
        prob = jnp.exp(scores - logs)
        prob_back = nt(v_ref[rows, :], out_back)
        score_back = (prob * (prob_back - delta)).astype(BF16)
        dv_ref[rows, :] += nn(prob.astype(BF16), out_back)
        dk_ref[rows, :] += nn(score_back, query)
        acc_ref[...] += tn(key_tile, score_back)
        return carried

    lax.fori_loop(low, step + 5, body, 0)
    return (heads_of(acc_ref[...]) * SCALE).T.astype(BF16)


def early_kernel(meta_ref, start_ref, q_ref, k_ref, v_ref, do_ref, turned_ref, log_ref, dq_ref, gone_ref, dk_ref, dv_ref, kept_k, kept_v, acc_ref):
    step = pl.program_id(0)

    @pl.when(step == 0)
    def _():
        kept_k[...] = jnp.zeros_like(kept_k)
        kept_v[...] = jnp.zeros_like(kept_v)

    dq_ref[...] = back_tile(
        0, meta_ref[step], start_ref, q_ref, k_ref, v_ref, do_ref, turned_ref, log_ref,
        kept_k, kept_v, acc_ref,
    )

    @pl.when(step == pl.num_programs(0) - 1)
    def _():
        gone_ref[:, :PAIR] = kept_k[:DOC_MAX, :].astype(BF16)
        gone_ref[:, PAIR:] = kept_v[:DOC_MAX, :].astype(BF16)
        dk_ref[...] = kept_k[DOC_MAX:, :]
        dv_ref[...] = kept_v[DOC_MAX:, :]


def late_kernel(base, fresh, per, count, meta_ref, start_ref, q_ref, k_ref, v_ref, do_ref, turned_ref, log_ref, dq_in, dk_in, dv_in, back_ref, packed_ref, value_ref, sums_ref, kept_k, kept_v, acc_ref):
    step = pl.program_id(0)
    held = dk_in.shape[0]
    tiles = packed_ref.shape[0] // TILE

    def rows_of(tile):
        row = turn(tile, meta_ref, tiles, per, count) * TILE
        return pl.ds(pl.multiple_of(row, TILE), TILE)

    @pl.when(step == 0)
    def _():
        kept_k[:held, :] = dk_in[...]
        kept_v[:held, :] = dv_in[...]
        kept_k[held:, :] = back_ref[:, :PAIR].astype(F32)
        kept_v[held:, :] = back_ref[:, PAIR:].astype(F32)
        for i in range(base):
            packed_ref[rows_of(i), :PAIR] = dq_in[i * TILE : (i + 1) * TILE, :]

    packed_ref[rows_of(base + step), :PAIR] = back_tile(
        DOC_MAX, meta_ref[base + step] - DOC_MAX // TILE, start_ref, q_ref, k_ref, v_ref, do_ref,
        turned_ref, log_ref, kept_k, kept_v, acc_ref,
    )

    @pl.when(step == pl.num_programs(0) - 1)
    def _():
        for i in range(tiles):
            span = slice(i * TILE, (i + 1) * TILE)
            packed_ref[rows_of(i), PAIR : 2 * PAIR] = kept_k[span, :].astype(BF16)
            if fresh:
                packed_ref[rows_of(i), 2 * PAIR :] = kept_v[span, :].astype(BF16)
        if not fresh:
            value_ref[...] = kept_v[...]
        else:
            value_ref[...] = jnp.zeros_like(value_ref)
        sums_ref[...] = jnp.broadcast_to(
            jnp.sum(packed_ref[...].astype(F32), axis=0, keepdims=True), sums_ref.shape
        )


def back_specs(base, qcol, n, kcol, vcol, tiles, per, count):
    return [
        pl.BlockSpec((1, TILE), lambda i, m: (0, base + i)),
        pl.BlockSpec((TILE, PAIR), lambda i, m: (base + i, qcol)),
        pl.BlockSpec((n, PAIR), lambda i, m: (0, kcol)),
        pl.BlockSpec((n, PAIR), lambda i, m: (0, vcol)),
        pl.BlockSpec((TILE, PAIR), lambda i, m: (turn(base + i, m, tiles, per, count), 0)),
        pl.BlockSpec((PAIR, TILE), lambda i, m: (0, base + i)),
        pl.BlockSpec((8, TILE), lambda i, m: (0, base + i)),
    ]


def whole(shape):
    return pl.BlockSpec(shape, lambda i, m: (0,) * len(shape))


def back_early(meta, start, q, qcol, k, kcol, v, vcol, do, turned, logs, tokens, count):
    n = k.shape[0]
    held = n - DOC_MAX
    tiles = tokens // TILE
    return pl.pallas_call(
        early_kernel,
        grid_spec=pltpu.PrefetchScalarGridSpec(
            num_scalar_prefetch=1,
            grid=(held // TILE,),
            in_specs=back_specs(0, qcol, n, kcol, vcol, tiles, tiles // count, count),
            out_specs=[
                pl.BlockSpec((TILE, PAIR), lambda i, m: (i, 0)),
                whole((DOC_MAX, 2 * PAIR)),
                whole((held, PAIR)),
                whole((held, PAIR)),
            ],
            scratch_shapes=[
                pltpu.VMEM((n, PAIR), F32),
                pltpu.VMEM((n, PAIR), F32),
                pltpu.VMEM((PAIR, 2 * TILE), F32),
            ],
        ),
        out_shape=[
            jax.ShapeDtypeStruct((held, PAIR), BF16),
            jax.ShapeDtypeStruct((DOC_MAX, 2 * PAIR), BF16),
            jax.ShapeDtypeStruct((held, PAIR), F32),
            jax.ShapeDtypeStruct((held, PAIR), F32),
        ],
        cost_estimate=light(12 * n * PAIR),
        name="back_early",
    )(meta, start, q, k, v, do, turned, logs)


def back_late(meta, start, q, qcol, k, kcol, v, vcol, do, turned, logs, dq, dk, dv, back, fresh, tokens, count):
    n = k.shape[0]
    held = n - DOC_MAX
    tiles = tokens // TILE
    per = tiles // count
    base = (tokens - held) // TILE
    cols = (3 if fresh else 2) * PAIR
    return pl.pallas_call(
        functools.partial(late_kernel, base, fresh, per, count),
        grid_spec=pltpu.PrefetchScalarGridSpec(
            num_scalar_prefetch=1,
            grid=(held // TILE,),
            in_specs=back_specs(base, qcol, n, kcol, vcol, tiles, per, count)
            + [whole(dq.shape), whole(dk.shape), whole(dv.shape), whole(back.shape)],
            out_specs=[
                whole((tokens, cols)),
                whole((8, PAIR) if fresh else (tokens, PAIR)),
                whole((8, cols)),
            ],
            scratch_shapes=[
                pltpu.VMEM((n, PAIR), F32),
                pltpu.VMEM((n, PAIR), F32),
                pltpu.VMEM((PAIR, 2 * TILE), F32),
            ],
        ),
        out_shape=[
            jax.ShapeDtypeStruct((tokens, cols), BF16),
            jax.ShapeDtypeStruct((8, PAIR) if fresh else (tokens, PAIR), F32),
            jax.ShapeDtypeStruct((8, cols), F32),
        ],
        cost_estimate=light(12 * n * PAIR),
        name="back_late",
    )(meta, start, q, k, v, do, turned, logs, dq, dk, dv, back)


def up_kernel(parts, places_ref, sn_ref, cot_ref, up_ref, bias_ref, down_ref, out_ref, slope_ref, sent_ref, kept_ref):
    step = pl.program_id(0)
    rows = up_ref.shape[0] * up_ref.shape[1]
    hidden = nn(sn_ref[...], up_ref[...].reshape(rows, UNIT)) + bias_ref[0]
    square = hidden * hidden
    curve = jnp.tanh(GELU_A * (hidden + GELU_B * (hidden * square)))
    half = 0.5 * (1.0 + curve)
    activated = (hidden * half).astype(BF16)
    slope_ref[...] = half + 0.5 * hidden * (1.0 - curve * curve) * (
        GELU_A * (1.0 + 3.0 * GELU_B * square)
    )
    part = nn(activated, down_ref[...].reshape(UNIT, rows))

    @pl.when(step == 0)
    def _():
        out_ref[...] = part

    @pl.when(step > 0)
    def _():
        out_ref[...] += part

    grad = nn(cot_ref[...], activated).astype(BF16)
    sent_ref[0] = grad[: rows // 2]
    kept_ref[0] = grad[rows // 2 :]


def feed_specs(gathered, seq, parts, width):
    part = width // seq
    per = width // UNIT

    def spot(i, p):
        return lax.rem(p[0] + i // per, parts)

    return (
        pl.BlockSpec((seq, part, UNIT), lambda i, p: (spot(i, p), 0, lax.rem(i, per))),
        pl.BlockSpec((UNIT // part, part, width), lambda i, p: (spot(i, p) * per + lax.rem(i, per), 1, 0)),
        pl.BlockSpec((1, width // 2, UNIT), lambda i, p: (i // per, 0, lax.rem(i, per))),
        per,
    )


def feed_up(places, sn, cot_turned, gathered, bias, seq, parts):
    rows, width = sn.shape
    up_spec, down_spec, grad_spec, per = feed_specs(gathered, seq, parts, width)
    grad = jax.ShapeDtypeStruct((parts, width // 2, width), BF16)
    return pl.pallas_call(
        functools.partial(up_kernel, parts),
        grid_spec=pltpu.PrefetchScalarGridSpec(
            num_scalar_prefetch=1,
            grid=(parts * per,),
            in_specs=[
                pl.BlockSpec((rows, width), lambda i, p: (0, 0)),
                pl.BlockSpec((width, rows), lambda i, p: (0, 0)),
                up_spec,
                pl.BlockSpec((1, 1, UNIT), lambda i, p: (lax.rem(parts - i // per, parts), 0, lax.rem(i, per))),
                down_spec,
            ],
            out_specs=[
                pl.BlockSpec((rows, width), lambda i, p: (0, 0)),
                pl.BlockSpec((rows, UNIT), lambda i, p: (0, i)),
                grad_spec,
                grad_spec,
            ],
        ),
        out_shape=[
            jax.ShapeDtypeStruct((rows, width), F32),
            jax.ShapeDtypeStruct((rows, parts * width), F32),
            grad,
            grad,
        ],
        cost_estimate=light(16 * rows * width),
        name="feed_up",
    )(places, sn, cot_turned, gathered, bias, gathered)


def down_kernel(seq, places_ref, cot_ref, sn_ref, slope_ref, up_ref, down_ref, back_ref, sent_ref, kept_ref, bias_ref, plain_ref, turned_ref):
    step = pl.program_id(0)
    rows = up_ref.shape[0] * up_ref.shape[1]
    part = rows // seq

    @pl.when(step == 0)
    def _():
        plain_ref[...] = sn_ref[...].T
        for spot, r in enumerate(halves_order(seq)):
            lines = pl.ds(pl.multiple_of(jnp.bitwise_xor(places_ref[1], r) * part, part), part)
            turned_ref[spot * part : (spot + 1) * part, :] = plain_ref[lines, :]

    hidden_back = nt(cot_ref[...], down_ref[...].reshape(UNIT, rows)) * slope_ref[...]
    rounded = hidden_back.astype(BF16)
    bias_ref[0] = jnp.sum(rounded.astype(F32), axis=0, keepdims=True)
    share = nt(rounded, up_ref[...].reshape(rows, UNIT))

    @pl.when(step == 0)
    def _():
        back_ref[...] = share

    @pl.when(step > 0)
    def _():
        back_ref[...] += share

    grad = nn(turned_ref[...], rounded).astype(BF16)
    sent_ref[0] = grad[: rows // 2]
    kept_ref[0] = grad[rows // 2 :]


def feed_down(places, cot, sn, slope, gathered, seq, parts):
    rows, width = cot.shape
    up_spec, down_spec, grad_spec, per = feed_specs(gathered, seq, parts, width)
    grad = jax.ShapeDtypeStruct((parts, width // 2, width), BF16)
    return pl.pallas_call(
        functools.partial(down_kernel, seq),
        grid_spec=pltpu.PrefetchScalarGridSpec(
            num_scalar_prefetch=1,
            grid=(parts * per,),
            in_specs=[
                pl.BlockSpec((rows, width), lambda i, p: (0, 0)),
                pl.BlockSpec((rows, width), lambda i, p: (0, 0)),
                pl.BlockSpec((rows, UNIT), lambda i, p: (0, i)),
                up_spec,
                down_spec,
            ],
            out_specs=[
                pl.BlockSpec((rows, width), lambda i, p: (0, 0)),
                grad_spec,
                grad_spec,
                pl.BlockSpec((1, 1, UNIT), lambda i, p: (i // per, 0, lax.rem(i, per))),
            ],
            scratch_shapes=[pltpu.VMEM((width, rows), BF16)] * 2,
        ),
        out_shape=[
            jax.ShapeDtypeStruct((rows, width), F32),
            grad,
            grad,
            jax.ShapeDtypeStruct((parts, 1, width), F32),
        ],
        cost_estimate=light(16 * rows * width),
        name="feed_down",
    )(places, cot, sn, slope, gathered, gathered)


def around(value, steps):
    count = lax.axis_size("tp")
    return lax.ppermute(value, "tp", [(i, (i + steps) % count) for i in range(count)])


def flipped(value, axis, bit):
    count = lax.axis_size(axis)
    return lax.ppermute(value, axis, [(i, i ^ bit) for i in range(count)])


def along(value, steps):
    count = lax.axis_size("seq")
    first, last = max(0, -steps), min(count, count - steps)
    return lax.ppermute(value, "seq", [(i, i + steps) for i in range(first, last)])


def summed(value):
    for axis in ("seq", "tp"):
        bit = 1
        while bit < lax.axis_size(axis):
            value = value + flipped(value, axis, bit)
            bit *= 2
    return value


def halves_order(seq):
    return list(range(1, seq, 2)) + list(range(0, seq, 2))


def pick(value, index, dim):
    return lax.dynamic_index_in_dim(value, index, dim, keepdims=False)


def joined(a, b):
    return (a.astype(F32) + b.astype(F32)).astype(BF16)


def seq_bits():
    bits, bit = [], 1
    while bit < lax.axis_size("seq"):
        bits.append(bit)
        bit *= 2
    return bits


class Scatter:
    def __init__(self, sent, kept, sign):
        self.sign = sign
        left = list(range(0, lax.axis_size("seq"), 2))
        got = flipped(sent, "seq", 1)
        cut = kept.shape[0] // 2
        tail = seq_bits()[1:]
        self.lanes = [
            (kept[:cut], got[:cut], left, tail),
            (kept[cut:], got[cut:], left, tail[1:] + tail[:1]),
        ]
        self.moves = None

    def merge(self):
        arrays, plans = [], []
        for kept, got, left, bits in self.lanes:
            if not bits:
                arrays.append(joined(kept, got))
                plans.append(None)
                continue
            bit = bits[0]
            goes = [i for i, r in enumerate(left) if r & bit]
            stays = [i for i, r in enumerate(left) if not r & bit]

            def some(array, spots):
                return jnp.concatenate([array[:, i : i + 1] for i in spots], axis=1)

            for spots in (goes, stays):
                arrays.append(joined(some(kept, spots), some(got, spots)))
            plans.append(([left[i] for i in stays], bits))
        self.plans = plans
        return tuple(arrays)

    def send(self, arrays):
        arrays = list(arrays)
        if self.plans[0] is None:
            blocks = [part[i, 0] for part in arrays for i in range(part.shape[0])]
            self.blocks = [blocks[0]] + [
                around(blocks[k], self.sign * k) for k in range(1, len(blocks))
            ]
            self.lanes = None
            return
        lanes = []
        for left, bits in self.plans:
            goes, stays = arrays.pop(0), arrays.pop(0)
            lanes.append((stays, flipped(goes, "seq", bits[0]), left, bits[1:]))
        self.lanes = lanes

    def result(self):
        while self.lanes is not None:
            self.send(self.merge())
        total = self.blocks[0].astype(F32)
        for block in self.blocks[1:]:
            total = total + block.astype(F32)
        return total


def tied(*groups):
    return lax.optimization_barrier(groups)


def scatter_seq(value, place):
    seq = value.shape[0]
    bits = sorted(seq_bits(), reverse=True)
    left = value.reshape((2,) * len(bits) + value.shape[1:])
    for bit in bits:
        mine = (place // bit) % 2
        left = joined(pick(left, mine, 0), flipped(pick(left, 1 - mine, 0), "seq", bit))
    return left


def center(rows):
    average = jnp.mean(rows, axis=-1, keepdims=True)
    centered = rows - average
    inverse = lax.rsqrt(jnp.mean(centered * centered, axis=-1, keepdims=True) + EPSILON)
    return centered * inverse, inverse


def norm_back(grad, gain, xhat, inverse):
    e = grad * gain
    return inverse * (
        e
        - jnp.mean(e, axis=-1, keepdims=True)
        - xhat * jnp.mean(e * xhat, axis=-1, keepdims=True)
    )


def local(
    stream, segments, skip_values, first_gain, first_shift, query_weight, query_bias, key_weight,
    value_weight, value_bias, mixing_weight, mixing_bias, second_gain, second_shift, up_weight,
    up_bias, down_weight, down_bias, cotangent,
):
    rows, width = stream.shape
    tokens = skip_values.shape[0]
    own = query_weight.shape[1]
    tp = lax.axis_size("tp")
    seq = lax.axis_size("seq")
    seq_place = lax.axis_index("seq")
    tp_place = lax.axis_index("tp")
    places = jnp.stack((tp_place, seq_place)).astype(jnp.int32)
    half = tokens - DOC_MAX
    part = width // seq
    kcol = own // PAIR

    stream_wide = stream.astype(F32)
    first_hat, first_inverse = center(stream_wide)
    piece = (first_hat * first_gain + first_shift).astype(BF16)
    piece, up_weight, down_weight, mixing_weight, segments, cotangent = lax.optimization_barrier(
        (piece, up_weight, down_weight, mixing_weight, segments, cotangent)
    )

    def own_rows(shard):
        size = shard.shape[0] // seq
        return lax.dynamic_slice_in_dim(shard, seq_place * size, size, 0)

    packet = jnp.concatenate([own_rows(w) for w in (up_weight, down_weight, mixing_weight)], axis=0)
    gathered = lax.all_gather(packet, ("tp", "seq"), axis=0, tiled=False)
    mixing_full = gathered[:, 2 * part :].reshape(tp, own, width)
    mixing_rot = jnp.concatenate([pick(mixing_full, (tp_place - k) % tp, 0) for k in range(tp)], axis=0)
    qkv_turned = jnp.concatenate(
        (
            query_weight[:, :PAIR], key_weight[:, :PAIR], value_weight,
            query_weight[:, PAIR:], key_weight[:, PAIR:],
        ),
        axis=1,
    ).T
    bias_pieces = jnp.stack([up_bias] + [around(up_bias, k) for k in range(1, tp)])[:, None]

    wqkv = jnp.concatenate((query_weight, key_weight, value_weight), axis=1)
    bias = jnp.concatenate((query_bias, jnp.zeros((own,), F32), value_bias))[None]
    made = None
    for k in range(tp):
        ahead = around(piece, 1) if k < tp - 1 else None
        made = project(k, tp, places, piece, wqkv, bias, made)
        piece = ahead
    qkv, normed = made
    qkv, packet = tied(qkv, own_rows(qkv_turned))
    qkv_full = lax.all_gather(packet, ("tp", "seq"), axis=0, tiled=False).reshape(tp, -1, width)
    shares = [
        jnp.concatenate([pick(part, (tp_place - k) % tp, 0) for k in range(tp)], axis=0)
        for part in (qkv_full[:, : 3 * PAIR], qkv_full[:, 3 * PAIR :])
    ]

    padded = jnp.concatenate((jnp.full((DOC_MAX,), -1, jnp.int32), segments))
    window = lax.dynamic_slice_in_dim(padded, seq_place * tokens, DOC_MAX + tokens, 0)
    start = jnp.sum(
        (window[:, None] < window[None, DOC_MAX:]).astype(jnp.int32), axis=0, keepdims=True
    )
    meta = jnp.concatenate((start[0, ::TILE] // TILE, places))

    halo_skip = along(skip_values[half:], 1)
    halo = along(qkv[half:, own:], 1)
    skip_early = jnp.concatenate((halo_skip, skip_values[:half]), axis=0)
    early = jnp.concatenate((halo, qkv[:half, own:]), axis=0)

    def values_of(pair):
        if pair == 0:
            return (qkv, 2 * kcol), (early, kcol)
        return (skip_values, 0), (skip_early, 0)

    steps = half // TILE
    attended = []
    for pair in range(2):
        (v, vcol), _ = values_of(pair)
        attended.append(
            attend(steps, DOC_MAX, meta, start, qkv, pair, qkv, kcol + pair, v, vcol, None, tokens, tp)
        )
    arrived = []
    for pair in range(2):
        _, (v, vcol) = values_of(pair)
        attended[pair] = attend(
            0, 0, meta, start, qkv, pair, early, pair, v, vcol, attended[pair], tokens, tp
        )
        blocks = attended[pair][0].reshape(tp, rows, PAIR)
        arrived.append([blocks[0]] + [around(blocks[k], k) for k in range(1, tp)])

    mixed_in = jnp.concatenate([arrived[pair][k] for k in range(tp) for pair in range(2)], axis=1)
    middle = stream_wide + nn(mixed_in, mixing_rot) + mixing_bias
    second_hat, second_inverse = center(middle)
    second = (second_hat * second_gain + second_shift).astype(BF16)

    def by_distance(value):
        cut = value.reshape(rows, seq, part)
        return jnp.concatenate([pick(cut, seq_place ^ r, 1) for r in halves_order(seq)], axis=1)

    lost, slope, down_sent, down_kept = feed_up(
        places, second, by_distance(cotangent).T, gathered, bias_pieces, seq, tp
    )
    output = (middle + lost + down_bias).astype(BF16)

    shape = (tp, seq // 2, part, width)
    down_sum = Scatter(down_sent.reshape(shape), down_kept.reshape(shape), 1)
    second_back, up_sent, up_kept, up_bias_grad = feed_down(
        places, cotangent, second, slope, gathered, seq, tp
    )
    up_sum = Scatter(up_sent.reshape(shape), up_kept.reshape(shape), 1)
    second_back, ready = tied(second_back, down_sum.merge())
    down_sum.send(ready)

    upstream = cotangent.astype(F32)
    middle_back = upstream + norm_back(second_back, second_gain, second_hat, second_inverse)
    mixing_back = middle_back.astype(BF16)
    attended_back = nt(mixing_back, mixing_rot).astype(BF16)
    returned = []
    for pair in range(2):
        pieces = [attended_back[:, (2 * k + pair) * PAIR :][:, :PAIR] for k in range(tp)]
        got = [pieces[0]] + [around(pieces[k], -k) for k in range(1, tp)]
        returned.append(jnp.concatenate(got, axis=0))
    mixing_grad = tn(by_distance(mixing_back), mixed_in).astype(BF16)
    mixing_grad = mixing_grad.reshape(seq, part, tp, own).transpose(2, 0, 1, 3)
    mixing_sum = Scatter(mixing_grad[:, : seq // 2], mixing_grad[:, seq // 2 :], -1)

    returned[0], ready_down, ready_up = tied(returned[0], down_sum.merge(), up_sum.merge())
    down_sum.send(ready_down)
    up_sum.send(ready_up)
    halves = []
    for pair in range(2):
        _, (v, vcol) = values_of(pair)
        _, turned, logs = attended[pair]
        dq, gone, dk, dv = back_early(
            meta, start, qkv, pair, early, pair, v, vcol, returned[pair], turned, logs, tokens, tp
        )
        halves.append((dq, dk, dv, along(gone, -1)))
    halves[0], ready_down, ready_mixing = tied(halves[0], down_sum.merge(), mixing_sum.merge())
    down_sum.send(ready_down)
    mixing_sum.send(ready_mixing)
    packets, column_sums, pieces = [], [], []
    skip_gradient = None
    for pair in range(2):
        (v, vcol), _ = values_of(pair)
        _, turned, logs = attended[pair]
        packed, values, sums = back_late(
            meta, start, qkv, pair, qkv, kcol + pair, v, vcol, returned[pair], turned, logs,
            *halves[pair], pair == 0, tokens, tp,
        )
        if pair == 0:
            halves[1], packed, ready_up, ready_mixing = tied(
                halves[1], packed, up_sum.merge(), mixing_sum.merge()
            )
            up_sum.send(ready_up)
            mixing_sum.send(ready_mixing)
        else:
            skip_gradient = values
            packed, sums, ready_up, ready_mixing = tied(
                packed, sums, up_sum.merge(), mixing_sum.merge()
            )
        packets.append(packed)
        column_sums.append(sums[0])
        blocks = packed.reshape(tp, rows, packed.shape[1])
        pieces.append([blocks[0]] + [around(blocks[k], k) for k in range(1, tp)])
    up_sum.send(ready_up)
    mixing_sum.send(ready_mixing)
    first_back = nn(jnp.concatenate(pieces[0], axis=1), shares[0])
    first_back = first_back + nn(jnp.concatenate(pieces[1], axis=1), shares[1])
    down_gradient = down_sum.result().T
    up_gradient = up_sum.result()
    mixing_gradient = mixing_sum.result().T

    stream_gradient = middle_back + norm_back(first_back, first_gain, first_hat, first_inverse)
    wide_grad = jnp.concatenate([tn(normed, packed) for packed in packets], axis=1)
    weight_grad = scatter_seq(
        wide_grad.astype(BF16).reshape(seq, part, wide_grad.shape[1]), seq_place
    ).astype(F32)
    query_gradient = jnp.concatenate(
        (weight_grad[:, :PAIR], weight_grad[:, 3 * PAIR : 4 * PAIR]), axis=1
    )
    key_gradient = jnp.concatenate(
        (weight_grad[:, PAIR : 2 * PAIR], weight_grad[:, 4 * PAIR :]), axis=1
    )
    value_gradient = weight_grad[:, 2 * PAIR : 3 * PAIR]

    column_sum = jnp.concatenate(column_sums)
    columns = qkv_turned.T.astype(F32)
    first_shift_part = jnp.sum(columns * column_sum, axis=1)
    hat_grad = (wide_grad - first_shift[:, None] * column_sum) / first_gain[:, None]
    first_gain_part = jnp.sum(columns * hat_grad, axis=1)

    def widen(value):
        size = value.shape[0]
        return lax.dynamic_update_slice_in_dim(
            jnp.zeros((size * tp,), F32), value, tp_place * size, 0
        )

    def total(parts):
        sums = summed(jnp.concatenate(parts).reshape(-1, PAIR)).reshape(-1)
        cuts, offset = [], 0
        for value in parts:
            cuts.append(sums[offset : offset + value.shape[0]])
            offset += value.shape[0]
        return cuts

    up_bias_grad = up_bias_grad.reshape(tp, width)
    up_bias_grad = jnp.concatenate([pick(up_bias_grad, (k - tp_place) % tp, 0) for k in range(tp)])
    query_part = jnp.concatenate((column_sum[:PAIR], column_sum[3 * PAIR : 4 * PAIR]))
    (
        second_gain_grad, second_shift_grad, mixing_bias_grad, down_bias_grad, up_bias_grad,
        first_gain_grad, first_shift_grad, query_bias_grad, value_bias_grad,
    ) = total(
        [
            jnp.sum(second_back * second_hat, axis=0),
            jnp.sum(second_back, axis=0),
            jnp.sum(middle_back, axis=0),
            jnp.sum(upstream, axis=0),
            up_bias_grad,
            first_gain_part,
            first_shift_part,
            widen(query_part),
            widen(column_sum[2 * PAIR : 3 * PAIR]),
        ]
    )
    return (
        output,
        stream_gradient,
        skip_gradient,
        query_gradient,
        query_bias_grad,
        key_gradient,
        value_gradient,
        value_bias_grad,
        mixing_gradient,
        mixing_bias_grad,
        first_gain_grad,
        first_shift_grad,
        second_gain_grad,
        second_shift_grad,
        up_gradient,
        up_bias_grad,
        down_gradient,
        down_bias_grad,
    )


def solution(mesh):
    split = P(("seq", "tp"), None)
    column = P(None, "tp")
    in_specs = (
        split, P(), P("seq", "tp"), P(), P(), column, P("tp"), column, column, P("tp"),
        P("tp", None), P(), P(), P(), column, P("tp"), P("tp", None), P(), split,
    )
    tile = P("seq", "tp")
    out_specs = (
        split, split, tile, tile, P(), tile, tile, P(), P("tp", "seq"), P(), P(), P(), P(), P(),
        tile, P(), P("tp", "seq"), P(),
    )
    return jax.shard_map(local, mesh=mesh, in_specs=in_specs, out_specs=out_specs, check_vma=False)
```

```python
import functools

import jax
import jax.numpy as jnp
from jax import lax
from jax.experimental import pallas as pl
from jax.experimental.pallas import tpu as pltpu
from jax.sharding import PartitionSpec as P

HEAD = 64
DOC_MAX = 1024
PAIR = 2 * HEAD
TILE = 256
UNIT = 512
EPSILON = 1e-05
F32 = jnp.float32
BF16 = jnp.bfloat16
SCALE = HEAD ** -0.5
GELU_A = 0.7978845608028654
GELU_B = 0.044715
SEQ = ("run", "core")


def dot(a, b, dims, out=F32):
    return lax.dot_general(a, b, (dims, ((), ())), preferred_element_type=out)


def nn(a, b):
    return dot(a, b, ((1,), (0,)))


def nt(a, b):
    return dot(a, b, ((1,), (1,)))


def tn(a, b):
    return dot(a, b, ((0,), (0,)))


def light(bytes_accessed):
    return pl.CostEstimate(flops=1, bytes_accessed=bytes_accessed, transcendentals=0)


ANY = pl.BlockSpec(memory_space=pl.ANY)


def project_kernel(slot, place_ref, piece_ref, weight_ref, bias_ref, *rest):
    qkv_ref, normed_ref = rest[-2:]
    piece = piece_ref[...]
    qkv_ref[...] = (nn(piece, weight_ref[...]) + bias_ref[...]).astype(BF16)
    normed_ref[...] = piece


def project(k, count, place, piece, weight, bias, earlier):
    rows, width = piece.shape
    cols = weight.shape[1]
    slot = (count - k) % count
    tile = rows // 2
    alias = earlier is not None
    return pl.pallas_call(
        functools.partial(project_kernel, slot),
        grid_spec=pltpu.PrefetchScalarGridSpec(
            num_scalar_prefetch=1,
            grid=(2,),
            in_specs=[
                pl.BlockSpec((tile, width), lambda i, p: (i, 0)),
                pl.BlockSpec((width, cols), lambda i, p: (0, 0)),
                pl.BlockSpec((1, cols), lambda i, p: (0, 0)),
            ]
            + ([ANY, ANY] if alias else []),
            out_specs=[
                pl.BlockSpec((tile, cols), lambda i, p: (2 * lax.rem(p[0] + slot, count) + i, 0)),
                pl.BlockSpec((tile, width), lambda i, p: (2 * slot + i, 0)),
            ],
        ),
        out_shape=[
            jax.ShapeDtypeStruct((count * rows, cols), BF16),
            jax.ShapeDtypeStruct((count * rows, width), BF16),
        ],
        input_output_aliases={4: 0, 5: 1} if alias else {},
        cost_estimate=light(4 * rows * width),
        name="project",
    )(place, piece, weight, bias, *(earlier if alias else ()))


def wide(tile):
    lane = lax.broadcasted_iota(jnp.int32, tile.shape, 1)
    zero = jnp.zeros_like(tile)
    return jnp.concatenate(
        (jnp.where(lane < HEAD, tile, zero), jnp.where(lane < HEAD, zero, tile)), axis=0
    )


def both(row):
    return jnp.concatenate((row, row), axis=1)


def heads_of(acc):
    return jnp.concatenate((acc[:HEAD, :TILE], acc[HEAD:, TILE:]), axis=0)


def mask_rows(start_ref, step, shift):
    start = both(start_ref[...] - shift)
    place = both((step + 4) * TILE + lax.broadcasted_iota(jnp.int32, (1, TILE), 1))
    return start, place


def allowed(tile_index, start, place):
    key = tile_index * TILE + lax.broadcasted_iota(jnp.int32, (TILE, 2 * TILE), 0)
    return (key >= start) & (key <= place)


def turn(tile, meta_ref, tiles, per, count):
    block = tile // per
    return per * lax.rem(block - meta_ref[tiles] + count, count) + lax.rem(tile, per)


def attend_kernel(base, shift, meta_ref, start_ref, q_ref, k_ref, v_ref, *rest):
    o_ref, turned_ref, log_ref, acc_ref = rest[-4:]
    step = pl.program_id(0)
    query = wide(q_ref[...] * jnp.asarray(SCALE, BF16))
    start, place = mask_rows(start_ref, step, shift)
    acc_ref[...] = jnp.zeros_like(acc_ref)

    def body(j, carried):
        top, total = carried
        rows = pl.ds(pl.multiple_of(j * TILE, TILE), TILE)
        scores = nt(k_ref[rows, :], query)
        scores = jnp.where(allowed(j, start, place), scores, -1e30)
        new_top = jnp.maximum(top, jnp.max(scores, axis=0, keepdims=True))
        part = jnp.exp(scores - new_top)
        factor = jnp.exp(top - new_top)
        total = total * factor + jnp.sum(part, axis=0, keepdims=True)
        acc_ref[...] = acc_ref[...] * factor + tn(v_ref[rows, :], part.astype(BF16))
        return new_top, total

    top, total = lax.fori_loop(
        meta_ref[base + step] - shift // TILE,
        step + 5,
        body,
        (jnp.full((1, 2 * TILE), -1e30, F32), jnp.zeros((1, 2 * TILE), F32)),
    )
    turned = heads_of(acc_ref[...] / total)
    turned_ref[...] = turned
    o_ref[...] = turned.T.astype(BF16)
    logs = top + jnp.log(total)
    log_ref[0:1, :] = logs[:, :TILE]
    log_ref[1:2, :] = logs[:, TILE:]


def attend(base, shift, meta, start, q, qcol, k, kcol, v, vcol, earlier, tokens, count):
    n = k.shape[0]
    steps = (n - DOC_MAX) // TILE
    tiles = tokens // TILE
    per = tiles // count
    alias = earlier is not None
    specs = [
        pl.BlockSpec((1, TILE), lambda i, m: (0, base + i)),
        pl.BlockSpec((TILE, PAIR), lambda i, m: (base + i, qcol)),
        pl.BlockSpec((n, PAIR), lambda i, m: (0, kcol)),
        pl.BlockSpec((n, PAIR), lambda i, m: (0, vcol)),
    ] + [ANY] * (3 if alias else 0)
    return pl.pallas_call(
        functools.partial(attend_kernel, base, shift),
        grid_spec=pltpu.PrefetchScalarGridSpec(
            num_scalar_prefetch=1,
            grid=(steps,),
            in_specs=specs,
            out_specs=[
                pl.BlockSpec((TILE, PAIR), lambda i, m: (turn(base + i, m, tiles, per, count), 0)),
                pl.BlockSpec((PAIR, TILE), lambda i, m: (0, base + i)),
                pl.BlockSpec((8, TILE), lambda i, m: (0, base + i)),
            ],
            scratch_shapes=[pltpu.VMEM((PAIR, 2 * TILE), F32)],
        ),
        out_shape=[
            jax.ShapeDtypeStruct((tokens, PAIR), BF16),
            jax.ShapeDtypeStruct((PAIR, tokens), F32),
            jax.ShapeDtypeStruct((8, tokens), F32),
        ],
        input_output_aliases={5: 0, 6: 1, 7: 2} if alias else {},
        cost_estimate=light(4 * n * PAIR),
        name="attend",
    )(meta, start, q, k, v, *(earlier if alias else ()))


def back_tile(shift, low, start_ref, q_ref, k_ref, v_ref, do_ref, turned_ref, log_ref, dk_ref, dv_ref, acc_ref):
    step = pl.program_id(0)
    query = wide(q_ref[...] * jnp.asarray(SCALE, BF16))
    out_back = wide(do_ref[...])
    start, place = mask_rows(start_ref, step, shift)
    product = do_ref[...].astype(F32).T * turned_ref[...]
    delta = jnp.concatenate(
        (
            jnp.sum(product[:HEAD], axis=0, keepdims=True),
            jnp.sum(product[HEAD:], axis=0, keepdims=True),
        ),
        axis=1,
    )
    logs = jnp.concatenate((log_ref[0:1, :], log_ref[1:2, :]), axis=1)
    acc_ref[...] = jnp.zeros_like(acc_ref)

    def body(j, carried):
        rows = pl.ds(pl.multiple_of(j * TILE, TILE), TILE)
        key_tile = k_ref[rows, :]
        scores = jnp.where(allowed(j, start, place), nt(key_tile, query), -1e30)
        prob = jnp.exp(scores - logs)
        prob_back = nt(v_ref[rows, :], out_back)
        score_back = (prob * (prob_back - delta)).astype(BF16)
        dv_ref[rows, :] += nn(prob.astype(BF16), out_back)
        dk_ref[rows, :] += nn(score_back, query)
        acc_ref[...] += tn(key_tile, score_back)
        return carried

    lax.fori_loop(low, step + 5, body, 0)
    return (heads_of(acc_ref[...]) * SCALE).T.astype(BF16)


def early_kernel(meta_ref, start_ref, q_ref, k_ref, v_ref, do_ref, turned_ref, log_ref, dq_ref, gone_ref, dk_ref, dv_ref, kept_k, kept_v, acc_ref):
    step = pl.program_id(0)

    @pl.when(step == 0)
    def _():
        kept_k[...] = jnp.zeros_like(kept_k)
        kept_v[...] = jnp.zeros_like(kept_v)

    dq_ref[...] = back_tile(
        0, meta_ref[step], start_ref, q_ref, k_ref, v_ref, do_ref, turned_ref, log_ref,
        kept_k, kept_v, acc_ref,
    )

    @pl.when(step == pl.num_programs(0) - 1)
    def _():
        gone_ref[:, :PAIR] = kept_k[:DOC_MAX, :].astype(BF16)
        gone_ref[:, PAIR:] = kept_v[:DOC_MAX, :].astype(BF16)
        dk_ref[...] = kept_k[DOC_MAX:, :]
        dv_ref[...] = kept_v[DOC_MAX:, :]


def late_kernel(base, fresh, per, count, meta_ref, start_ref, q_ref, k_ref, v_ref, do_ref, turned_ref, log_ref, dq_in, dk_in, dv_in, back_ref, packed_ref, value_ref, sums_ref, kept_k, kept_v, acc_ref):
    step = pl.program_id(0)
    held = dk_in.shape[0]
    tiles = packed_ref.shape[0] // TILE

    def rows_of(tile):
        row = turn(tile, meta_ref, tiles, per, count) * TILE
        return pl.ds(pl.multiple_of(row, TILE), TILE)

    @pl.when(step == 0)
    def _():
        kept_k[:held, :] = dk_in[...]
        kept_v[:held, :] = dv_in[...]
        kept_k[held:, :] = back_ref[:, :PAIR].astype(F32)
        kept_v[held:, :] = back_ref[:, PAIR:].astype(F32)
        for i in range(base):
            packed_ref[rows_of(i), :PAIR] = dq_in[i * TILE : (i + 1) * TILE, :]

    packed_ref[rows_of(base + step), :PAIR] = back_tile(
        DOC_MAX, meta_ref[base + step] - DOC_MAX // TILE, start_ref, q_ref, k_ref, v_ref, do_ref,
        turned_ref, log_ref, kept_k, kept_v, acc_ref,
    )

    @pl.when(step == pl.num_programs(0) - 1)
    def _():
        for i in range(tiles):
            span = slice(i * TILE, (i + 1) * TILE)
            packed_ref[rows_of(i), PAIR : 2 * PAIR] = kept_k[span, :].astype(BF16)
            if fresh:
                packed_ref[rows_of(i), 2 * PAIR :] = kept_v[span, :].astype(BF16)
        if not fresh:
            value_ref[...] = kept_v[...]
        else:
            value_ref[...] = jnp.zeros_like(value_ref)
        sums_ref[...] = jnp.broadcast_to(
            jnp.sum(packed_ref[...].astype(F32), axis=0, keepdims=True), sums_ref.shape
        )


def back_specs(base, qcol, n, kcol, vcol, tiles, per, count):
    return [
        pl.BlockSpec((1, TILE), lambda i, m: (0, base + i)),
        pl.BlockSpec((TILE, PAIR), lambda i, m: (base + i, qcol)),
        pl.BlockSpec((n, PAIR), lambda i, m: (0, kcol)),
        pl.BlockSpec((n, PAIR), lambda i, m: (0, vcol)),
        pl.BlockSpec((TILE, PAIR), lambda i, m: (turn(base + i, m, tiles, per, count), 0)),
        pl.BlockSpec((PAIR, TILE), lambda i, m: (0, base + i)),
        pl.BlockSpec((8, TILE), lambda i, m: (0, base + i)),
    ]


def whole(shape):
    return pl.BlockSpec(shape, lambda i, m: (0,) * len(shape))


def back_early(meta, start, q, qcol, k, kcol, v, vcol, do, turned, logs, tokens, count):
    n = k.shape[0]
    held = n - DOC_MAX
    tiles = tokens // TILE
    return pl.pallas_call(
        early_kernel,
        grid_spec=pltpu.PrefetchScalarGridSpec(
            num_scalar_prefetch=1,
            grid=(held // TILE,),
            in_specs=back_specs(0, qcol, n, kcol, vcol, tiles, tiles // count, count),
            out_specs=[
                pl.BlockSpec((TILE, PAIR), lambda i, m: (i, 0)),
                whole((DOC_MAX, 2 * PAIR)),
                whole((held, PAIR)),
                whole((held, PAIR)),
            ],
            scratch_shapes=[
                pltpu.VMEM((n, PAIR), F32),
                pltpu.VMEM((n, PAIR), F32),
                pltpu.VMEM((PAIR, 2 * TILE), F32),
            ],
        ),
        out_shape=[
            jax.ShapeDtypeStruct((held, PAIR), BF16),
            jax.ShapeDtypeStruct((DOC_MAX, 2 * PAIR), BF16),
            jax.ShapeDtypeStruct((held, PAIR), F32),
            jax.ShapeDtypeStruct((held, PAIR), F32),
        ],
        cost_estimate=light(12 * n * PAIR),
        name="back_early",
    )(meta, start, q, k, v, do, turned, logs)


def back_late(meta, start, q, qcol, k, kcol, v, vcol, do, turned, logs, dq, dk, dv, back, fresh, tokens, count):
    n = k.shape[0]
    held = n - DOC_MAX
    tiles = tokens // TILE
    per = tiles // count
    base = (tokens - held) // TILE
    cols = (3 if fresh else 2) * PAIR
    return pl.pallas_call(
        functools.partial(late_kernel, base, fresh, per, count),
        grid_spec=pltpu.PrefetchScalarGridSpec(
            num_scalar_prefetch=1,
            grid=(held // TILE,),
            in_specs=back_specs(base, qcol, n, kcol, vcol, tiles, per, count)
            + [whole(dq.shape), whole(dk.shape), whole(dv.shape), whole(back.shape)],
            out_specs=[
                whole((tokens, cols)),
                whole((8, PAIR) if fresh else (tokens, PAIR)),
                whole((8, cols)),
            ],
            scratch_shapes=[
                pltpu.VMEM((n, PAIR), F32),
                pltpu.VMEM((n, PAIR), F32),
                pltpu.VMEM((PAIR, 2 * TILE), F32),
            ],
        ),
        out_shape=[
            jax.ShapeDtypeStruct((tokens, cols), BF16),
            jax.ShapeDtypeStruct((8, PAIR) if fresh else (tokens, PAIR), F32),
            jax.ShapeDtypeStruct((8, cols), F32),
        ],
        cost_estimate=light(12 * n * PAIR),
        name="back_late",
    )(meta, start, q, k, v, do, turned, logs, dq, dk, dv, back)


def store_grad(grad_ref, grad):
    runs, _, lanes, rows, cols = grad_ref.shape
    for j in range(lanes):
        grad_ref[:, 0, j] = grad[:, j * cols : (j + 1) * cols].reshape(runs, rows, cols)


def accumulate(ref, value):
    @pl.when(pl.program_id(0) == 0)
    def _():
        ref[...] = value

    @pl.when(pl.program_id(0) > 0)
    def _():
        ref[...] += value


def up_kernel(places_ref, sn_ref, got_ref, cot_ref, up_ref, bias_ref, down_ref, out_ref, other_ref, slope_ref, grad_ref, act_ref):
    width = up_ref.shape[0] * up_ref.shape[1]
    rows = sn_ref.shape[0]
    up = up_ref[...].reshape(width, UNIT)
    down = down_ref[...].reshape(UNIT, width)
    for i, (piece_ref, sum_ref) in enumerate(((sn_ref, out_ref), (got_ref, other_ref))):
        span = slice(i * rows, (i + 1) * rows)
        hidden = nn(piece_ref[...], up) + bias_ref[0]
        square = hidden * hidden
        curve = jnp.tanh(GELU_A * (hidden + GELU_B * (hidden * square)))
        half = 0.5 * (1.0 + curve)
        activated = (hidden * half).astype(BF16)
        slope_ref[span, :] = half + 0.5 * hidden * (1.0 - curve * curve) * (
            GELU_A * (1.0 + 3.0 * GELU_B * square)
        )
        act_ref[span, :] = activated
        accumulate(sum_ref, nn(activated, down))
    store_grad(grad_ref, nn(cot_ref[...], act_ref[...]).astype(BF16))


def feed_specs(gathered, seq, parts, width):
    part = width // seq
    per = width // UNIT
    run = seq // 2

    def spot(i, p):
        return lax.rem(p[0] + i, parts)

    def grad_spec(kind):
        return pl.BlockSpec(
            (run, 1, UNIT // PAIR, width // run, PAIR), lambda i, p: (0, spot(i, p), kind, 0, 0)
        )

    grad = jax.ShapeDtypeStruct((run, parts, 2 * UNIT // PAIR, width // run, PAIR), BF16)
    return (
        pl.BlockSpec((seq, part, UNIT), lambda i, p: (spot(i, p), 0, p[1])),
        pl.BlockSpec((UNIT // part, part, width), lambda i, p: (spot(i, p) * per + p[1], 1, 0)),
        grad_spec,
        grad,
    )


def fixed(shape):
    return pl.BlockSpec(shape, lambda i, p: (0,) * len(shape))


def feed_up(places, sn, got, cot_turned, gathered, bias, seq, parts):
    rows, width = sn.shape
    up_spec, down_spec, grad_spec, grad = feed_specs(gathered, seq, parts, width)
    return pl.pallas_call(
        up_kernel,
        grid_spec=pltpu.PrefetchScalarGridSpec(
            num_scalar_prefetch=1,
            grid=(parts,),
            in_specs=[
                fixed((rows, width)),
                fixed((rows, width)),
                fixed((width, 2 * rows)),
                up_spec,
                pl.BlockSpec((1, 1, UNIT), lambda i, p: (lax.rem(parts - i, parts), 0, p[1])),
                down_spec,
            ],
            out_specs=[
                fixed((rows, width)),
                fixed((rows, width)),
                pl.BlockSpec((2 * rows, UNIT), lambda i, p: (0, i)),
                grad_spec(0),
            ],
            scratch_shapes=[pltpu.VMEM((2 * rows, UNIT), BF16)],
        ),
        out_shape=[
            jax.ShapeDtypeStruct((rows, width), F32),
            jax.ShapeDtypeStruct((rows, width), F32),
            jax.ShapeDtypeStruct((2 * rows, parts * UNIT), F32),
            grad,
        ],
        cost_estimate=light(16 * rows * width),
        name="feed_up",
    )(places, sn, got, cot_turned, gathered, bias, gathered)


def down_kernel(places_ref, cot_ref, cot_got_ref, sn_ref, got_ref, slope_ref, up_ref, down_ref, grads_ref, back_ref, other_ref, grad_ref, bias_ref, turned_ref, hidden_ref):
    width = up_ref.shape[0] * up_ref.shape[1]
    rows = sn_ref.shape[0]

    @pl.when(pl.program_id(0) == 0)
    def _():
        turned_ref[:, :rows] = sn_ref[...].T
        turned_ref[:, rows:] = got_ref[...].T

    up = up_ref[...].reshape(width, UNIT)
    down = down_ref[...].reshape(UNIT, width)
    total = jnp.zeros((1, UNIT), F32)
    for i, (piece_ref, sum_ref) in enumerate(((cot_ref, back_ref), (cot_got_ref, other_ref))):
        span = slice(i * rows, (i + 1) * rows)
        rounded = (nt(piece_ref[...], down) * slope_ref[span, :]).astype(BF16)
        total = total + jnp.sum(rounded.astype(F32), axis=0, keepdims=True)
        hidden_ref[span, :] = rounded
        accumulate(sum_ref, nt(rounded, up))
    bias_ref[0] = total
    store_grad(grad_ref, nn(turned_ref[...], hidden_ref[...]).astype(BF16))


def feed_down(places, cot, cot_got, sn, got, slope, gathered, grads, seq, parts):
    rows, width = cot.shape
    up_spec, down_spec, grad_spec, grad = feed_specs(gathered, seq, parts, width)
    return pl.pallas_call(
        down_kernel,
        grid_spec=pltpu.PrefetchScalarGridSpec(
            num_scalar_prefetch=1,
            grid=(parts,),
            in_specs=[fixed((rows, width))] * 4
            + [
                pl.BlockSpec((2 * rows, UNIT), lambda i, p: (0, i)),
                up_spec,
                down_spec,
                ANY,
            ],
            out_specs=[
                fixed((rows, width)),
                fixed((rows, width)),
                grad_spec(1),
                pl.BlockSpec((1, 1, UNIT), lambda i, p: (i, 0, 0)),
            ],
            scratch_shapes=[
                pltpu.VMEM((width, 2 * rows), BF16),
                pltpu.VMEM((2 * rows, UNIT), BF16),
            ],
        ),
        out_shape=[
            jax.ShapeDtypeStruct((rows, width), F32),
            jax.ShapeDtypeStruct((rows, width), F32),
            grad,
            jax.ShapeDtypeStruct((parts, 1, UNIT), F32),
        ],
        input_output_aliases={8: 2},
        cost_estimate=light(16 * rows * width),
        name="feed_down",
    )(places, cot, cot_got, sn, got, slope, gathered, gathered, grads)


def around(value, steps):
    count = lax.axis_size("tp")
    return lax.ppermute(value, "tp", [(i, (i + steps) % count) for i in range(count)])


def flipped(value, axis, bit):
    count = lax.axis_size(axis)
    return lax.ppermute(value, axis, [(i, i ^ bit) for i in range(count)])


def along(value, steps):
    count = lax.axis_size(SEQ)
    first, last = max(0, -steps), min(count, count - steps)
    return lax.ppermute(value, SEQ, [(i, i + steps) for i in range(first, last)])


def summed(value):
    for axis in (SEQ, "tp"):
        bit = 1
        while bit < lax.axis_size(axis):
            value = value + flipped(value, axis, bit)
            bit *= 2
    return value


def halves_order(seq):
    return list(range(1, seq, 2)) + list(range(0, seq, 2))


def pick(value, index, dim):
    return lax.dynamic_index_in_dim(value, index, dim, keepdims=False)


def joined(a, b):
    return (a.astype(F32) + b.astype(F32)).astype(BF16)


def seq_bits():
    bits, bit = [], 1
    while bit < lax.axis_size(SEQ):
        bits.append(bit)
        bit *= 2
    return bits


class Scatter:
    def __init__(self, sent, kept, sign):
        self.sign = sign
        left = list(range(0, lax.axis_size(SEQ), 2))
        got = flipped(sent, SEQ, 1)
        cut = kept.shape[0] // 2
        tail = seq_bits()[1:]
        self.lanes = [
            (kept[:cut], got[:cut], left, tail),
            (kept[cut:], got[cut:], left, tail[1:] + tail[:1]),
        ]
        self.moves = None

    def merge(self):
        arrays, plans = [], []
        for kept, got, left, bits in self.lanes:
            if not bits:
                arrays.append(joined(kept, got))
                plans.append(None)
                continue
            bit = bits[0]
            goes = [i for i, r in enumerate(left) if r & bit]
            stays = [i for i, r in enumerate(left) if not r & bit]

            def some(array, spots):
                return jnp.concatenate([array[:, i : i + 1] for i in spots], axis=1)

            for spots in (goes, stays):
                arrays.append(joined(some(kept, spots), some(got, spots)))
            plans.append(([left[i] for i in stays], bits))
        self.plans = plans
        return tuple(arrays)

    def send(self, arrays):
        arrays = list(arrays)
        if self.plans[0] is None:
            blocks = [part[i, 0] for part in arrays for i in range(part.shape[0])]
            self.blocks = [blocks[0]] + [
                around(blocks[k], self.sign * k) for k in range(1, len(blocks))
            ]
            self.lanes = None
            return
        lanes = []
        for left, bits in self.plans:
            goes, stays = arrays.pop(0), arrays.pop(0)
            lanes.append((stays, flipped(goes, SEQ, bits[0]), left, bits[1:]))
        self.lanes = lanes

    def result(self):
        while self.lanes is not None:
            self.send(self.merge())
        total = self.blocks[0].astype(F32)
        for block in self.blocks[1:]:
            total = total + block.astype(F32)
        return total


def tied(*groups):
    return lax.optimization_barrier(groups)


def scatter_seq(value, place):
    bits = seq_bits()
    left = value.reshape((2,) * len(bits) + value.shape[1:])
    for spot, bit in enumerate(bits):
        dim = len(bits) - 1 - spot
        mine = (place // bit) % 2
        left = joined(pick(left, mine, dim), flipped(pick(left, 1 - mine, dim), SEQ, bit))
    return left


def swapped(value, bit, place, dim):
    other = flipped(value, SEQ, bit)
    low = (place // bit) % 2 == 0
    return jnp.stack((jnp.where(low, value, other), jnp.where(low, other, value)), axis=dim)


def quarter(shard, place):
    size = shard.shape[0] // 4
    spot = 2 * ((place // 2) % 2) + place % 2
    return lax.dynamic_slice_in_dim(shard, spot * size, size, 0)


def shards(own, piece, place):
    got = jnp.stack([around(piece, k) for k in range(1, lax.axis_size("tp"))])
    got = swapped(swapped(got, 2, place, 1), 1, place, 2)
    return jnp.concatenate((own[None], got.reshape((-1,) + own.shape)), axis=0)


def center(rows):
    average = jnp.mean(rows, axis=-1, keepdims=True)
    centered = rows - average
    inverse = lax.rsqrt(jnp.mean(centered * centered, axis=-1, keepdims=True) + EPSILON)
    return centered * inverse, inverse


def norm_back(grad, gain, xhat, inverse):
    e = grad * gain
    return inverse * (
        e
        - jnp.mean(e, axis=-1, keepdims=True)
        - xhat * jnp.mean(e * xhat, axis=-1, keepdims=True)
    )


def local(
    stream, segments, skip_values, first_gain, first_shift, query_weight, query_bias, key_weight,
    value_weight, value_bias, mixing_weight, mixing_bias, second_gain, second_shift, up_weight,
    up_bias, down_weight, down_bias, cotangent,
):
    rows, width = stream.shape
    tokens = skip_values.shape[0]
    own = query_weight.shape[1]
    tp = lax.axis_size("tp")
    seq = lax.axis_size(SEQ)
    seq_place = lax.axis_index(SEQ)
    tp_place = lax.axis_index("tp")
    core = lax.axis_index("core")
    places = jnp.stack((tp_place, core)).astype(jnp.int32)
    half = tokens - DOC_MAX
    part = width // seq
    kcol = own // PAIR

    stream_wide = stream.astype(F32)
    first_hat, first_inverse = center(stream_wide)
    piece = (first_hat * first_gain + first_shift).astype(BF16)
    piece, up_weight, down_weight, mixing_weight, segments, cotangent = lax.optimization_barrier(
        (piece, up_weight, down_weight, mixing_weight, segments, cotangent)
    )

    def own_rows(shard):
        size = shard.shape[0] // seq
        return lax.dynamic_slice_in_dim(shard, seq_place * size, size, 0)

    packet = jnp.concatenate([own_rows(w) for w in (up_weight, down_weight)], axis=0)
    qkv_turned = jnp.concatenate(
        (
            query_weight[:, :PAIR], key_weight[:, :PAIR], value_weight,
            query_weight[:, PAIR:], key_weight[:, PAIR:],
        ),
        axis=1,
    ).T
    qkv_piece = quarter(qkv_turned, seq_place)
    bias_pieces = jnp.stack([up_bias] + [around(up_bias, k) for k in range(1, tp)])[:, None]
    cot_got = flipped(cotangent, "core", 1)
    cot_turned = jnp.concatenate((cotangent, cot_got), axis=0).T

    padded = jnp.concatenate((jnp.full((DOC_MAX,), -1, jnp.int32), segments))
    window = lax.dynamic_slice_in_dim(padded, seq_place * tokens, DOC_MAX + tokens, 0)
    start = jnp.sum(
        (window[:, None] < window[None, DOC_MAX:]).astype(jnp.int32), axis=0, keepdims=True
    )
    meta = jnp.concatenate((start[0, ::TILE] // TILE, places))
    halo_skip = along(skip_values[half:], 1)
    skip_early = jnp.concatenate((halo_skip, skip_values[:half]), axis=0)

    wqkv = jnp.concatenate((query_weight, key_weight, value_weight), axis=1)
    bias = jnp.concatenate((query_bias, jnp.zeros((own,), F32), value_bias))[None]
    made = None
    for k in range(tp):
        if k == tp - 1:
            (
                piece, meta, start, skip_early, bias_pieces, cot_got, cot_turned, qkv_piece,
                mixing_piece,
            ) = tied(
                piece, meta, start, skip_early, bias_pieces, cot_got, cot_turned, qkv_piece,
                quarter(mixing_weight, seq_place),
            )
        ahead = around(piece, 1) if k < tp - 1 else None
        made = project(k, tp, places, piece, wqkv, bias, made)
        piece = ahead
        if k == 0:
            piece, packet = tied(piece, packet)
            gathered = lax.all_gather(packet, ("tp",) + SEQ, axis=0, tiled=False)
    qkv, normed = made
    mixing_rot = shards(mixing_weight, mixing_piece, seq_place).reshape(tp * own, width)

    halo = along(qkv[half:, own:], 1)
    early = jnp.concatenate((halo, qkv[:half, own:]), axis=0)

    def values_of(pair):
        if pair == 0:
            return (qkv, 2 * kcol), (early, kcol)
        return (skip_values, 0), (skip_early, 0)

    steps = half // TILE
    attended = []
    for pair in range(2):
        (v, vcol), _ = values_of(pair)
        attended.append(
            attend(steps, DOC_MAX, meta, start, qkv, pair, qkv, kcol + pair, v, vcol, None, tokens, tp)
        )
    arrived = []
    for pair in range(2):
        _, (v, vcol) = values_of(pair)
        attended[pair] = attend(
            0, 0, meta, start, qkv, pair, early, pair, v, vcol, attended[pair], tokens, tp
        )
        blocks = attended[pair][0].reshape(tp, rows, PAIR)
        arrived.append([blocks[0]] + [around(blocks[k], k) for k in range(1, tp)])

    mixed_in = jnp.concatenate([arrived[pair][k] for k in range(tp) for pair in range(2)], axis=1)
    middle = stream_wide + nn(mixed_in, mixing_rot) + mixing_bias
    second_hat, second_inverse = center(middle)
    second = (second_hat * second_gain + second_shift).astype(BF16)

    def by_distance(value):
        cut = value.reshape(rows, seq, part)
        return jnp.concatenate([pick(cut, seq_place ^ r, 1) for r in halves_order(seq)], axis=1)

    got = flipped(second, "core", 1)
    lost, lost_other, slope, grads = feed_up(
        places, second, got, cot_turned, gathered, bias_pieces, seq, tp
    )
    qkv_piece, lost_other = tied(qkv_piece, lost_other)
    output = (middle + (lost + flipped(lost_other, "core", 1)) + down_bias).astype(BF16)
    second_back, back_other, grads, up_bias_grad = feed_down(
        places, cotangent, cot_got, second, got, slope, gathered, grads, seq, tp
    )
    qkv_full = shards(qkv_turned, qkv_piece, seq_place)
    shares = [
        qkv_full[:, cut].reshape(-1, width) for cut in (slice(0, 3 * PAIR), slice(3 * PAIR, None))
    ]
    back_other, grads = tied(back_other, grads)
    second_back = second_back + flipped(back_other, "core", 1)
    grads = lax.psum_scatter(
        grads.reshape((-1,) + grads.shape[2:]), ("run", "tp"), scatter_dimension=0, tiled=True
    )[0]

    upstream = cotangent.astype(F32)
    middle_back = upstream + norm_back(second_back, second_gain, second_hat, second_inverse)
    mixing_back = middle_back.astype(BF16)
    attended_back = nt(mixing_back, mixing_rot).astype(BF16)
    returned = []
    for pair in range(2):
        pieces = [attended_back[:, (2 * k + pair) * PAIR :][:, :PAIR] for k in range(tp)]
        got = [pieces[0]] + [around(pieces[k], -k) for k in range(1, tp)]
        returned.append(jnp.concatenate(got, axis=0))
    mixing_grad = tn(by_distance(mixing_back), mixed_in).astype(BF16)
    mixing_grad = mixing_grad.reshape(seq, part, tp, own).transpose(2, 0, 1, 3)
    mixing_sum = Scatter(mixing_grad[:, : seq // 2], mixing_grad[:, seq // 2 :], -1)

    halves = []
    for pair in range(2):
        _, (v, vcol) = values_of(pair)
        _, turned, logs = attended[pair]
        dq, gone, dk, dv = back_early(
            meta, start, qkv, pair, early, pair, v, vcol, returned[pair], turned, logs, tokens, tp
        )
        halves.append((dq, dk, dv, along(gone, -1)))
    halves[0], ready_mixing = tied(halves[0], mixing_sum.merge())
    mixing_sum.send(ready_mixing)
    packets, column_sums, pieces = [], [], []
    weight_grads, wide_grads = [], []
    skip_gradient = None
    for pair in range(2):
        (v, vcol), _ = values_of(pair)
        _, turned, logs = attended[pair]
        packed, values, sums = back_late(
            meta, start, qkv, pair, qkv, kcol + pair, v, vcol, returned[pair], turned, logs,
            *halves[pair], pair == 0, tokens, tp,
        )
        if pair == 0:
            halves[1], packed, ready_mixing = tied(halves[1], packed, mixing_sum.merge())
            mixing_sum.send(ready_mixing)
        else:
            skip_gradient = values
            packed, sums, ready_mixing = tied(packed, sums, mixing_sum.merge())
            mixing_sum.send(ready_mixing)
        column_sums.append(sums[0])
        blocks = packed.reshape(tp, rows, packed.shape[1])
        pieces.append([blocks[0]] + [around(blocks[k], k) for k in range(1, tp)])
        wide_grads.append(tn(normed, packed))
        weight_grads.append(
            scatter_seq(wide_grads[pair].astype(BF16).reshape(seq, part, -1), seq_place)
        )
    first_back = nn(jnp.concatenate(pieces[0], axis=1), shares[0])
    first_back = first_back + nn(jnp.concatenate(pieces[1], axis=1), shares[1])
    mixing_gradient = mixing_sum.result().T

    cut = grads.reshape(grads.shape[0], 2, part, PAIR)
    kept = pick(cut, core, 1)
    came = flipped(pick(cut, 1 - core, 1), "core", 1)
    ordered = jnp.stack((jnp.where(core == 0, kept, came), jnp.where(core == 0, came, kept)))
    ordered = ordered.astype(F32).reshape(2, 2, -1, part, PAIR)
    down_gradient = ordered[:, 0].transpose(0, 1, 3, 2).reshape(-1, part)
    up_gradient = ordered[:, 1].transpose(2, 0, 1, 3).reshape(part, -1)

    stream_gradient = middle_back + norm_back(first_back, first_gain, first_hat, first_inverse)
    wide_grad = jnp.concatenate(wide_grads, axis=1)
    weight_grad = jnp.concatenate(weight_grads, axis=1).astype(F32)
    query_gradient = jnp.concatenate(
        (weight_grad[:, :PAIR], weight_grad[:, 3 * PAIR : 4 * PAIR]), axis=1
    )
    key_gradient = jnp.concatenate(
        (weight_grad[:, PAIR : 2 * PAIR], weight_grad[:, 4 * PAIR :]), axis=1
    )
    value_gradient = weight_grad[:, 2 * PAIR : 3 * PAIR]

    column_sum = jnp.concatenate(column_sums)
    columns = qkv_turned.T.astype(F32)
    first_shift_part = jnp.sum(columns * column_sum, axis=1)
    hat_grad = (wide_grad - first_shift[:, None] * column_sum) / first_gain[:, None]
    first_gain_part = jnp.sum(columns * hat_grad, axis=1)

    def widen(value):
        size = value.shape[0]
        return lax.dynamic_update_slice_in_dim(
            jnp.zeros((size * tp,), F32), value, tp_place * size, 0
        )

    def total(parts):
        sums = summed(jnp.concatenate(parts).reshape(-1, PAIR)).reshape(-1)
        cuts, offset = [], 0
        for value in parts:
            cuts.append(sums[offset : offset + value.shape[0]])
            offset += value.shape[0]
        return cuts

    up_bias_grad = up_bias_grad.reshape(tp, UNIT)
    zero = jnp.zeros((UNIT,), F32)
    up_parts = []
    for k in range(tp):
        made_here = pick(up_bias_grad, (k - tp_place) % tp, 0)
        up_parts += [jnp.where(core == 0, made_here, zero), jnp.where(core == 0, zero, made_here)]
    up_bias_grad = jnp.concatenate(up_parts)
    query_part = jnp.concatenate((column_sum[:PAIR], column_sum[3 * PAIR : 4 * PAIR]))
    first_gain_grad, first_shift_grad, query_bias_grad, value_bias_grad = total(
        [
            first_gain_part,
            first_shift_part,
            widen(query_part),
            widen(column_sum[2 * PAIR : 3 * PAIR]),
        ]
    )
    second_gain_grad, second_shift_grad, mixing_bias_grad, down_bias_grad, up_bias_grad = total(
        [
            jnp.sum(second_back * second_hat, axis=0),
            jnp.sum(second_back, axis=0),
            jnp.sum(middle_back, axis=0),
            jnp.sum(upstream, axis=0),
            up_bias_grad,
        ]
    )
    return (
        output,
        stream_gradient,
        skip_gradient,
        query_gradient,
        query_bias_grad,
        key_gradient,
        value_gradient,
        value_bias_grad,
        mixing_gradient,
        mixing_bias_grad,
        first_gain_grad,
        first_shift_grad,
        second_gain_grad,
        second_shift_grad,
        up_gradient,
        up_bias_grad,
        down_gradient,
        down_bias_grad,
    )


def solution(mesh):
    seq, tp = mesh.shape["seq"], mesh.shape["tp"]
    mesh = jax.sharding.Mesh(mesh.devices.reshape(seq // 2, 2, tp), SEQ + ("tp",))
    split = P(SEQ + ("tp",), None)
    column = P(None, "tp")
    tile = P(SEQ, "tp")
    turned = P("tp", SEQ)
    in_specs = (
        split, P(), tile, P(), P(), column, P("tp"), column, column, P("tp"),
        P("tp", None), P(), P(), P(), column, P("tp"), P("tp", None), P(), split,
    )
    out_specs = (
        split, split, tile, tile, P(), tile, tile, P(), turned, P(), P(), P(), P(), P(),
        tile, P(), turned, P(),
    )
    return jax.shard_map(local, mesh=mesh, in_specs=in_specs, out_specs=out_specs, check_vma=False)
```

```python
import functools

import jax
import jax.numpy as jnp
from jax import lax
from jax.experimental import pallas as pl
from jax.experimental.pallas import tpu as pltpu
from jax.sharding import PartitionSpec as P

HEAD = 64
DOC_MAX = 1024
PAIR = 2 * HEAD
TILE = 256
UNIT = 512
EPSILON = 1e-05
F32 = jnp.float32
BF16 = jnp.bfloat16
SCALE = HEAD ** -0.5
GELU_A = 0.7978845608028654
GELU_B = 0.044715
SEQ = ("run", "core")
GATHER_STEP = 1


def dot(a, b, dims, out=F32):
    return lax.dot_general(a, b, (dims, ((), ())), preferred_element_type=out)


def nn(a, b):
    return dot(a, b, ((1,), (0,)))


def nt(a, b):
    return dot(a, b, ((1,), (1,)))


def tn(a, b):
    return dot(a, b, ((0,), (0,)))


def light(bytes_accessed, flops=1):
    return pl.CostEstimate(flops=flops, bytes_accessed=bytes_accessed, transcendentals=0)


ANY = pl.BlockSpec(memory_space=pl.ANY)


def project_kernel(slot, place_ref, piece_ref, weight_ref, bias_ref, *rest):
    qkv_ref, turned_ref = rest[-2:]
    piece = piece_ref[...]
    qkv_ref[...] = (nn(piece, weight_ref[...]) + bias_ref[...]).astype(BF16)
    turned_ref[...] = piece.T


def project(k, count, place, piece, weight, bias, earlier):
    rows, width = piece.shape
    cols = weight.shape[1]
    slot = (count - k) % count
    tile = rows // 2
    alias = earlier is not None
    return pl.pallas_call(
        functools.partial(project_kernel, slot),
        grid_spec=pltpu.PrefetchScalarGridSpec(
            num_scalar_prefetch=1,
            grid=(2,),
            in_specs=[
                pl.BlockSpec((tile, width), lambda i, p: (i, 0)),
                pl.BlockSpec((width, cols), lambda i, p: (0, 0)),
                pl.BlockSpec((1, cols), lambda i, p: (0, 0)),
            ]
            + ([ANY, ANY] if alias else []),
            out_specs=[
                pl.BlockSpec((tile, cols), lambda i, p: (2 * lax.rem(p[0] + slot, count) + i, 0)),
                pl.BlockSpec((width, tile), lambda i, p: (0, 2 * slot + i)),
            ],
        ),
        out_shape=[
            jax.ShapeDtypeStruct((count * rows, cols), BF16),
            jax.ShapeDtypeStruct((width, count * rows), BF16),
        ],
        input_output_aliases={4: 0, 5: 1} if alias else {},
        cost_estimate=light(4 * rows * width, 2 * rows * width * cols),
        name="project",
    )(place, piece, weight, bias, *(earlier if alias else ()))


def turn_kernel(own_ref, got_ref, out_ref):
    rows = own_ref.shape[0]
    out_ref[:, :rows] = own_ref[...].T
    out_ref[:, rows:] = got_ref[...].T


def turn_rows(own, got):
    rows, width = own.shape
    tile = width // 4
    return pl.pallas_call(
        turn_kernel,
        grid=(4,),
        in_specs=[pl.BlockSpec((rows, tile), lambda i: (0, i))] * 2,
        out_specs=pl.BlockSpec((tile, 2 * rows), lambda i: (i, 0)),
        out_shape=jax.ShapeDtypeStruct((width, 2 * rows), BF16),
        cost_estimate=light(8 * rows * width),
        name="turn_rows",
    )(own, got)


def wide(tile):
    lane = lax.broadcasted_iota(jnp.int32, tile.shape, 1)
    zero = jnp.zeros_like(tile)
    return jnp.concatenate(
        (jnp.where(lane < HEAD, tile, zero), jnp.where(lane < HEAD, zero, tile)), axis=0
    )


def both(row):
    return jnp.concatenate((row, row), axis=1)


def heads_of(acc):
    return jnp.concatenate((acc[:HEAD, :TILE], acc[HEAD:, TILE:]), axis=0)


def mask_rows(start_ref, step, shift):
    start = both(start_ref[...] - shift)
    place = both((step + 4) * TILE + lax.broadcasted_iota(jnp.int32, (1, TILE), 1))
    return start, place


def allowed(tile_index, start, place):
    key = tile_index * TILE + lax.broadcasted_iota(jnp.int32, (TILE, 2 * TILE), 0)
    return (key >= start) & (key <= place)


def turn(tile, meta_ref, tiles, per, count):
    block = tile // per
    return per * lax.rem(block - meta_ref[tiles] + count, count) + lax.rem(tile, per)


def attend_kernel(base, shift, meta_ref, start_ref, q_ref, k_ref, v_ref, *rest):
    o_ref, turned_ref, log_ref, acc_ref = rest[-4:]
    step = pl.program_id(0)
    query = wide(q_ref[...] * jnp.asarray(SCALE, BF16))
    start, place = mask_rows(start_ref, step, shift)
    acc_ref[...] = jnp.zeros_like(acc_ref)

    def body(j, carried):
        top, total = carried
        rows = pl.ds(pl.multiple_of(j * TILE, TILE), TILE)
        scores = nt(k_ref[rows, :], query)
        scores = jnp.where(allowed(j, start, place), scores, -1e30)
        new_top = jnp.maximum(top, jnp.max(scores, axis=0, keepdims=True))
        part = jnp.exp(scores - new_top)
        factor = jnp.exp(top - new_top)
        total = total * factor + jnp.sum(part, axis=0, keepdims=True)
        acc_ref[...] = acc_ref[...] * factor + tn(v_ref[rows, :], part.astype(BF16))
        return new_top, total

    top, total = lax.fori_loop(
        meta_ref[base + step] - shift // TILE,
        step + 5,
        body,
        (jnp.full((1, 2 * TILE), -1e30, F32), jnp.zeros((1, 2 * TILE), F32)),
    )
    turned = heads_of(acc_ref[...] / total)
    turned_ref[...] = turned
    o_ref[...] = turned.T.astype(BF16)
    logs = top + jnp.log(total)
    log_ref[0:1, :] = logs[:, :TILE]
    log_ref[1:2, :] = logs[:, TILE:]


def attend(base, shift, meta, start, q, qcol, k, kcol, v, vcol, earlier, tokens, count):
    n = k.shape[0]
    steps = (n - DOC_MAX) // TILE
    tiles = tokens // TILE
    per = tiles // count
    alias = earlier is not None
    specs = [
        pl.BlockSpec((1, TILE), lambda i, m: (0, base + i)),
        pl.BlockSpec((TILE, PAIR), lambda i, m: (base + i, qcol)),
        pl.BlockSpec((n, PAIR), lambda i, m: (0, kcol)),
        pl.BlockSpec((n, PAIR), lambda i, m: (0, vcol)),
    ] + [ANY] * (3 if alias else 0)
    return pl.pallas_call(
        functools.partial(attend_kernel, base, shift),
        grid_spec=pltpu.PrefetchScalarGridSpec(
            num_scalar_prefetch=1,
            grid=(steps,),
            in_specs=specs,
            out_specs=[
                pl.BlockSpec((TILE, PAIR), lambda i, m: (turn(base + i, m, tiles, per, count), 0)),
                pl.BlockSpec((PAIR, TILE), lambda i, m: (0, base + i)),
                pl.BlockSpec((8, TILE), lambda i, m: (0, base + i)),
            ],
            scratch_shapes=[pltpu.VMEM((PAIR, 2 * TILE), F32)],
        ),
        out_shape=[
            jax.ShapeDtypeStruct((tokens, PAIR), BF16),
            jax.ShapeDtypeStruct((PAIR, tokens), F32),
            jax.ShapeDtypeStruct((8, tokens), F32),
        ],
        input_output_aliases={5: 0, 6: 1, 7: 2} if alias else {},
        cost_estimate=light(4 * n * PAIR, 8 * n * n * PAIR),
        name="attend",
    )(meta, start, q, k, v, *(earlier if alias else ()))


def back_tile(shift, low, start_ref, q_ref, k_ref, v_ref, do_ref, turned_ref, log_ref, dk_ref, dv_ref, acc_ref):
    step = pl.program_id(0)
    query = wide(q_ref[...] * jnp.asarray(SCALE, BF16))
    out_back = wide(do_ref[...])
    start, place = mask_rows(start_ref, step, shift)
    product = do_ref[...].astype(F32).T * turned_ref[...]
    delta = jnp.concatenate(
        (
            jnp.sum(product[:HEAD], axis=0, keepdims=True),
            jnp.sum(product[HEAD:], axis=0, keepdims=True),
        ),
        axis=1,
    )
    logs = jnp.concatenate((log_ref[0:1, :], log_ref[1:2, :]), axis=1)
    acc_ref[...] = jnp.zeros_like(acc_ref)

    def body(j, carried):
        rows = pl.ds(pl.multiple_of(j * TILE, TILE), TILE)
        key_tile = k_ref[rows, :]
        scores = jnp.where(allowed(j, start, place), nt(key_tile, query), -1e30)
        prob = jnp.exp(scores - logs)
        prob_back = nt(v_ref[rows, :], out_back)
        score_back = (prob * (prob_back - delta)).astype(BF16)
        dv_ref[rows, :] += nn(prob.astype(BF16), out_back)
        dk_ref[rows, :] += nn(score_back, query)
        acc_ref[...] += tn(key_tile, score_back)
        return carried

    lax.fori_loop(low, step + 5, body, 0)
    return (heads_of(acc_ref[...]) * SCALE).T.astype(BF16)


def early_kernel(meta_ref, start_ref, q_ref, k_ref, v_ref, do_ref, turned_ref, log_ref, dq_ref, gone_ref, dk_ref, dv_ref, kept_k, kept_v, acc_ref):
    step = pl.program_id(0)

    @pl.when(step == 0)
    def _():
        kept_k[...] = jnp.zeros_like(kept_k)
        kept_v[...] = jnp.zeros_like(kept_v)

    dq_ref[...] = back_tile(
        0, meta_ref[step], start_ref, q_ref, k_ref, v_ref, do_ref, turned_ref, log_ref,
        kept_k, kept_v, acc_ref,
    )

    @pl.when(step == pl.num_programs(0) - 1)
    def _():
        gone_ref[:, :PAIR] = kept_k[:DOC_MAX, :].astype(BF16)
        gone_ref[:, PAIR:] = kept_v[:DOC_MAX, :].astype(BF16)
        dk_ref[...] = kept_k[DOC_MAX:, :]
        dv_ref[...] = kept_v[DOC_MAX:, :]


def late_kernel(base, fresh, per, count, meta_ref, start_ref, q_ref, k_ref, v_ref, do_ref, turned_ref, log_ref, dq_in, dk_in, dv_in, back_ref, packed_ref, value_ref, sums_ref, kept_k, kept_v, acc_ref):
    step = pl.program_id(0)
    held = dk_in.shape[0]
    tiles = packed_ref.shape[0] // TILE

    def rows_of(tile):
        row = turn(tile, meta_ref, tiles, per, count) * TILE
        return pl.ds(pl.multiple_of(row, TILE), TILE)

    @pl.when(step == 0)
    def _():
        kept_k[:held, :] = dk_in[...]
        kept_v[:held, :] = dv_in[...]
        kept_k[held:, :] = back_ref[:, :PAIR].astype(F32)
        kept_v[held:, :] = back_ref[:, PAIR:].astype(F32)
        for i in range(base):
            packed_ref[rows_of(i), :PAIR] = dq_in[i * TILE : (i + 1) * TILE, :]

    packed_ref[rows_of(base + step), :PAIR] = back_tile(
        DOC_MAX, meta_ref[base + step] - DOC_MAX // TILE, start_ref, q_ref, k_ref, v_ref, do_ref,
        turned_ref, log_ref, kept_k, kept_v, acc_ref,
    )

    @pl.when(step == pl.num_programs(0) - 1)
    def _():
        for i in range(tiles):
            span = slice(i * TILE, (i + 1) * TILE)
            packed_ref[rows_of(i), PAIR : 2 * PAIR] = kept_k[span, :].astype(BF16)
            if fresh:
                packed_ref[rows_of(i), 2 * PAIR :] = kept_v[span, :].astype(BF16)
        if not fresh:
            value_ref[...] = kept_v[...]
        else:
            value_ref[...] = jnp.zeros_like(value_ref)
        sums_ref[...] = jnp.broadcast_to(
            jnp.sum(packed_ref[...].astype(F32), axis=0, keepdims=True), sums_ref.shape
        )


def back_specs(base, qcol, n, kcol, vcol, tiles, per, count):
    return [
        pl.BlockSpec((1, TILE), lambda i, m: (0, base + i)),
        pl.BlockSpec((TILE, PAIR), lambda i, m: (base + i, qcol)),
        pl.BlockSpec((n, PAIR), lambda i, m: (0, kcol)),
        pl.BlockSpec((n, PAIR), lambda i, m: (0, vcol)),
        pl.BlockSpec((TILE, PAIR), lambda i, m: (turn(base + i, m, tiles, per, count), 0)),
        pl.BlockSpec((PAIR, TILE), lambda i, m: (0, base + i)),
        pl.BlockSpec((8, TILE), lambda i, m: (0, base + i)),
    ]


def whole(shape):
    return pl.BlockSpec(shape, lambda i, m: (0,) * len(shape))


def back_early(meta, start, q, qcol, k, kcol, v, vcol, do, turned, logs, tokens, count):
    n = k.shape[0]
    held = n - DOC_MAX
    tiles = tokens // TILE
    return pl.pallas_call(
        early_kernel,
        grid_spec=pltpu.PrefetchScalarGridSpec(
            num_scalar_prefetch=1,
            grid=(held // TILE,),
            in_specs=back_specs(0, qcol, n, kcol, vcol, tiles, tiles // count, count),
            out_specs=[
                pl.BlockSpec((TILE, PAIR), lambda i, m: (i, 0)),
                whole((DOC_MAX, 2 * PAIR)),
                whole((held, PAIR)),
                whole((held, PAIR)),
            ],
            scratch_shapes=[
                pltpu.VMEM((n, PAIR), F32),
                pltpu.VMEM((n, PAIR), F32),
                pltpu.VMEM((PAIR, 2 * TILE), F32),
            ],
        ),
        out_shape=[
            jax.ShapeDtypeStruct((held, PAIR), BF16),
            jax.ShapeDtypeStruct((DOC_MAX, 2 * PAIR), BF16),
            jax.ShapeDtypeStruct((held, PAIR), F32),
            jax.ShapeDtypeStruct((held, PAIR), F32),
        ],
        cost_estimate=light(12 * n * PAIR, 12 * n * n * PAIR),
        name="back_early",
    )(meta, start, q, k, v, do, turned, logs)


def back_late(meta, start, q, qcol, k, kcol, v, vcol, do, turned, logs, dq, dk, dv, back, fresh, tokens, count):
    n = k.shape[0]
    held = n - DOC_MAX
    tiles = tokens // TILE
    per = tiles // count
    base = (tokens - held) // TILE
    cols = (3 if fresh else 2) * PAIR
    return pl.pallas_call(
        functools.partial(late_kernel, base, fresh, per, count),
        grid_spec=pltpu.PrefetchScalarGridSpec(
            num_scalar_prefetch=1,
            grid=(held // TILE,),
            in_specs=back_specs(base, qcol, n, kcol, vcol, tiles, per, count)
            + [whole(dq.shape), whole(dk.shape), whole(dv.shape), whole(back.shape)],
            out_specs=[
                whole((tokens, cols)),
                whole((8, PAIR) if fresh else (tokens, PAIR)),
                whole((8, cols)),
            ],
            scratch_shapes=[
                pltpu.VMEM((n, PAIR), F32),
                pltpu.VMEM((n, PAIR), F32),
                pltpu.VMEM((PAIR, 2 * TILE), F32),
            ],
        ),
        out_shape=[
            jax.ShapeDtypeStruct((tokens, cols), BF16),
            jax.ShapeDtypeStruct((8, PAIR) if fresh else (tokens, PAIR), F32),
            jax.ShapeDtypeStruct((8, cols), F32),
        ],
        cost_estimate=light(12 * n * PAIR, 12 * n * n * PAIR),
        name="back_late",
    )(meta, start, q, k, v, do, turned, logs, dq, dk, dv, back)


def store_grad(grad_ref, grad):
    runs, _, lanes, rows, cols = grad_ref.shape
    for j in range(lanes):
        grad_ref[:, 0, j] = grad[:, j * cols : (j + 1) * cols].reshape(runs, rows, cols)


def accumulate(ref, value):
    @pl.when(pl.program_id(0) == 0)
    def _():
        ref[...] = value

    @pl.when(pl.program_id(0) > 0)
    def _():
        ref[...] += value


def up_kernel(places_ref, sn_ref, got_ref, cot_ref, up_ref, bias_ref, down_ref, out_ref, other_ref, slope_ref, grad_ref, act_ref):
    width = up_ref.shape[0] * up_ref.shape[1]
    rows = sn_ref.shape[0]
    up = up_ref[...].reshape(width, UNIT)
    down = down_ref[...].reshape(UNIT, width)
    for i, (piece_ref, sum_ref) in enumerate(((sn_ref, out_ref), (got_ref, other_ref))):
        span = slice(i * rows, (i + 1) * rows)
        hidden = nn(piece_ref[...], up) + bias_ref[0]
        square = hidden * hidden
        curve = jnp.tanh(GELU_A * (hidden + GELU_B * (hidden * square)))
        half = 0.5 * (1.0 + curve)
        activated = (hidden * half).astype(BF16)
        slope_ref[span, :] = half + 0.5 * hidden * (1.0 - curve * curve) * (
            GELU_A * (1.0 + 3.0 * GELU_B * square)
        )
        act_ref[span, :] = activated
        accumulate(sum_ref, nn(activated, down))
    store_grad(grad_ref, nn(cot_ref[...], act_ref[...]).astype(BF16))


def feed_specs(gathered, seq, parts, width):
    part = width // seq
    per = width // UNIT
    run = seq // 2

    def spot(i, p):
        return lax.rem(p[0] + i, parts)

    grad_spec = pl.BlockSpec(
        (run, 1, UNIT // PAIR, width // run, PAIR), lambda i, p: (0, i, 0, 0, 0)
    )

    grad = jax.ShapeDtypeStruct((run, parts, UNIT // PAIR, width // run, PAIR), BF16)
    return (
        pl.BlockSpec((seq, part, UNIT), lambda i, p: (spot(i, p), 0, p[1])),
        pl.BlockSpec((UNIT // part, part, width), lambda i, p: (spot(i, p) * per + p[1], 1, 0)),
        grad_spec,
        grad,
    )


def fixed(shape):
    return pl.BlockSpec(shape, lambda i, p: (0,) * len(shape))


def feed_up(places, sn, got, cot_turned, gathered, bias, seq, parts):
    rows, width = sn.shape
    up_spec, down_spec, grad_spec, grad = feed_specs(gathered, seq, parts, width)
    return pl.pallas_call(
        up_kernel,
        grid_spec=pltpu.PrefetchScalarGridSpec(
            num_scalar_prefetch=1,
            grid=(parts,),
            in_specs=[
                fixed((rows, width)),
                fixed((rows, width)),
                fixed((width, 2 * rows)),
                up_spec,
                pl.BlockSpec((1, 1, UNIT), lambda i, p: (lax.rem(parts - i, parts), 0, p[1])),
                down_spec,
            ],
            out_specs=[
                fixed((rows, width)),
                fixed((rows, width)),
                pl.BlockSpec((2 * rows, UNIT), lambda i, p: (0, i)),
                grad_spec,
            ],
            scratch_shapes=[pltpu.VMEM((2 * rows, UNIT), BF16)],
        ),
        out_shape=[
            jax.ShapeDtypeStruct((rows, width), F32),
            jax.ShapeDtypeStruct((rows, width), F32),
            jax.ShapeDtypeStruct((2 * rows, parts * UNIT), F32),
            grad,
        ],
        cost_estimate=light(16 * rows * width, 24 * rows * width * width),
        name="feed_up",
    )(places, sn, got, cot_turned, gathered, bias, gathered)


def down_kernel(places_ref, cot_ref, cot_got_ref, sn_ref, got_ref, slope_ref, up_ref, down_ref, back_ref, other_ref, grad_ref, bias_ref, turned_ref, hidden_ref):
    width = up_ref.shape[0] * up_ref.shape[1]
    rows = sn_ref.shape[0]

    @pl.when(pl.program_id(0) == 0)
    def _():
        turned_ref[:, :rows] = sn_ref[...].T
        turned_ref[:, rows:] = got_ref[...].T

    up = up_ref[...].reshape(width, UNIT)
    down = down_ref[...].reshape(UNIT, width)
    total = jnp.zeros((1, UNIT), F32)
    for i, (piece_ref, sum_ref) in enumerate(((cot_ref, back_ref), (cot_got_ref, other_ref))):
        span = slice(i * rows, (i + 1) * rows)
        rounded = (nt(piece_ref[...], down) * slope_ref[span, :]).astype(BF16)
        total = total + jnp.sum(rounded.astype(F32), axis=0, keepdims=True)
        hidden_ref[span, :] = rounded
        accumulate(sum_ref, nt(rounded, up))
    bias_ref[0] = total
    store_grad(grad_ref, nn(turned_ref[...], hidden_ref[...]).astype(BF16))


def feed_down(places, cot, cot_got, sn, got, slope, gathered, seq, parts):
    rows, width = cot.shape
    up_spec, down_spec, grad_spec, grad = feed_specs(gathered, seq, parts, width)
    return pl.pallas_call(
        down_kernel,
        grid_spec=pltpu.PrefetchScalarGridSpec(
            num_scalar_prefetch=1,
            grid=(parts,),
            in_specs=[fixed((rows, width))] * 4
            + [
                pl.BlockSpec((2 * rows, UNIT), lambda i, p: (0, i)),
                up_spec,
                down_spec,
            ],
            out_specs=[
                fixed((rows, width)),
                fixed((rows, width)),
                grad_spec,
                pl.BlockSpec((1, 1, UNIT), lambda i, p: (i, 0, 0)),
            ],
            scratch_shapes=[
                pltpu.VMEM((width, 2 * rows), BF16),
                pltpu.VMEM((2 * rows, UNIT), BF16),
            ],
        ),
        out_shape=[
            jax.ShapeDtypeStruct((rows, width), F32),
            jax.ShapeDtypeStruct((rows, width), F32),
            grad,
            jax.ShapeDtypeStruct((parts, 1, UNIT), F32),
        ],
        cost_estimate=light(16 * rows * width, 24 * rows * width * width),
        name="feed_down",
    )(places, cot, cot_got, sn, got, slope, gathered, gathered)


def back_norm_kernel(own_ref, came_ref, cot_ref, hat_ref, inverse_ref, gain_ref, mixing_ref, middle_ref, rounded_ref, attended_ref, sums_ref):
    back = own_ref[...] + came_ref[...]
    hat = hat_ref[...]
    cot = cot_ref[...].astype(F32)
    middle_back = cot + norm_back(back, gain_ref[...], hat, inverse_ref[...])
    rounded = middle_back.astype(BF16)
    middle_ref[...] = middle_back
    rounded_ref[...] = rounded
    attended = nt(rounded, mixing_ref[...]).astype(BF16)
    for j in range(attended_ref.shape[0]):
        attended_ref[j] = attended[:, j * PAIR : (j + 1) * PAIR]

    @pl.when(pl.program_id(0) == 0)
    def _():
        sums_ref[...] = jnp.zeros_like(sums_ref)

    for i, value in enumerate((back * hat, back, middle_back, cot)):
        sums_ref[i : i + 1, :] += jnp.sum(value, axis=0, keepdims=True)


def back_norm(own, came, cot, hat, inverse, gain, mixing):
    rows, width = own.shape
    blocks = mixing.shape[0] // PAIR
    tile = rows // 4
    row = pl.BlockSpec((tile, width), lambda i: (i, 0))
    return pl.pallas_call(
        back_norm_kernel,
        grid=(4,),
        in_specs=[
            row, row, row, row,
            pl.BlockSpec((tile, 1), lambda i: (i, 0)),
            pl.BlockSpec((1, width), lambda i: (0, 0)),
            pl.BlockSpec(mixing.shape, lambda i: (0, 0)),
        ],
        out_specs=[
            row, row,
            pl.BlockSpec((blocks, tile, PAIR), lambda i: (0, i, 0)),
            pl.BlockSpec((8, width), lambda i: (0, 0)),
        ],
        out_shape=[
            jax.ShapeDtypeStruct((rows, width), F32),
            jax.ShapeDtypeStruct((rows, width), BF16),
            jax.ShapeDtypeStruct((blocks, rows, PAIR), BF16),
            jax.ShapeDtypeStruct((8, width), F32),
        ],
        cost_estimate=light(16 * rows * width, 2 * rows * width * width),
        name="back_norm",
    )(own, came, cot, hat, inverse, gain[None], mixing)


def front_norm_kernel(parts, places_ref, *refs):
    pieces, (weight_ref, middle_ref, hat_ref, inverse_ref, gain_ref, out_ref) = refs[:-6], refs[-6:]
    cut = pieces[0].shape[1]
    back = jnp.zeros(out_ref.shape, F32)
    for k in range(parts):
        spot = lax.rem(places_ref[0] - k + parts, parts)
        back = back + nn(pieces[2 * k][...], weight_ref[spot, :cut, :])
        back = back + nn(pieces[2 * k + 1][...], weight_ref[spot, cut:, :])
    out_ref[...] = middle_ref[...] + norm_back(
        back, gain_ref[...], hat_ref[...], inverse_ref[...]
    )


def front_norm(places, pieces, weight, middle, hat, inverse, gain):
    rows, width = middle.shape
    parts = weight.shape[0]
    tile = rows // 4

    def row(cols):
        return pl.BlockSpec((tile, cols), lambda i, p: (i, 0))

    return pl.pallas_call(
        functools.partial(front_norm_kernel, parts),
        grid_spec=pltpu.PrefetchScalarGridSpec(
            num_scalar_prefetch=1,
            grid=(4,),
            in_specs=[row(piece.shape[1]) for piece in pieces]
            + [fixed(weight.shape), row(width), row(width), row(1), fixed((1, width))],
            out_specs=row(width),
        ),
        out_shape=jax.ShapeDtypeStruct((rows, width), F32),
        cost_estimate=light(16 * rows * width, 2 * rows * width * weight.shape[0] * weight.shape[1]),
        name="front_norm",
    )(places, *pieces, weight, middle, hat, inverse, gain[None])


def around(value, steps):
    count = lax.axis_size("tp")
    return lax.ppermute(value, "tp", [(i, (i + steps) % count) for i in range(count)])


def flipped(value, axis, bit):
    count = lax.axis_size(axis)
    return lax.ppermute(value, axis, [(i, i ^ bit) for i in range(count)])


def along(value, steps):
    count = lax.axis_size(SEQ)
    first, last = max(0, -steps), min(count, count - steps)
    return lax.ppermute(value, SEQ, [(i, i + steps) for i in range(first, last)])


def summed(value):
    for axis in (SEQ, "tp"):
        bit = 1
        while bit < lax.axis_size(axis):
            value = value + flipped(value, axis, bit)
            bit *= 2
    return value


def pick(value, index, dim):
    return lax.dynamic_index_in_dim(value, index, dim, keepdims=False)


def joined(a, b):
    return (a.astype(F32) + b.astype(F32)).astype(BF16)


def seq_bits():
    bits, bit = [], 1
    while bit < lax.axis_size(SEQ):
        bits.append(bit)
        bit *= 2
    return bits


def tied(*groups):
    return lax.optimization_barrier(groups)


class Scatter:
    def __init__(self, value, place):
        self.place = place
        self.bits = seq_bits()
        self.left = value.reshape((2,) * len(self.bits) + value.shape[1:])
        self.issue()

    def issue(self):
        bit = self.bits.pop(0)
        dim = len(self.bits)
        mine = (self.place // bit) % 2
        self.parts = (
            pick(self.left, mine, dim), flipped(pick(self.left, 1 - mine, dim), SEQ, bit)
        )

    def merge(self):
        self.left = joined(*self.parts)
        if self.bits:
            self.issue()
            return True
        return False

    def result(self):
        while self.merge():
            pass
        return self.left


def in_order(own, other, bit, place, dim):
    low = (place // bit) % 2 == 0
    return jnp.stack((jnp.where(low, own, other), jnp.where(low, other, own)), axis=dim)


def quarter(shard, place):
    size = shard.shape[0] // 4
    spot = 2 * ((place // 2) % 2) + place % 2
    return lax.dynamic_slice_in_dim(shard, spot * size, size, 0)


def from_shards(piece):
    return [around(piece, k) for k in range(1, lax.axis_size("tp"))]


def center(rows):
    average = jnp.mean(rows, axis=-1, keepdims=True)
    centered = rows - average
    inverse = lax.rsqrt(jnp.mean(centered * centered, axis=-1, keepdims=True) + EPSILON)
    return centered * inverse, inverse


def norm_back(grad, gain, xhat, inverse):
    e = grad * gain
    return inverse * (
        e
        - jnp.mean(e, axis=-1, keepdims=True)
        - xhat * jnp.mean(e * xhat, axis=-1, keepdims=True)
    )


def local(
    stream, segments, skip_values, first_gain, first_shift, query_weight, query_bias, key_weight,
    value_weight, value_bias, mixing_weight, mixing_bias, second_gain, second_shift, up_weight,
    up_bias, down_weight, down_bias, cotangent,
):
    rows, width = stream.shape
    tokens = skip_values.shape[0]
    own = query_weight.shape[1]
    tp = lax.axis_size("tp")
    seq = lax.axis_size(SEQ)
    seq_place = lax.axis_index(SEQ)
    tp_place = lax.axis_index("tp")
    core = lax.axis_index("core")
    places = jnp.stack((tp_place, core)).astype(jnp.int32)
    half = tokens - DOC_MAX
    part = width // seq
    kcol = own // PAIR

    stream_wide = stream.astype(F32)
    first_hat, first_inverse = center(stream_wide)
    piece = (first_hat * first_gain + first_shift).astype(BF16)
    piece, up_weight, down_weight, mixing_weight, segments, cotangent = lax.optimization_barrier(
        (piece, up_weight, down_weight, mixing_weight, segments, cotangent)
    )

    def own_rows(shard):
        size = shard.shape[0] // seq
        return lax.dynamic_slice_in_dim(shard, seq_place * size, size, 0)

    qkv_turned = jnp.concatenate(
        (
            query_weight[:, :PAIR], key_weight[:, :PAIR], value_weight,
            query_weight[:, PAIR:], key_weight[:, PAIR:],
        ),
        axis=1,
    ).T
    packet = jnp.concatenate([own_rows(w) for w in (up_weight, down_weight)], axis=0)
    qkv_packet = own_rows(qkv_turned)
    bias_pieces = jnp.stack([up_bias] + [around(up_bias, k) for k in range(1, tp)])[:, None]
    cot_got = flipped(cotangent, "core", 1)

    padded = jnp.concatenate((jnp.full((DOC_MAX,), -1, jnp.int32), segments))
    window = lax.dynamic_slice_in_dim(padded, seq_place * tokens, DOC_MAX + tokens, 0)
    start = jnp.sum(
        (window[:, None] < window[None, DOC_MAX:]).astype(jnp.int32), axis=0, keepdims=True
    )
    meta = jnp.concatenate((start[0, ::TILE] // TILE, places))
    halo_skip = along(skip_values[half:], 1)
    wqkv = jnp.concatenate((query_weight, key_weight, value_weight), axis=1)
    bias = jnp.concatenate((query_bias, jnp.zeros((own,), F32), value_bias))[None]
    made = None
    for k in range(tp):
        if k == tp - 1:
            piece, meta, start, bias_pieces, cot_got, mixing_piece = tied(
                piece, meta, start, bias_pieces, cot_got, quarter(mixing_weight, seq_place)
            )
        elif k > 0:
            piece, made = tied(piece, made)
        ahead = around(piece, 1) if k < tp - 1 else None
        made = project(k, tp, places, piece, wqkv, bias, made)
        piece = ahead
        if k == GATHER_STEP:
            piece, packet = tied(piece, packet)
            gathered = lax.all_gather(packet, ("tp",) + SEQ, axis=0, tiled=False)
    qkv, normed_turned = made
    halo = along(qkv[half:, own:], 1)
    qkv, mixing_piece = tied(qkv, mixing_piece)
    mixing_got = from_shards(mixing_piece)
    early = early_skip = None

    def values_of(pair):
        if pair == 0:
            return (qkv, 2 * kcol), (early, kcol)
        return (skip_values, 0), (early_skip, 0)

    steps = half // TILE
    attended = []
    for pair in range(2):
        (v, vcol), _ = values_of(pair)
        attended.append(
            attend(steps, DOC_MAX, meta, start, qkv, pair, qkv, kcol + pair, v, vcol, None, tokens, tp)
        )
    attended, halo, halo_skip, mixing_got = tied(attended, halo, halo_skip, mixing_got)
    early_skip = jnp.concatenate((halo_skip, skip_values[:half]), axis=0)
    early = jnp.concatenate((halo, qkv[:half, own:]), axis=0)
    mixing_got = jnp.stack(mixing_got)
    mixing_other = flipped(mixing_got, SEQ, 2)
    arrived = []
    for pair in range(2):
        _, (v, vcol) = values_of(pair)
        attended[pair] = attend(
            0, 0, meta, start, qkv, pair, early, pair, v, vcol, attended[pair], tokens, tp
        )
        blocks = attended[pair][0].reshape(tp, rows, PAIR)
        arrived.append([blocks[0]] + [around(blocks[k], k) for k in range(1, tp)])
    attended[1], mixing_got, mixing_other, cotangent, cot_got = tied(
        attended[1], mixing_got, mixing_other, cotangent, cot_got
    )
    mixing_got = in_order(mixing_got, mixing_other, 2, seq_place, 1)
    mixing_other = flipped(mixing_got, "core", 1)
    cot_turned = turn_rows(cotangent, cot_got)
    mixing_rot = in_order(mixing_got, mixing_other, 1, seq_place, 2).reshape(-1, width)
    mixing_rot = jnp.concatenate((mixing_weight, mixing_rot), axis=0)
    arrived, mixing_rot, cot_turned = tied(arrived, mixing_rot, cot_turned)

    mixed_in = jnp.concatenate([arrived[pair][k] for k in range(tp) for pair in range(2)], axis=1)
    middle = stream_wide + nn(mixed_in, mixing_rot) + mixing_bias
    second_hat, second_inverse = center(middle)
    second = (second_hat * second_gain + second_shift).astype(BF16)

    got = flipped(second, "core", 1)
    got, qkv_packet = tied(got, qkv_packet)
    qkv_full = lax.all_gather(qkv_packet, ("tp",) + SEQ, axis=0, tiled=False)
    qkv_full = qkv_full.reshape(tp, -1, width)
    lost, lost_other, slope, down_grads = feed_up(
        places, second, got, cot_turned, gathered, bias_pieces, seq, tp
    )

    def over_runs(grads):
        return lax.psum_scatter(grads, "run", scatter_dimension=0, tiled=True)[0]

    def over_shards(grads):
        return [grads[0]] + [around(grads[k], k) for k in range(1, tp)]

    down_grads = over_runs(down_grads)
    back_own, back_other, up_grads, up_bias_grad = feed_down(
        places, cotangent, cot_got, second, got, slope, gathered, seq, tp
    )
    up_grads = over_runs(up_grads)
    back_came = flipped(back_other, "core", 1)
    middle_back, mixing_back, attended_back, norm_sums = back_norm(
        back_own, back_came, cotangent, second_hat, second_inverse, second_gain, mixing_rot
    )
    mixing_back, attended_back, lost_other = tied(mixing_back, attended_back, lost_other)

    def send_back(pair):
        return [attended_back[pair]] + [
            around(attended_back[2 * k + pair], -k) for k in range(1, tp)
        ]

    moved = send_back(0)
    mixing_grad = tn(mixing_back, mixed_in).astype(BF16).reshape(seq, part, tp * own)
    moved, attended_back, mixing_grad, lost_other = tied(
        moved, attended_back, mixing_grad, lost_other
    )
    returned = [jnp.concatenate(moved, axis=0)]
    moved = send_back(1)
    mixing_sum = Scatter(mixing_grad, seq_place)
    lost_came = flipped(lost_other, "core", 1)

    halves = []
    for pair in range(2):
        _, (v, vcol) = values_of(pair)
        _, turned, logs = attended[pair]
        dq, gone, dk, dv = back_early(
            meta, start, qkv, pair, early, pair, v, vcol, returned[pair], turned, logs, tokens, tp
        )
        halves.append((dq, dk, dv, along(gone, -1)))
        if pair == 0:
            dq, moved, mixing_sum.parts, lost_came, down_grads = tied(
                dq, moved, mixing_sum.parts, lost_came, down_grads
            )
            returned.append(jnp.concatenate(moved, axis=0))
            mixing_sum.merge()
            down_grads = over_shards(down_grads)
    halves, norm_sums, up_bias_grad = tied(halves, norm_sums, up_bias_grad)
    halves = [list(group) for group in halves]
    def total(parts):
        sums = summed(jnp.concatenate(parts).reshape(-1, PAIR)).reshape(-1)
        cuts, offset = [], 0
        for value in parts:
            cuts.append(sums[offset : offset + value.shape[0]])
            offset += value.shape[0]
        return cuts

    up_bias_grad = up_bias_grad.reshape(tp, UNIT)
    zero = jnp.zeros((UNIT,), F32)
    up_parts = []
    for k in range(tp):
        made_here = pick(up_bias_grad, (k - tp_place) % tp, 0)
        up_parts += [jnp.where(core == 0, made_here, zero), jnp.where(core == 0, zero, made_here)]
    up_bias_grad = jnp.concatenate(up_parts)
    second_gain_grad, second_shift_grad, mixing_bias_grad, down_bias_grad, up_bias_grad = total(
        [
            norm_sums[0], norm_sums[1], norm_sums[2], norm_sums[3],
            up_bias_grad,
        ]
    )
    packets, column_sums, pieces = [], [], []
    skip_gradient = None
    for pair in range(2):
        (v, vcol), _ = values_of(pair)
        _, turned, logs = attended[pair]
        packed, values, sums = back_late(
            meta, start, qkv, pair, qkv, kcol + pair, v, vcol, returned[pair], turned, logs,
            *halves[pair], pair == 0, tokens, tp,
        )
        blocks = packed.reshape(tp, rows, packed.shape[1])
        pieces.append([blocks[0]] + [around(blocks[k], k) for k in range(1, tp)])
        if pair == 0:
            halves[1], packed, mixing_sum.parts = tied(halves[1], packed, mixing_sum.parts)
            mixing_sum.merge()
        else:
            skip_gradient = values
        packets.append(packed)
        column_sums.append(sums[0])
    packets, mixing_sum.parts, middle, up_grads, down_grads = tied(
        packets, mixing_sum.parts, middle, up_grads, down_grads
    )
    up_grads = over_shards(up_grads)
    output = (middle + (lost + lost_came) + down_bias).astype(BF16)
    wide_grad = nn(normed_turned, jnp.concatenate(packets, axis=1))
    weight_sum = Scatter(wide_grad.astype(BF16).reshape(seq, part, -1), seq_place)
    mixing_blocks = mixing_sum.result().reshape(part, tp, own)
    mixing_blocks = [mixing_blocks[:, 0]] + [
        around(mixing_blocks[:, k], -k) for k in range(1, tp)
    ]
    stream_gradient = front_norm(
        places, [pieces[pair][k] for k in range(tp) for pair in range(2)], qkv_full, middle_back,
        first_hat, first_inverse, first_gain,
    )
    weight_grad = weight_sum.result().astype(F32)
    mixing_gradient = sum(block.astype(F32) for block in mixing_blocks).T

    def halves_of(blocks):
        cut = sum(block.astype(F32) for block in blocks)
        cut = cut.reshape(cut.shape[0], 2, part, PAIR)
        kept = pick(cut, core, 1)
        came = flipped(pick(cut, 1 - core, 1), "core", 1)
        return jnp.concatenate(
            (jnp.where(core == 0, kept, came), jnp.where(core == 0, came, kept)), axis=0
        )

    down_gradient = halves_of(down_grads).transpose(0, 2, 1).reshape(-1, part)
    up_gradient = halves_of(up_grads).transpose(1, 0, 2).reshape(part, -1)

    query_gradient = jnp.concatenate(
        (weight_grad[:, :PAIR], weight_grad[:, 3 * PAIR : 4 * PAIR]), axis=1
    )
    key_gradient = jnp.concatenate(
        (weight_grad[:, PAIR : 2 * PAIR], weight_grad[:, 4 * PAIR :]), axis=1
    )
    value_gradient = weight_grad[:, 2 * PAIR : 3 * PAIR]

    column_sum = jnp.concatenate(column_sums)
    columns = qkv_turned.T.astype(F32)
    first_shift_part = jnp.sum(columns * column_sum, axis=1)
    hat_grad = (wide_grad - first_shift[:, None] * column_sum) / first_gain[:, None]
    first_gain_part = jnp.sum(columns * hat_grad, axis=1)

    def widen(value):
        size = value.shape[0]
        return lax.dynamic_update_slice_in_dim(
            jnp.zeros((size * tp,), F32), value, tp_place * size, 0
        )

    query_part = jnp.concatenate((column_sum[:PAIR], column_sum[3 * PAIR : 4 * PAIR]))
    first_gain_grad, first_shift_grad, query_bias_grad, value_bias_grad = total(
        [
            first_gain_part,
            first_shift_part,
            widen(query_part),
            widen(column_sum[2 * PAIR : 3 * PAIR]),
        ]
    )
    return (
        output,
        stream_gradient,
        skip_gradient,
        query_gradient,
        query_bias_grad,
        key_gradient,
        value_gradient,
        value_bias_grad,
        mixing_gradient,
        mixing_bias_grad,
        first_gain_grad,
        first_shift_grad,
        second_gain_grad,
        second_shift_grad,
        up_gradient,
        up_bias_grad,
        down_gradient,
        down_bias_grad,
    )


def solution(mesh):
    seq, tp = mesh.shape["seq"], mesh.shape["tp"]
    mesh = jax.sharding.Mesh(mesh.devices.reshape(seq // 2, 2, tp), SEQ + ("tp",))
    split = P(SEQ + ("tp",), None)
    column = P(None, "tp")
    tile = P(SEQ, "tp")
    turned = P("tp", SEQ)
    in_specs = (
        split, P(), tile, P(), P(), column, P("tp"), column, column, P("tp"),
        P("tp", None), P(), P(), P(), column, P("tp"), P("tp", None), P(), split,
    )
    out_specs = (
        split, split, tile, tile, P(), tile, tile, P(), turned, P(), P(), P(), P(), P(),
        tile, P(), turned, P(),
    )
    return jax.shard_map(local, mesh=mesh, in_specs=in_specs, out_specs=out_specs, check_vma=False)
```

```python
import functools

import jax
import jax.numpy as jnp
from jax import lax
from jax.experimental import pallas as pl
from jax.experimental.pallas import tpu as pltpu
from jax.sharding import PartitionSpec as P

HEAD = 64
DOC_MAX = 1024
PAIR = 2 * HEAD
TILE = 256
UNIT = 512
EPSILON = 1e-05
F32 = jnp.float32
BF16 = jnp.bfloat16
SCALE = HEAD ** -0.5
GELU_A = 0.7978845608028654
GELU_B = 0.044715
SEQ = ("run", "core")
GATHER_STEP = 1


def dot(a, b, dims, out=F32):
    return lax.dot_general(a, b, (dims, ((), ())), preferred_element_type=out)


def nn(a, b):
    return dot(a, b, ((1,), (0,)))


def nt(a, b):
    return dot(a, b, ((1,), (1,)))


def tn(a, b):
    return dot(a, b, ((0,), (0,)))


def light(bytes_accessed, flops=1):
    return pl.CostEstimate(flops=flops, bytes_accessed=bytes_accessed, transcendentals=0)


ANY = pl.BlockSpec(memory_space=pl.ANY)


def project_kernel(slot, place_ref, piece_ref, weight_ref, bias_ref, *rest):
    qkv_ref, turned_ref = rest[-2:]
    piece = piece_ref[...]
    qkv_ref[...] = (nn(piece, weight_ref[...]) + bias_ref[...]).astype(BF16)
    turned_ref[...] = piece.T


def project(k, count, place, piece, weight, bias, earlier):
    rows, width = piece.shape
    cols = weight.shape[1]
    slot = (count - k) % count
    tile = rows // 2
    alias = earlier is not None
    return pl.pallas_call(
        functools.partial(project_kernel, slot),
        grid_spec=pltpu.PrefetchScalarGridSpec(
            num_scalar_prefetch=1,
            grid=(2,),
            in_specs=[
                pl.BlockSpec((tile, width), lambda i, p: (i, 0)),
                pl.BlockSpec((width, cols), lambda i, p: (0, 0)),
                pl.BlockSpec((1, cols), lambda i, p: (0, 0)),
            ]
            + ([ANY, ANY] if alias else []),
            out_specs=[
                pl.BlockSpec((tile, cols), lambda i, p: (2 * lax.rem(p[0] + slot, count) + i, 0)),
                pl.BlockSpec((width, tile), lambda i, p: (0, 2 * slot + i)),
            ],
        ),
        out_shape=[
            jax.ShapeDtypeStruct((count * rows, cols), BF16),
            jax.ShapeDtypeStruct((width, count * rows), BF16),
        ],
        input_output_aliases={4: 0, 5: 1} if alias else {},
        cost_estimate=light(4 * rows * width, 2 * rows * width * cols),
        name="project",
    )(place, piece, weight, bias, *(earlier if alias else ()))


def turn_kernel(own_ref, got_ref, out_ref):
    rows = own_ref.shape[0]
    out_ref[:, :rows] = own_ref[...].T
    out_ref[:, rows:] = got_ref[...].T


def turn_rows(own, got):
    rows, width = own.shape
    tile = width // 4
    return pl.pallas_call(
        turn_kernel,
        grid=(4,),
        in_specs=[pl.BlockSpec((rows, tile), lambda i: (0, i))] * 2,
        out_specs=pl.BlockSpec((tile, 2 * rows), lambda i: (i, 0)),
        out_shape=jax.ShapeDtypeStruct((width, 2 * rows), BF16),
        cost_estimate=light(8 * rows * width),
        name="turn_rows",
    )(own, got)


def wide(tile):
    lane = lax.broadcasted_iota(jnp.int32, tile.shape, 1)
    zero = jnp.zeros_like(tile)
    return jnp.concatenate(
        (jnp.where(lane < HEAD, tile, zero), jnp.where(lane < HEAD, zero, tile)), axis=0
    )


def both(row):
    return jnp.concatenate((row, row), axis=1)


def heads_of(acc):
    return jnp.concatenate((acc[:HEAD, :TILE], acc[HEAD:, TILE:]), axis=0)


def mask_rows(start_ref, step, shift):
    start = both(start_ref[...] - shift)
    place = both((step + 4) * TILE + lax.broadcasted_iota(jnp.int32, (1, TILE), 1))
    return start, place


def allowed(tile_index, start, place):
    key = tile_index * TILE + lax.broadcasted_iota(jnp.int32, (TILE, 2 * TILE), 0)
    return (key >= start) & (key <= place)


def turn(tile, meta_ref, tiles, per, count):
    block = tile // per
    return per * lax.rem(block - meta_ref[tiles] + count, count) + lax.rem(tile, per)


def attend_kernel(base, shift, meta_ref, start_ref, q_ref, k_ref, v_ref, *rest):
    o_ref, turned_ref, log_ref, acc_ref = rest[-4:]
    step = pl.program_id(0)
    query = wide(q_ref[...] * jnp.asarray(SCALE, BF16))
    start, place = mask_rows(start_ref, step, shift)
    acc_ref[...] = jnp.zeros_like(acc_ref)

    def body(j, carried):
        top, total = carried
        rows = pl.ds(pl.multiple_of(j * TILE, TILE), TILE)
        scores = nt(k_ref[rows, :], query)
        scores = jnp.where(allowed(j, start, place), scores, -1e30)
        new_top = jnp.maximum(top, jnp.max(scores, axis=0, keepdims=True))
        part = jnp.exp(scores - new_top)
        factor = jnp.exp(top - new_top)
        total = total * factor + jnp.sum(part, axis=0, keepdims=True)
        acc_ref[...] = acc_ref[...] * factor + tn(v_ref[rows, :], part.astype(BF16))
        return new_top, total

    top, total = lax.fori_loop(
        meta_ref[base + step] - shift // TILE,
        step + 5,
        body,
        (jnp.full((1, 2 * TILE), -1e30, F32), jnp.zeros((1, 2 * TILE), F32)),
    )
    turned = heads_of(acc_ref[...] / total)
    turned_ref[...] = turned
    o_ref[...] = turned.T.astype(BF16)
    logs = top + jnp.log(total)
    log_ref[0:1, :] = logs[:, :TILE]
    log_ref[1:2, :] = logs[:, TILE:]


def attend(base, shift, meta, start, q, qcol, k, kcol, v, vcol, earlier, tokens, count):
    n = k.shape[0]
    steps = (n - DOC_MAX) // TILE
    tiles = tokens // TILE
    per = tiles // count
    alias = earlier is not None
    specs = [
        pl.BlockSpec((1, TILE), lambda i, m: (0, base + i)),
        pl.BlockSpec((TILE, PAIR), lambda i, m: (base + i, qcol)),
        pl.BlockSpec((n, PAIR), lambda i, m: (0, kcol)),
        pl.BlockSpec((n, PAIR), lambda i, m: (0, vcol)),
    ] + [ANY] * (3 if alias else 0)
    return pl.pallas_call(
        functools.partial(attend_kernel, base, shift),
        grid_spec=pltpu.PrefetchScalarGridSpec(
            num_scalar_prefetch=1,
            grid=(steps,),
            in_specs=specs,
            out_specs=[
                pl.BlockSpec((TILE, PAIR), lambda i, m: (turn(base + i, m, tiles, per, count), 0)),
                pl.BlockSpec((PAIR, TILE), lambda i, m: (0, base + i)),
                pl.BlockSpec((8, TILE), lambda i, m: (0, base + i)),
            ],
            scratch_shapes=[pltpu.VMEM((PAIR, 2 * TILE), F32)],
        ),
        out_shape=[
            jax.ShapeDtypeStruct((tokens, PAIR), BF16),
            jax.ShapeDtypeStruct((PAIR, tokens), F32),
            jax.ShapeDtypeStruct((8, tokens), F32),
        ],
        input_output_aliases={5: 0, 6: 1, 7: 2} if alias else {},
        cost_estimate=light(4 * n * PAIR),
        name="attend",
    )(meta, start, q, k, v, *(earlier if alias else ()))


def back_tile(shift, low, start_ref, q_ref, k_ref, v_ref, do_ref, turned_ref, log_ref, dk_ref, dv_ref, acc_ref):
    step = pl.program_id(0)
    query = wide(q_ref[...] * jnp.asarray(SCALE, BF16))
    out_back = wide(do_ref[...])
    start, place = mask_rows(start_ref, step, shift)
    product = do_ref[...].astype(F32).T * turned_ref[...]
    delta = jnp.concatenate(
        (
            jnp.sum(product[:HEAD], axis=0, keepdims=True),
            jnp.sum(product[HEAD:], axis=0, keepdims=True),
        ),
        axis=1,
    )
    logs = jnp.concatenate((log_ref[0:1, :], log_ref[1:2, :]), axis=1)
    acc_ref[...] = jnp.zeros_like(acc_ref)

    def body(j, carried):
        rows = pl.ds(pl.multiple_of(j * TILE, TILE), TILE)
        key_tile = k_ref[rows, :]
        scores = jnp.where(allowed(j, start, place), nt(key_tile, query), -1e30)
        prob = jnp.exp(scores - logs)
        prob_back = nt(v_ref[rows, :], out_back)
        score_back = (prob * (prob_back - delta)).astype(BF16)
        dv_ref[rows, :] += nn(prob.astype(BF16), out_back)
        dk_ref[rows, :] += nn(score_back, query)
        acc_ref[...] += tn(key_tile, score_back)
        return carried

    lax.fori_loop(low, step + 5, body, 0)
    return (heads_of(acc_ref[...]) * SCALE).T.astype(BF16)


def early_kernel(meta_ref, start_ref, q_ref, k_ref, v_ref, do_ref, turned_ref, log_ref, dq_ref, gone_ref, dk_ref, dv_ref, kept_k, kept_v, acc_ref):
    step = pl.program_id(0)

    @pl.when(step == 0)
    def _():
        kept_k[...] = jnp.zeros_like(kept_k)
        kept_v[...] = jnp.zeros_like(kept_v)

    dq_ref[...] = back_tile(
        0, meta_ref[step], start_ref, q_ref, k_ref, v_ref, do_ref, turned_ref, log_ref,
        kept_k, kept_v, acc_ref,
    )

    @pl.when(step == pl.num_programs(0) - 1)
    def _():
        gone_ref[:, :PAIR] = kept_k[:DOC_MAX, :].astype(BF16)
        gone_ref[:, PAIR:] = kept_v[:DOC_MAX, :].astype(BF16)
        dk_ref[...] = kept_k[DOC_MAX:, :]
        dv_ref[...] = kept_v[DOC_MAX:, :]


def late_kernel(base, fresh, per, count, meta_ref, start_ref, q_ref, k_ref, v_ref, do_ref, turned_ref, log_ref, dq_in, dk_in, dv_in, back_ref, packed_ref, value_ref, sums_ref, kept_k, kept_v, acc_ref):
    step = pl.program_id(0)
    held = dk_in.shape[0]
    tiles = packed_ref.shape[0] // TILE

    def rows_of(tile):
        row = turn(tile, meta_ref, tiles, per, count) * TILE
        return pl.ds(pl.multiple_of(row, TILE), TILE)

    @pl.when(step == 0)
    def _():
        kept_k[:held, :] = dk_in[...]
        kept_v[:held, :] = dv_in[...]
        kept_k[held:, :] = back_ref[:, :PAIR].astype(F32)
        kept_v[held:, :] = back_ref[:, PAIR:].astype(F32)
        for i in range(base):
            packed_ref[rows_of(i), :PAIR] = dq_in[i * TILE : (i + 1) * TILE, :]

    packed_ref[rows_of(base + step), :PAIR] = back_tile(
        DOC_MAX, meta_ref[base + step] - DOC_MAX // TILE, start_ref, q_ref, k_ref, v_ref, do_ref,
        turned_ref, log_ref, kept_k, kept_v, acc_ref,
    )

    @pl.when(step == pl.num_programs(0) - 1)
    def _():
        for i in range(tiles):
            span = slice(i * TILE, (i + 1) * TILE)
            packed_ref[rows_of(i), PAIR : 2 * PAIR] = kept_k[span, :].astype(BF16)
            if fresh:
                packed_ref[rows_of(i), 2 * PAIR :] = kept_v[span, :].astype(BF16)
        if not fresh:
            value_ref[...] = kept_v[...]
        else:
            value_ref[...] = jnp.zeros_like(value_ref)
        sums_ref[...] = jnp.broadcast_to(
            jnp.sum(packed_ref[...].astype(F32), axis=0, keepdims=True), sums_ref.shape
        )


def back_specs(base, qcol, n, kcol, vcol, tiles, per, count):
    return [
        pl.BlockSpec((1, TILE), lambda i, m: (0, base + i)),
        pl.BlockSpec((TILE, PAIR), lambda i, m: (base + i, qcol)),
        pl.BlockSpec((n, PAIR), lambda i, m: (0, kcol)),
        pl.BlockSpec((n, PAIR), lambda i, m: (0, vcol)),
        pl.BlockSpec((TILE, PAIR), lambda i, m: (turn(base + i, m, tiles, per, count), 0)),
        pl.BlockSpec((PAIR, TILE), lambda i, m: (0, base + i)),
        pl.BlockSpec((8, TILE), lambda i, m: (0, base + i)),
    ]


def whole(shape):
    return pl.BlockSpec(shape, lambda i, m: (0,) * len(shape))


def back_early(meta, start, q, qcol, k, kcol, v, vcol, do, turned, logs, tokens, count):
    n = k.shape[0]
    held = n - DOC_MAX
    tiles = tokens // TILE
    return pl.pallas_call(
        early_kernel,
        grid_spec=pltpu.PrefetchScalarGridSpec(
            num_scalar_prefetch=1,
            grid=(held // TILE,),
            in_specs=back_specs(0, qcol, n, kcol, vcol, tiles, tiles // count, count),
            out_specs=[
                pl.BlockSpec((TILE, PAIR), lambda i, m: (i, 0)),
                whole((DOC_MAX, 2 * PAIR)),
                whole((held, PAIR)),
                whole((held, PAIR)),
            ],
            scratch_shapes=[
                pltpu.VMEM((n, PAIR), F32),
                pltpu.VMEM((n, PAIR), F32),
                pltpu.VMEM((PAIR, 2 * TILE), F32),
            ],
        ),
        out_shape=[
            jax.ShapeDtypeStruct((held, PAIR), BF16),
            jax.ShapeDtypeStruct((DOC_MAX, 2 * PAIR), BF16),
            jax.ShapeDtypeStruct((held, PAIR), F32),
            jax.ShapeDtypeStruct((held, PAIR), F32),
        ],
        cost_estimate=light(12 * n * PAIR),
        name="back_early",
    )(meta, start, q, k, v, do, turned, logs)


def back_late(meta, start, q, qcol, k, kcol, v, vcol, do, turned, logs, dq, dk, dv, back, fresh, tokens, count):
    n = k.shape[0]
    held = n - DOC_MAX
    tiles = tokens // TILE
    per = tiles // count
    base = (tokens - held) // TILE
    cols = (3 if fresh else 2) * PAIR
    return pl.pallas_call(
        functools.partial(late_kernel, base, fresh, per, count),
        grid_spec=pltpu.PrefetchScalarGridSpec(
            num_scalar_prefetch=1,
            grid=(held // TILE,),
            in_specs=back_specs(base, qcol, n, kcol, vcol, tiles, per, count)
            + [whole(dq.shape), whole(dk.shape), whole(dv.shape), whole(back.shape)],
            out_specs=[
                whole((tokens, cols)),
                whole((8, PAIR) if fresh else (tokens, PAIR)),
                whole((8, cols)),
            ],
            scratch_shapes=[
                pltpu.VMEM((n, PAIR), F32),
                pltpu.VMEM((n, PAIR), F32),
                pltpu.VMEM((PAIR, 2 * TILE), F32),
            ],
        ),
        out_shape=[
            jax.ShapeDtypeStruct((tokens, cols), BF16),
            jax.ShapeDtypeStruct((8, PAIR) if fresh else (tokens, PAIR), F32),
            jax.ShapeDtypeStruct((8, cols), F32),
        ],
        cost_estimate=light(12 * n * PAIR),
        name="back_late",
    )(meta, start, q, k, v, do, turned, logs, dq, dk, dv, back)


def store_grad(grad_ref, grad):
    runs, _, lanes, rows, cols = grad_ref.shape
    for j in range(lanes):
        grad_ref[:, 0, j] = grad[:, j * cols : (j + 1) * cols].reshape(runs, rows, cols)


def accumulate(ref, value):
    @pl.when(pl.program_id(0) == 0)
    def _():
        ref[...] = value

    @pl.when(pl.program_id(0) > 0)
    def _():
        ref[...] += value


def up_kernel(places_ref, sn_ref, got_ref, cot_ref, up_ref, bias_ref, down_ref, out_ref, other_ref, slope_ref, grad_ref, act_ref):
    width = up_ref.shape[0] * up_ref.shape[1]
    rows = sn_ref.shape[0]
    up = up_ref[...].reshape(width, UNIT)
    down = down_ref[...].reshape(UNIT, width)
    for i, (piece_ref, sum_ref) in enumerate(((sn_ref, out_ref), (got_ref, other_ref))):
        span = slice(i * rows, (i + 1) * rows)
        hidden = nn(piece_ref[...], up) + bias_ref[0]
        square = hidden * hidden
        curve = jnp.tanh(GELU_A * (hidden + GELU_B * (hidden * square)))
        half = 0.5 * (1.0 + curve)
        activated = (hidden * half).astype(BF16)
        slope_ref[span, :] = half + 0.5 * hidden * (1.0 - curve * curve) * (
            GELU_A * (1.0 + 3.0 * GELU_B * square)
        )
        act_ref[span, :] = activated
        accumulate(sum_ref, nn(activated, down))
    store_grad(grad_ref, nn(cot_ref[...], act_ref[...]).astype(BF16))


def feed_specs(gathered, seq, parts, width):
    part = width // seq
    per = width // UNIT
    run = seq // 2

    def spot(i, p):
        return lax.rem(p[0] + i, parts)

    grad_spec = pl.BlockSpec(
        (run, 1, UNIT // PAIR, width // run, PAIR), lambda i, p: (0, i, 0, 0, 0)
    )

    grad = (run, parts, UNIT // PAIR, width // run, PAIR)
    return (
        pl.BlockSpec((seq, part, UNIT), lambda i, p: (spot(i, p), 0, p[1])),
        pl.BlockSpec((UNIT // part, part, width), lambda i, p: (spot(i, p) * per + p[1], 1, 0)),
        grad_spec,
        grad,
    )


def fixed(shape):
    return pl.BlockSpec(shape, lambda i, p: (0,) * len(shape))


def feed_up(places, sn, got, cot_turned, gathered, bias, seq, parts):
    rows, width = sn.shape
    up_spec, down_spec, grad_spec, grad = feed_specs(gathered, seq, parts, width)
    return pl.pallas_call(
        up_kernel,
        grid_spec=pltpu.PrefetchScalarGridSpec(
            num_scalar_prefetch=1,
            grid=(parts,),
            in_specs=[
                fixed((rows, width)),
                fixed((rows, width)),
                fixed((width, 2 * rows)),
                up_spec,
                pl.BlockSpec((1, 1, UNIT), lambda i, p: (lax.rem(parts - i, parts), 0, p[1])),
                down_spec,
            ],
            out_specs=[
                fixed((rows, width)),
                fixed((rows, width)),
                pl.BlockSpec((2 * rows, UNIT), lambda i, p: (0, i)),
                grad_spec,
            ],
            scratch_shapes=[pltpu.VMEM((2 * rows, UNIT), BF16)],
        ),
        out_shape=[
            jax.ShapeDtypeStruct((rows, width), F32),
            jax.ShapeDtypeStruct((rows, width), F32),
            jax.ShapeDtypeStruct((2 * rows, parts * UNIT), F32),
            jax.ShapeDtypeStruct(grad, BF16),
        ],
        cost_estimate=light(16 * rows * width, 24 * rows * width * width),
        name="feed_up",
    )(places, sn, got, cot_turned, gathered, bias, gathered)


def down_kernel(places_ref, cot_ref, cot_got_ref, sn_ref, got_ref, slope_ref, up_ref, down_ref, back_ref, other_ref, grad_ref, bias_ref, turned_ref, hidden_ref):
    width = up_ref.shape[0] * up_ref.shape[1]
    rows = sn_ref.shape[0]

    @pl.when(pl.program_id(0) == 0)
    def _():
        turned_ref[:, :rows] = sn_ref[...].T
        turned_ref[:, rows:] = got_ref[...].T

    up = up_ref[...].reshape(width, UNIT)
    down = down_ref[...].reshape(UNIT, width)
    total = jnp.zeros((1, UNIT), F32)
    for i, (piece_ref, sum_ref) in enumerate(((cot_ref, back_ref), (cot_got_ref, other_ref))):
        span = slice(i * rows, (i + 1) * rows)
        rounded = (nt(piece_ref[...], down) * slope_ref[span, :]).astype(BF16)
        total = total + jnp.sum(rounded.astype(F32), axis=0, keepdims=True)
        hidden_ref[span, :] = rounded
        accumulate(sum_ref, nt(rounded, up))
    bias_ref[0] = total
    store_grad(grad_ref, nn(turned_ref[...], hidden_ref[...]).astype(BF16))


def feed_down(places, cot, cot_got, sn, got, slope, gathered, seq, parts, extra):
    rows, width = cot.shape
    up_spec, down_spec, grad_spec, grad = feed_specs(gathered, seq, parts, width)
    return pl.pallas_call(
        down_kernel,
        grid_spec=pltpu.PrefetchScalarGridSpec(
            num_scalar_prefetch=1,
            grid=(parts,),
            in_specs=[fixed((rows, width))] * 4
            + [
                pl.BlockSpec((2 * rows, UNIT), lambda i, p: (0, i)),
                up_spec,
                down_spec,
            ],
            out_specs=[
                fixed((rows, width)),
                fixed((rows, width)),
                grad_spec,
                pl.BlockSpec((1, 1, UNIT), lambda i, p: (i, 0, 0)),
            ],
            scratch_shapes=[
                pltpu.VMEM((width, 2 * rows), BF16),
                pltpu.VMEM((2 * rows, UNIT), BF16),
            ],
        ),
        out_shape=[
            jax.ShapeDtypeStruct((rows, width), F32),
            jax.ShapeDtypeStruct((rows, width), F32),
            jax.ShapeDtypeStruct(grad[:2] + (grad[2] + extra,) + grad[3:], BF16),
            jax.ShapeDtypeStruct((parts, 1, UNIT), F32),
        ],
        cost_estimate=light(16 * rows * width, 24 * rows * width * width),
        name="feed_down",
    )(places, cot, cot_got, sn, got, slope, gathered, gathered)


def back_norm_kernel(own_ref, came_ref, cot_ref, hat_ref, inverse_ref, gain_ref, mixing_ref, mixed_ref, grads_ref, middle_ref, attended_ref, sums_ref, grad_ref, wide_ref):
    step = pl.program_id(0)
    back = own_ref[...] + came_ref[...]
    hat = hat_ref[...]
    cot = cot_ref[...].astype(F32)
    middle_back = cot + norm_back(back, gain_ref[...], hat, inverse_ref[...])
    rounded = middle_back.astype(BF16)
    middle_ref[...] = middle_back
    attended = nt(rounded, mixing_ref[...]).astype(BF16)
    for j in range(attended_ref.shape[0]):
        attended_ref[j] = attended[:, j * PAIR : (j + 1) * PAIR]
    accumulate(wide_ref, nn(rounded.T, mixed_ref[...]))

    @pl.when(step == 0)
    def _():
        sums_ref[...] = jnp.zeros_like(sums_ref)

    for i, value in enumerate((back * hat, back, middle_back, cot)):
        sums_ref[i : i + 1, :] += jnp.sum(value, axis=0, keepdims=True)

    @pl.when(step == pl.num_programs(0) - 1)
    def _():
        runs, parts, lanes, rows, cols = grad_ref.shape
        for k in range(parts):
            for j in range(lanes):
                left = (k * lanes + j) * cols
                value = wide_ref[:, left : left + cols].astype(BF16)
                grad_ref[:, (parts - k) % parts, j] = value.reshape(runs, rows, cols)


def back_norm(own, came, cot, hat, inverse, gain, mixing, mixed, grads):
    rows, width = own.shape
    blocks = mixing.shape[0] // PAIR
    runs, parts, lanes, lines, cols = grads.shape
    extra = blocks // parts
    tile = rows // 2
    row = pl.BlockSpec((tile, width), lambda i: (i, 0))
    return pl.pallas_call(
        back_norm_kernel,
        grid=(2,),
        in_specs=[
            row, row, row, row,
            pl.BlockSpec((tile, 1), lambda i: (i, 0)),
            pl.BlockSpec((1, width), lambda i: (0, 0)),
            pl.BlockSpec(mixing.shape, lambda i: (0, 0)),
            row,
            ANY,
        ],
        out_specs=[
            row,
            pl.BlockSpec((blocks, tile, PAIR), lambda i: (0, i, 0)),
            pl.BlockSpec((8, width), lambda i: (0, 0)),
            pl.BlockSpec((runs, parts, extra, lines, cols), lambda i: (0, 0, UNIT // PAIR // extra, 0, 0)),
        ],
        out_shape=[
            jax.ShapeDtypeStruct((rows, width), F32),
            jax.ShapeDtypeStruct((blocks, rows, PAIR), BF16),
            jax.ShapeDtypeStruct((8, width), F32),
            jax.ShapeDtypeStruct(grads.shape, BF16),
        ],
        input_output_aliases={8: 3},
        scratch_shapes=[pltpu.VMEM((width, width), F32)],
        cost_estimate=light(16 * rows * width, 4 * rows * width * width),
        name="back_norm",
    )(own, came, cot, hat, inverse, gain[None], mixing, mixed, grads)


def front_norm_kernel(parts, places_ref, *refs):
    pieces, (weight_ref, middle_ref, hat_ref, inverse_ref, gain_ref, out_ref) = refs[:-6], refs[-6:]
    cut = pieces[0].shape[1]
    back = jnp.zeros(out_ref.shape, F32)
    for k in range(parts):
        spot = lax.rem(places_ref[0] - k + parts, parts)
        back = back + nn(pieces[2 * k][...], weight_ref[spot, :cut, :])
        back = back + nn(pieces[2 * k + 1][...], weight_ref[spot, cut:, :])
    out_ref[...] = middle_ref[...] + norm_back(
        back, gain_ref[...], hat_ref[...], inverse_ref[...]
    )


def front_norm(places, pieces, weight, middle, hat, inverse, gain):
    rows, width = middle.shape
    parts = weight.shape[0]
    tile = rows // 4

    def row(cols):
        return pl.BlockSpec((tile, cols), lambda i, p: (i, 0))

    return pl.pallas_call(
        functools.partial(front_norm_kernel, parts),
        grid_spec=pltpu.PrefetchScalarGridSpec(
            num_scalar_prefetch=1,
            grid=(4,),
            in_specs=[row(piece.shape[1]) for piece in pieces]
            + [fixed(weight.shape), row(width), row(width), row(1), fixed((1, width))],
            out_specs=row(width),
        ),
        out_shape=jax.ShapeDtypeStruct((rows, width), F32),
        cost_estimate=light(16 * rows * width, 2 * rows * width * weight.shape[0] * weight.shape[1]),
        name="front_norm",
    )(places, *pieces, weight, middle, hat, inverse, gain[None])


def around(value, steps):
    count = lax.axis_size("tp")
    return lax.ppermute(value, "tp", [(i, (i + steps) % count) for i in range(count)])


def flipped(value, axis, bit):
    count = lax.axis_size(axis)
    return lax.ppermute(value, axis, [(i, i ^ bit) for i in range(count)])


def along(value, steps):
    count = lax.axis_size(SEQ)
    first, last = max(0, -steps), min(count, count - steps)
    return lax.ppermute(value, SEQ, [(i, i + steps) for i in range(first, last)])


def butterfly(value, axis):
    bit = 1
    while bit < lax.axis_size(axis):
        value = value + flipped(value, axis, bit)
        bit *= 2
    return value


def pick(value, index, dim):
    return lax.dynamic_index_in_dim(value, index, dim, keepdims=False)


def joined(a, b):
    return (a.astype(F32) + b.astype(F32)).astype(BF16)


def seq_bits():
    bits, bit = [], 1
    while bit < lax.axis_size(SEQ):
        bits.append(bit)
        bit *= 2
    return bits


def tied(*groups):
    return lax.optimization_barrier(groups)


class Scatter:
    def __init__(self, value, place):
        self.place = place
        self.bits = seq_bits()
        self.left = value.reshape((2,) * len(self.bits) + value.shape[1:])
        self.issue()

    def issue(self):
        bit = self.bits.pop(0)
        dim = len(self.bits)
        mine = (self.place // bit) % 2
        self.parts = (
            pick(self.left, mine, dim), flipped(pick(self.left, 1 - mine, dim), SEQ, bit)
        )

    def merge(self):
        self.left = joined(*self.parts)
        if self.bits:
            self.issue()
            return True
        return False

    def result(self):
        while self.merge():
            pass
        return self.left


def in_order(own, other, bit, place, dim):
    low = (place // bit) % 2 == 0
    return jnp.stack((jnp.where(low, own, other), jnp.where(low, other, own)), axis=dim)


def quarter(shard, place):
    size = shard.shape[0] // 4
    spot = 2 * ((place // 2) % 2) + place % 2
    return lax.dynamic_slice_in_dim(shard, spot * size, size, 0)


def from_shards(piece):
    return [around(piece, k) for k in range(1, lax.axis_size("tp"))]


def center(rows):
    average = jnp.mean(rows, axis=-1, keepdims=True)
    centered = rows - average
    inverse = lax.rsqrt(jnp.mean(centered * centered, axis=-1, keepdims=True) + EPSILON)
    return centered * inverse, inverse


def norm_back(grad, gain, xhat, inverse):
    e = grad * gain
    return inverse * (
        e
        - jnp.mean(e, axis=-1, keepdims=True)
        - xhat * jnp.mean(e * xhat, axis=-1, keepdims=True)
    )


def local(
    stream, segments, skip_values, first_gain, first_shift, query_weight, query_bias, key_weight,
    value_weight, value_bias, mixing_weight, mixing_bias, second_gain, second_shift, up_weight,
    up_bias, down_weight, down_bias, cotangent,
):
    rows, width = stream.shape
    tokens = skip_values.shape[0]
    own = query_weight.shape[1]
    tp = lax.axis_size("tp")
    seq = lax.axis_size(SEQ)
    seq_place = lax.axis_index(SEQ)
    tp_place = lax.axis_index("tp")
    core = lax.axis_index("core")
    places = jnp.stack((tp_place, core)).astype(jnp.int32)
    half = tokens - DOC_MAX
    part = width // seq
    kcol = own // PAIR

    stream_wide = stream.astype(F32)
    first_hat, first_inverse = center(stream_wide)
    piece = (first_hat * first_gain + first_shift).astype(BF16)
    piece, up_weight, down_weight, mixing_weight, segments, cotangent = lax.optimization_barrier(
        (piece, up_weight, down_weight, mixing_weight, segments, cotangent)
    )

    def own_rows(shard):
        size = shard.shape[0] // seq
        return lax.dynamic_slice_in_dim(shard, seq_place * size, size, 0)

    qkv_turned = jnp.concatenate(
        (
            query_weight[:, :PAIR], key_weight[:, :PAIR], value_weight,
            query_weight[:, PAIR:], key_weight[:, PAIR:],
        ),
        axis=1,
    ).T
    packet = jnp.concatenate([own_rows(w) for w in (up_weight, down_weight)], axis=0)
    qkv_packet = own_rows(qkv_turned)
    bias_pieces = jnp.stack([up_bias] + [around(up_bias, k) for k in range(1, tp)])[:, None]
    cot_got = flipped(cotangent, "core", 1)

    padded = jnp.concatenate((jnp.full((DOC_MAX,), -1, jnp.int32), segments))
    window = lax.dynamic_slice_in_dim(padded, seq_place * tokens, DOC_MAX + tokens, 0)
    start = jnp.sum(
        (window[:, None] < window[None, DOC_MAX:]).astype(jnp.int32), axis=0, keepdims=True
    )
    meta = jnp.concatenate((start[0, ::TILE] // TILE, places))
    halo_skip = along(skip_values[half:], 1)
    wqkv = jnp.concatenate((query_weight, key_weight, value_weight), axis=1)
    bias = jnp.concatenate((query_bias, jnp.zeros((own,), F32), value_bias))[None]
    made = None
    for k in range(tp):
        if k == tp - 1:
            piece, meta, start, bias_pieces, cot_got, mixing_piece = tied(
                piece, meta, start, bias_pieces, cot_got, quarter(mixing_weight, seq_place)
            )
        elif k > 0:
            piece, made = tied(piece, made)
        ahead = around(piece, 1) if k < tp - 1 else None
        made = project(k, tp, places, piece, wqkv, bias, made)
        piece = ahead
        if k == GATHER_STEP:
            piece, packet = tied(piece, packet)
            gathered = lax.all_gather(packet, ("tp",) + SEQ, axis=0, tiled=False)
    qkv, normed_turned = made
    halo = along(qkv[half:, own:], 1)
    qkv, mixing_piece = tied(qkv, mixing_piece)
    mixing_got = from_shards(mixing_piece)
    early = early_skip = None

    def values_of(pair):
        if pair == 0:
            return (qkv, 2 * kcol), (early, kcol)
        return (skip_values, 0), (early_skip, 0)

    steps = half // TILE
    attended = []
    for pair in range(2):
        (v, vcol), _ = values_of(pair)
        attended.append(
            attend(steps, DOC_MAX, meta, start, qkv, pair, qkv, kcol + pair, v, vcol, None, tokens, tp)
        )
    attended, halo, halo_skip, mixing_got = tied(attended, halo, halo_skip, mixing_got)
    early_skip = jnp.concatenate((halo_skip, skip_values[:half]), axis=0)
    early = jnp.concatenate((halo, qkv[:half, own:]), axis=0)
    mixing_got = jnp.stack(mixing_got)
    mixing_other = flipped(mixing_got, SEQ, 2)
    arrived = []
    for pair in range(2):
        _, (v, vcol) = values_of(pair)
        attended[pair] = attend(
            0, 0, meta, start, qkv, pair, early, pair, v, vcol, attended[pair], tokens, tp
        )
        blocks = attended[pair][0].reshape(tp, rows, PAIR)
        arrived.append([blocks[0]] + [around(blocks[k], k) for k in range(1, tp)])
    attended[1], mixing_got, mixing_other, cotangent, cot_got = tied(
        attended[1], mixing_got, mixing_other, cotangent, cot_got
    )
    mixing_got = in_order(mixing_got, mixing_other, 2, seq_place, 1)
    mixing_other = flipped(mixing_got, "core", 1)
    cot_turned = turn_rows(cotangent, cot_got)
    mixing_rot = in_order(mixing_got, mixing_other, 1, seq_place, 2).reshape(-1, width)
    mixing_rot = jnp.concatenate((mixing_weight, mixing_rot), axis=0)
    arrived, mixing_rot, cot_turned = tied(arrived, mixing_rot, cot_turned)

    mixed_in = jnp.concatenate([arrived[pair][k] for k in range(tp) for pair in range(2)], axis=1)
    middle = stream_wide + nn(mixed_in, mixing_rot) + mixing_bias
    second_hat, second_inverse = center(middle)
    second = (second_hat * second_gain + second_shift).astype(BF16)

    got = flipped(second, "core", 1)
    got, qkv_packet = tied(got, qkv_packet)
    qkv_full = lax.all_gather(qkv_packet, ("tp",) + SEQ, axis=0, tiled=False)
    qkv_full = qkv_full.reshape(tp, -1, width)
    lost, lost_other, slope, down_grads = feed_up(
        places, second, got, cot_turned, gathered, bias_pieces, seq, tp
    )

    def over_runs(grads):
        flat = grads.reshape(grads.shape[0], -1, PAIR)
        flat = lax.psum_scatter(flat, "run", scatter_dimension=0, tiled=True)
        return flat.reshape(grads.shape[1:])

    def over_shards(grads):
        return [grads[0]] + [around(grads[k], k) for k in range(1, tp)]

    down_grads = over_runs(down_grads)
    back_own, back_other, up_grads, up_bias_grad = feed_down(
        places, cotangent, cot_got, second, got, slope, gathered, seq, tp, UNIT // PAIR
    )
    back_came = flipped(back_other, "core", 1)
    middle_back, attended_back, norm_sums, up_grads = back_norm(
        back_own, back_came, cotangent, second_hat, second_inverse, second_gain, mixing_rot,
        mixed_in, up_grads,
    )
    up_grads = over_runs(up_grads)[:, : (UNIT + own) // PAIR]

    def send_back(pair):
        return [attended_back[pair]] + [
            around(attended_back[2 * k + pair], -k) for k in range(1, tp)
        ]

    moved = send_back(0)
    moved, attended_back, lost_other, qkv_full = tied(moved, attended_back, lost_other, qkv_full)
    returned = [jnp.concatenate(moved, axis=0)]
    moved = send_back(1)
    lost_came = flipped(lost_other, "core", 1)

    halves = []
    for pair in range(2):
        _, (v, vcol) = values_of(pair)
        _, turned, logs = attended[pair]
        dq, gone, dk, dv = back_early(
            meta, start, qkv, pair, early, pair, v, vcol, returned[pair], turned, logs, tokens, tp
        )
        halves.append((dq, dk, dv, along(gone, -1)))
        if pair == 0:
            dq, moved, lost_came = tied(dq, moved, lost_came)
            returned.append(jnp.concatenate(moved, axis=0))
    halves, norm_sums, up_bias_grad = tied(halves, norm_sums, up_bias_grad)
    halves = [list(group) for group in halves]
    made_here = [pick(up_bias_grad.reshape(tp, UNIT), (k - tp_place) % tp, 0) for k in range(tp)]
    made_here = jnp.stack(made_here).reshape(tp, 1, -1, PAIR)
    which = lax.broadcasted_iota(jnp.int32, (tp, 2) + made_here.shape[2:], 1)
    early_sums = jnp.concatenate(
        (
            norm_sums[:4].reshape(-1, PAIR),
            jnp.where(which == core, made_here, 0.0).reshape(-1, PAIR),
        ),
        axis=0,
    )
    packets, column_sums, pieces = [], [], []
    skip_gradient = None
    for pair in range(2):
        (v, vcol), _ = values_of(pair)
        _, turned, logs = attended[pair]
        packed, values, sums = back_late(
            meta, start, qkv, pair, qkv, kcol + pair, v, vcol, returned[pair], turned, logs,
            *halves[pair], pair == 0, tokens, tp,
        )
        blocks = packed.reshape(tp, rows, packed.shape[1])
        pieces.append([blocks[0]] + [around(blocks[k], k) for k in range(1, tp)])
        if pair == 0:
            halves[1], packed, down_grads = tied(halves[1], packed, down_grads)
            down_grads = over_shards(down_grads)
        else:
            skip_gradient = values
        packets.append(packed)
        column_sums.append(sums[0])
    packets, pieces[0], middle = tied(packets, pieces[0], middle)
    output = (middle + (lost + lost_came) + down_bias).astype(BF16)
    wide_grad = nn(normed_turned, jnp.concatenate(packets, axis=1))
    weight_sum = Scatter(wide_grad.astype(BF16).reshape(seq, part, -1), seq_place)
    pieces[1], weight_sum.parts, up_grads = tied(pieces[1], weight_sum.parts, up_grads)
    up_grads = over_shards(up_grads)
    weight_sum.merge()
    stream_gradient = front_norm(
        places, [pieces[pair][k] for k in range(tp) for pair in range(2)], qkv_full, middle_back,
        first_hat, first_inverse, first_gain,
    )
    column_sum = jnp.concatenate(column_sums)
    columns = qkv_turned.T.astype(F32)
    first_shift_part = jnp.sum(columns * column_sum, axis=1)
    hat_grad = (wide_grad - first_shift[:, None] * column_sum) / first_gain[:, None]
    first_gain_part = jnp.sum(columns * hat_grad, axis=1)

    def widen(value):
        size = value.shape[0]
        return lax.dynamic_update_slice_in_dim(
            jnp.zeros((size * tp,), F32), value, tp_place * size, 0
        )

    query_part = jnp.concatenate((column_sum[:PAIR], column_sum[3 * PAIR : 4 * PAIR]))
    late_sums = (
        first_gain_part, first_shift_part, widen(query_part),
        widen(column_sum[2 * PAIR : 3 * PAIR]),
    )
    late_sums = [value.reshape(-1, PAIR) for value in late_sums]
    sums = jnp.concatenate(late_sums + [early_sums], axis=0)
    for spot, bit in enumerate(seq_bits()):
        if spot + 1 < tp:
            sums, down_grads[spot + 1] = tied(sums, down_grads[spot + 1])
        sums = sums + flipped(sums, SEQ, bit)
    sums = butterfly(sums, "tp")
    weight_grad = weight_sum.result().astype(F32)

    def both_cores(blocks):
        cut = sum(block.astype(F32) for block in blocks)
        cut = cut.reshape(cut.shape[0], 2, part, PAIR)
        kept = pick(cut, core, 1)
        came = flipped(pick(cut, 1 - core, 1), "core", 1)
        lanes = UNIT // PAIR
        return jnp.concatenate(
            (
                jnp.where(core == 0, kept[:lanes], came[:lanes]),
                jnp.where(core == 0, came[:lanes], kept[:lanes]),
            ),
            axis=0,
        ), kept[lanes:] + came[lanes:]

    down_gradient = both_cores(down_grads)[0].transpose(0, 2, 1).reshape(-1, part)
    up_gradient, mixing_gradient = both_cores(up_grads)
    up_gradient = up_gradient.transpose(1, 0, 2).reshape(part, -1)
    mixing_gradient = mixing_gradient.transpose(0, 2, 1).reshape(-1, part)

    query_gradient = jnp.concatenate(
        (weight_grad[:, :PAIR], weight_grad[:, 3 * PAIR : 4 * PAIR]), axis=1
    )
    key_gradient = jnp.concatenate(
        (weight_grad[:, PAIR : 2 * PAIR], weight_grad[:, 4 * PAIR :]), axis=1
    )
    value_gradient = weight_grad[:, 2 * PAIR : 3 * PAIR]

    cuts = []
    for size in (width, width, width, width // 2) + (width,) * 4 + (tp * width,):
        cuts.append(sums[: size // PAIR].reshape(-1))
        sums = sums[size // PAIR :]
    (
        first_gain_grad, first_shift_grad, query_bias_grad, value_bias_grad, second_gain_grad,
        second_shift_grad, mixing_bias_grad, down_bias_grad, up_bias_grad,
    ) = cuts
    return (
        output,
        stream_gradient,
        skip_gradient,
        query_gradient,
        query_bias_grad,
        key_gradient,
        value_gradient,
        value_bias_grad,
        mixing_gradient,
        mixing_bias_grad,
        first_gain_grad,
        first_shift_grad,
        second_gain_grad,
        second_shift_grad,
        up_gradient,
        up_bias_grad,
        down_gradient,
        down_bias_grad,
    )


def solution(mesh):
    seq, tp = mesh.shape["seq"], mesh.shape["tp"]
    mesh = jax.sharding.Mesh(mesh.devices.reshape(seq // 2, 2, tp), SEQ + ("tp",))
    split = P(SEQ + ("tp",), None)
    column = P(None, "tp")
    tile = P(SEQ, "tp")
    turned = P("tp", SEQ)
    in_specs = (
        split, P(), tile, P(), P(), column, P("tp"), column, column, P("tp"),
        P("tp", None), P(), P(), P(), column, P("tp"), P("tp", None), P(), split,
    )
    out_specs = (
        split, split, tile, tile, P(), tile, tile, P(), turned, P(), P(), P(), P(), P(),
        tile, P(), turned, P(),
    )
    return jax.shard_map(local, mesh=mesh, in_specs=in_specs, out_specs=out_specs, check_vma=False)
```

```python
import functools

import jax
import jax.numpy as jnp
from jax import lax
from jax.experimental import pallas as pl
from jax.experimental.pallas import tpu as pltpu
from jax.sharding import PartitionSpec as P

HEAD = 64
DOC_MAX = 1024
PAIR = 2 * HEAD
TILE = 256
UNIT = 512
EPSILON = 1e-05
F32 = jnp.float32
BF16 = jnp.bfloat16
SCALE = HEAD ** -0.5
GELU_A = 0.7978845608028654
GELU_B = 0.044715
SEQ = ("run", "core")
GATHER_STEP = 1


def dot(a, b, dims, out=F32):
    return lax.dot_general(a, b, (dims, ((), ())), preferred_element_type=out)


def nn(a, b):
    return dot(a, b, ((1,), (0,)))


def nt(a, b):
    return dot(a, b, ((1,), (1,)))


def tn(a, b):
    return dot(a, b, ((0,), (0,)))


def light(bytes_accessed, flops=1):
    return pl.CostEstimate(flops=flops, bytes_accessed=bytes_accessed, transcendentals=0)


ANY = pl.BlockSpec(memory_space=pl.ANY)


def project_kernel(slot, place_ref, piece_ref, weight_ref, bias_ref, *rest):
    qkv_ref, turned_ref = rest[-2:]
    piece = piece_ref[...]
    qkv_ref[...] = (nn(piece, weight_ref[...]) + bias_ref[...]).astype(BF16)
    turned_ref[...] = piece.T


def project(k, count, place, piece, weight, bias, earlier):
    rows, width = piece.shape
    cols = weight.shape[1]
    slot = (count - k) % count
    tile = rows // 2
    alias = earlier is not None
    return pl.pallas_call(
        functools.partial(project_kernel, slot),
        grid_spec=pltpu.PrefetchScalarGridSpec(
            num_scalar_prefetch=1,
            grid=(2,),
            in_specs=[
                pl.BlockSpec((tile, width), lambda i, p: (i, 0)),
                pl.BlockSpec((width, cols), lambda i, p: (0, 0)),
                pl.BlockSpec((1, cols), lambda i, p: (0, 0)),
            ]
            + ([ANY, ANY] if alias else []),
            out_specs=[
                pl.BlockSpec((tile, cols), lambda i, p: (2 * lax.rem(p[0] + slot, count) + i, 0)),
                pl.BlockSpec((width, tile), lambda i, p: (0, 2 * slot + i)),
            ],
        ),
        out_shape=[
            jax.ShapeDtypeStruct((count * rows, cols), BF16),
            jax.ShapeDtypeStruct((width, count * rows), BF16),
        ],
        input_output_aliases={4: 0, 5: 1} if alias else {},
        cost_estimate=light(4 * rows * width, 2 * rows * width * cols),
        name="project",
    )(place, piece, weight, bias, *(earlier if alias else ()))


def turn_kernel(own_ref, got_ref, out_ref):
    rows = own_ref.shape[0]
    out_ref[:, :rows] = own_ref[...].T
    out_ref[:, rows:] = got_ref[...].T


def turn_rows(own, got):
    rows, width = own.shape
    tile = width // 4
    return pl.pallas_call(
        turn_kernel,
        grid=(4,),
        in_specs=[pl.BlockSpec((rows, tile), lambda i: (0, i))] * 2,
        out_specs=pl.BlockSpec((tile, 2 * rows), lambda i: (i, 0)),
        out_shape=jax.ShapeDtypeStruct((width, 2 * rows), BF16),
        cost_estimate=light(8 * rows * width),
        name="turn_rows",
    )(own, got)


def wide(tile):
    lane = lax.broadcasted_iota(jnp.int32, tile.shape, 1)
    zero = jnp.zeros_like(tile)
    return jnp.concatenate(
        (jnp.where(lane < HEAD, tile, zero), jnp.where(lane < HEAD, zero, tile)), axis=0
    )


def both(row):
    return jnp.concatenate((row, row), axis=1)


def heads_of(acc):
    return jnp.concatenate((acc[:HEAD, :TILE], acc[HEAD:, TILE:]), axis=0)


def mask_rows(start_ref, step, shift):
    start = both(start_ref[...] - shift)
    place = both((step + 4) * TILE + lax.broadcasted_iota(jnp.int32, (1, TILE), 1))
    return start, place


def allowed(tile_index, start, place):
    key = tile_index * TILE + lax.broadcasted_iota(jnp.int32, (TILE, 2 * TILE), 0)
    return (key >= start) & (key <= place)


def turn(tile, meta_ref, tiles, per, count):
    block = tile // per
    return per * lax.rem(block - meta_ref[tiles] + count, count) + lax.rem(tile, per)


def attend_kernel(base, shift, meta_ref, start_ref, q_ref, k_ref, v_ref, *rest):
    o_ref, turned_ref, log_ref, acc_ref = rest[-4:]
    step = pl.program_id(0)
    query = wide(q_ref[...] * jnp.asarray(SCALE, BF16))
    start, place = mask_rows(start_ref, step, shift)
    acc_ref[...] = jnp.zeros_like(acc_ref)

    def body(j, carried):
        top, total = carried
        rows = pl.ds(pl.multiple_of(j * TILE, TILE), TILE)
        scores = nt(k_ref[rows, :], query)
        scores = jnp.where(allowed(j, start, place), scores, -1e30)
        new_top = jnp.maximum(top, jnp.max(scores, axis=0, keepdims=True))
        part = jnp.exp(scores - new_top)
        factor = jnp.exp(top - new_top)
        total = total * factor + jnp.sum(part, axis=0, keepdims=True)
        acc_ref[...] = acc_ref[...] * factor + tn(v_ref[rows, :], part.astype(BF16))
        return new_top, total

    top, total = lax.fori_loop(
        meta_ref[base + step] - shift // TILE,
        step + 5,
        body,
        (jnp.full((1, 2 * TILE), -1e30, F32), jnp.zeros((1, 2 * TILE), F32)),
    )
    turned = heads_of(acc_ref[...] / total)
    turned_ref[...] = turned
    o_ref[...] = turned.T.astype(BF16)
    logs = top + jnp.log(total)
    log_ref[0:1, :] = logs[:, :TILE]
    log_ref[1:2, :] = logs[:, TILE:]


def attend(base, shift, meta, start, q, qcol, k, kcol, v, vcol, earlier, tokens, count):
    n = k.shape[0]
    steps = (n - DOC_MAX) // TILE
    tiles = tokens // TILE
    per = tiles // count
    alias = earlier is not None
    specs = [
        pl.BlockSpec((1, TILE), lambda i, m: (0, base + i)),
        pl.BlockSpec((TILE, PAIR), lambda i, m: (base + i, qcol)),
        pl.BlockSpec((n, PAIR), lambda i, m: (0, kcol)),
        pl.BlockSpec((n, PAIR), lambda i, m: (0, vcol)),
    ] + [ANY] * (3 if alias else 0)
    return pl.pallas_call(
        functools.partial(attend_kernel, base, shift),
        grid_spec=pltpu.PrefetchScalarGridSpec(
            num_scalar_prefetch=1,
            grid=(steps,),
            in_specs=specs,
            out_specs=[
                pl.BlockSpec((TILE, PAIR), lambda i, m: (turn(base + i, m, tiles, per, count), 0)),
                pl.BlockSpec((PAIR, TILE), lambda i, m: (0, base + i)),
                pl.BlockSpec((8, TILE), lambda i, m: (0, base + i)),
            ],
            scratch_shapes=[pltpu.VMEM((PAIR, 2 * TILE), F32)],
        ),
        out_shape=[
            jax.ShapeDtypeStruct((tokens, PAIR), BF16),
            jax.ShapeDtypeStruct((PAIR, tokens), F32),
            jax.ShapeDtypeStruct((8, tokens), F32),
        ],
        input_output_aliases={5: 0, 6: 1, 7: 2} if alias else {},
        cost_estimate=light(4 * n * PAIR),
        name="attend",
    )(meta, start, q, k, v, *(earlier if alias else ()))


def back_tile(shift, low, start_ref, q_ref, k_ref, v_ref, do_ref, turned_ref, log_ref, dk_ref, dv_ref, acc_ref):
    step = pl.program_id(0)
    query = wide(q_ref[...] * jnp.asarray(SCALE, BF16))
    out_back = wide(do_ref[...])
    start, place = mask_rows(start_ref, step, shift)
    product = do_ref[...].astype(F32).T * turned_ref[...]
    delta = jnp.concatenate(
        (
            jnp.sum(product[:HEAD], axis=0, keepdims=True),
            jnp.sum(product[HEAD:], axis=0, keepdims=True),
        ),
        axis=1,
    )
    logs = jnp.concatenate((log_ref[0:1, :], log_ref[1:2, :]), axis=1)
    acc_ref[...] = jnp.zeros_like(acc_ref)

    def body(j, carried):
        rows = pl.ds(pl.multiple_of(j * TILE, TILE), TILE)
        key_tile = k_ref[rows, :]
        scores = jnp.where(allowed(j, start, place), nt(key_tile, query), -1e30)
        prob = jnp.exp(scores - logs)
        prob_back = nt(v_ref[rows, :], out_back)
        score_back = (prob * (prob_back - delta)).astype(BF16)
        dv_ref[rows, :] += nn(prob.astype(BF16), out_back)
        dk_ref[rows, :] += nn(score_back, query)
        acc_ref[...] += tn(key_tile, score_back)
        return carried

    lax.fori_loop(low, step + 5, body, 0)
    return (heads_of(acc_ref[...]) * SCALE).T.astype(BF16)


def early_kernel(meta_ref, start_ref, q_ref, k_ref, v_ref, do_ref, turned_ref, log_ref, dq_ref, gone_ref, dk_ref, dv_ref, kept_k, kept_v, acc_ref):
    step = pl.program_id(0)

    @pl.when(step == 0)
    def _():
        kept_k[...] = jnp.zeros_like(kept_k)
        kept_v[...] = jnp.zeros_like(kept_v)

    dq_ref[...] = back_tile(
        0, meta_ref[step], start_ref, q_ref, k_ref, v_ref, do_ref, turned_ref, log_ref,
        kept_k, kept_v, acc_ref,
    )

    @pl.when(step == pl.num_programs(0) - 1)
    def _():
        gone_ref[:, :PAIR] = kept_k[:DOC_MAX, :].astype(BF16)
        gone_ref[:, PAIR:] = kept_v[:DOC_MAX, :].astype(BF16)
        dk_ref[...] = kept_k[DOC_MAX:, :]
        dv_ref[...] = kept_v[DOC_MAX:, :]


def late_kernel(base, fresh, per, count, meta_ref, start_ref, q_ref, k_ref, v_ref, do_ref, turned_ref, log_ref, dq_in, dk_in, dv_in, back_ref, packed_ref, value_ref, sums_ref, kept_k, kept_v, acc_ref):
    step = pl.program_id(0)
    held = dk_in.shape[0]
    tiles = packed_ref.shape[0] // TILE

    def rows_of(tile):
        row = turn(tile, meta_ref, tiles, per, count) * TILE
        return pl.ds(pl.multiple_of(row, TILE), TILE)

    @pl.when(step == 0)
    def _():
        kept_k[:held, :] = dk_in[...]
        kept_v[:held, :] = dv_in[...]
        kept_k[held:, :] = back_ref[:, :PAIR].astype(F32)
        kept_v[held:, :] = back_ref[:, PAIR:].astype(F32)
        for i in range(base):
            packed_ref[rows_of(i), :PAIR] = dq_in[i * TILE : (i + 1) * TILE, :]

    packed_ref[rows_of(base + step), :PAIR] = back_tile(
        DOC_MAX, meta_ref[base + step] - DOC_MAX // TILE, start_ref, q_ref, k_ref, v_ref, do_ref,
        turned_ref, log_ref, kept_k, kept_v, acc_ref,
    )

    @pl.when(step == pl.num_programs(0) - 1)
    def _():
        for i in range(tiles):
            span = slice(i * TILE, (i + 1) * TILE)
            packed_ref[rows_of(i), PAIR : 2 * PAIR] = kept_k[span, :].astype(BF16)
            if fresh:
                packed_ref[rows_of(i), 2 * PAIR :] = kept_v[span, :].astype(BF16)
        if not fresh:
            value_ref[...] = kept_v[...]
        else:
            value_ref[...] = jnp.zeros_like(value_ref)
        sums_ref[...] = jnp.broadcast_to(
            jnp.sum(packed_ref[...].astype(F32), axis=0, keepdims=True), sums_ref.shape
        )


def back_specs(base, qcol, n, kcol, vcol, tiles, per, count):
    return [
        pl.BlockSpec((1, TILE), lambda i, m: (0, base + i)),
        pl.BlockSpec((TILE, PAIR), lambda i, m: (base + i, qcol)),
        pl.BlockSpec((n, PAIR), lambda i, m: (0, kcol)),
        pl.BlockSpec((n, PAIR), lambda i, m: (0, vcol)),
        pl.BlockSpec((TILE, PAIR), lambda i, m: (turn(base + i, m, tiles, per, count), 0)),
        pl.BlockSpec((PAIR, TILE), lambda i, m: (0, base + i)),
        pl.BlockSpec((8, TILE), lambda i, m: (0, base + i)),
    ]


def whole(shape):
    return pl.BlockSpec(shape, lambda i, m: (0,) * len(shape))


def back_early(meta, start, q, qcol, k, kcol, v, vcol, do, turned, logs, tokens, count):
    n = k.shape[0]
    held = n - DOC_MAX
    tiles = tokens // TILE
    return pl.pallas_call(
        early_kernel,
        grid_spec=pltpu.PrefetchScalarGridSpec(
            num_scalar_prefetch=1,
            grid=(held // TILE,),
            in_specs=back_specs(0, qcol, n, kcol, vcol, tiles, tiles // count, count),
            out_specs=[
                pl.BlockSpec((TILE, PAIR), lambda i, m: (i, 0)),
                whole((DOC_MAX, 2 * PAIR)),
                whole((held, PAIR)),
                whole((held, PAIR)),
            ],
            scratch_shapes=[
                pltpu.VMEM((n, PAIR), F32),
                pltpu.VMEM((n, PAIR), F32),
                pltpu.VMEM((PAIR, 2 * TILE), F32),
            ],
        ),
        out_shape=[
            jax.ShapeDtypeStruct((held, PAIR), BF16),
            jax.ShapeDtypeStruct((DOC_MAX, 2 * PAIR), BF16),
            jax.ShapeDtypeStruct((held, PAIR), F32),
            jax.ShapeDtypeStruct((held, PAIR), F32),
        ],
        cost_estimate=light(12 * n * PAIR),
        name="back_early",
    )(meta, start, q, k, v, do, turned, logs)


def back_late(meta, start, q, qcol, k, kcol, v, vcol, do, turned, logs, dq, dk, dv, back, fresh, tokens, count):
    n = k.shape[0]
    held = n - DOC_MAX
    tiles = tokens // TILE
    per = tiles // count
    base = (tokens - held) // TILE
    cols = (3 if fresh else 2) * PAIR
    return pl.pallas_call(
        functools.partial(late_kernel, base, fresh, per, count),
        grid_spec=pltpu.PrefetchScalarGridSpec(
            num_scalar_prefetch=1,
            grid=(held // TILE,),
            in_specs=back_specs(base, qcol, n, kcol, vcol, tiles, per, count)
            + [whole(dq.shape), whole(dk.shape), whole(dv.shape), whole(back.shape)],
            out_specs=[
                whole((tokens, cols)),
                whole((8, PAIR) if fresh else (tokens, PAIR)),
                whole((8, cols)),
            ],
            scratch_shapes=[
                pltpu.VMEM((n, PAIR), F32),
                pltpu.VMEM((n, PAIR), F32),
                pltpu.VMEM((PAIR, 2 * TILE), F32),
            ],
        ),
        out_shape=[
            jax.ShapeDtypeStruct((tokens, cols), BF16),
            jax.ShapeDtypeStruct((8, PAIR) if fresh else (tokens, PAIR), F32),
            jax.ShapeDtypeStruct((8, cols), F32),
        ],
        cost_estimate=light(12 * n * PAIR),
        name="back_late",
    )(meta, start, q, k, v, do, turned, logs, dq, dk, dv, back)


def store_grad(grad_ref, grad):
    runs, _, lanes, rows, cols = grad_ref.shape
    for j in range(lanes):
        grad_ref[:, 0, j] = grad[:, j * cols : (j + 1) * cols].reshape(runs, rows, cols)


def accumulate(ref, value):
    @pl.when(pl.program_id(0) == 0)
    def _():
        ref[...] = value

    @pl.when(pl.program_id(0) > 0)
    def _():
        ref[...] += value


def up_kernel(places_ref, sn_ref, got_ref, cot_ref, up_ref, bias_ref, down_ref, out_ref, other_ref, slope_ref, grad_ref, act_ref):
    width = up_ref.shape[0] * up_ref.shape[1]
    rows = sn_ref.shape[0]
    up = up_ref[...].reshape(width, UNIT)
    down = down_ref[...].reshape(UNIT, width)
    for i, (piece_ref, sum_ref) in enumerate(((sn_ref, out_ref), (got_ref, other_ref))):
        span = slice(i * rows, (i + 1) * rows)
        hidden = nn(piece_ref[...], up) + bias_ref[0]
        square = hidden * hidden
        curve = jnp.tanh(GELU_A * (hidden + GELU_B * (hidden * square)))
        half = 0.5 * (1.0 + curve)
        activated = (hidden * half).astype(BF16)
        slope_ref[span, :] = half + 0.5 * hidden * (1.0 - curve * curve) * (
            GELU_A * (1.0 + 3.0 * GELU_B * square)
        )
        act_ref[span, :] = activated
        accumulate(sum_ref, nn(activated, down))
    store_grad(grad_ref, nn(cot_ref[...], act_ref[...]).astype(BF16))


def feed_specs(gathered, seq, parts, width):
    part = width // seq
    per = width // UNIT
    run = seq // 2

    def spot(i, p):
        return lax.rem(p[0] + i, parts)

    grad_spec = pl.BlockSpec(
        (run, 1, UNIT // PAIR, width // run, PAIR), lambda i, p: (0, i, 0, 0, 0)
    )

    grad = (run, parts, UNIT // PAIR, width // run, PAIR)
    return (
        pl.BlockSpec((seq, part, UNIT), lambda i, p: (spot(i, p), 0, p[1])),
        pl.BlockSpec((UNIT // part, part, width), lambda i, p: (spot(i, p) * per + p[1], 1, 0)),
        grad_spec,
        grad,
    )


def fixed(shape):
    return pl.BlockSpec(shape, lambda i, p: (0,) * len(shape))


def feed_up(places, sn, got, cot_turned, gathered, bias, seq, parts):
    rows, width = sn.shape
    up_spec, down_spec, grad_spec, grad = feed_specs(gathered, seq, parts, width)
    return pl.pallas_call(
        up_kernel,
        grid_spec=pltpu.PrefetchScalarGridSpec(
            num_scalar_prefetch=1,
            grid=(parts,),
            in_specs=[
                fixed((rows, width)),
                fixed((rows, width)),
                fixed((width, 2 * rows)),
                up_spec,
                pl.BlockSpec((1, 1, UNIT), lambda i, p: (lax.rem(parts - i, parts), 0, p[1])),
                down_spec,
            ],
            out_specs=[
                fixed((rows, width)),
                fixed((rows, width)),
                pl.BlockSpec((2 * rows, UNIT), lambda i, p: (0, i)),
                grad_spec,
            ],
            scratch_shapes=[pltpu.VMEM((2 * rows, UNIT), BF16)],
        ),
        out_shape=[
            jax.ShapeDtypeStruct((rows, width), F32),
            jax.ShapeDtypeStruct((rows, width), F32),
            jax.ShapeDtypeStruct((2 * rows, parts * UNIT), F32),
            jax.ShapeDtypeStruct(grad, BF16),
        ],
        cost_estimate=light(16 * rows * width, 24 * rows * width * width),
        name="feed_up",
    )(places, sn, got, cot_turned, gathered, bias, gathered)


def down_kernel(places_ref, cot_ref, cot_got_ref, sn_ref, got_ref, slope_ref, up_ref, down_ref, back_ref, other_ref, grad_ref, bias_ref, turned_ref, hidden_ref):
    width = up_ref.shape[0] * up_ref.shape[1]
    rows = sn_ref.shape[0]

    @pl.when(pl.program_id(0) == 0)
    def _():
        turned_ref[:, :rows] = sn_ref[...].T
        turned_ref[:, rows:] = got_ref[...].T

    up = up_ref[...].reshape(width, UNIT)
    down = down_ref[...].reshape(UNIT, width)
    total = jnp.zeros((1, UNIT), F32)
    for i, (piece_ref, sum_ref) in enumerate(((cot_ref, back_ref), (cot_got_ref, other_ref))):
        span = slice(i * rows, (i + 1) * rows)
        rounded = (nt(piece_ref[...], down) * slope_ref[span, :]).astype(BF16)
        total = total + jnp.sum(rounded.astype(F32), axis=0, keepdims=True)
        hidden_ref[span, :] = rounded
        accumulate(sum_ref, nt(rounded, up))
    bias_ref[0] = total
    store_grad(grad_ref, nn(turned_ref[...], hidden_ref[...]).astype(BF16))


def feed_down(places, cot, cot_got, sn, got, slope, gathered, seq, parts, extra):
    rows, width = cot.shape
    up_spec, down_spec, grad_spec, grad = feed_specs(gathered, seq, parts, width)
    return pl.pallas_call(
        down_kernel,
        grid_spec=pltpu.PrefetchScalarGridSpec(
            num_scalar_prefetch=1,
            grid=(parts,),
            in_specs=[fixed((rows, width))] * 4
            + [
                pl.BlockSpec((2 * rows, UNIT), lambda i, p: (0, i)),
                up_spec,
                down_spec,
            ],
            out_specs=[
                fixed((rows, width)),
                fixed((rows, width)),
                grad_spec,
                pl.BlockSpec((1, 1, UNIT), lambda i, p: (i, 0, 0)),
            ],
            scratch_shapes=[
                pltpu.VMEM((width, 2 * rows), BF16),
                pltpu.VMEM((2 * rows, UNIT), BF16),
            ],
        ),
        out_shape=[
            jax.ShapeDtypeStruct((rows, width), F32),
            jax.ShapeDtypeStruct((rows, width), F32),
            jax.ShapeDtypeStruct(grad[:2] + (grad[2] + extra,) + grad[3:], BF16),
            jax.ShapeDtypeStruct((parts, 1, UNIT), F32),
        ],
        cost_estimate=light(16 * rows * width, 24 * rows * width * width),
        name="feed_down",
    )(places, cot, cot_got, sn, got, slope, gathered, gathered)


def back_norm_kernel(own_ref, came_ref, cot_ref, hat_ref, inverse_ref, gain_ref, mixing_ref, mixed_ref, grads_ref, middle_ref, attended_ref, sums_ref, grad_ref, wide_ref):
    step = pl.program_id(0)
    back = own_ref[...] + came_ref[...]
    hat = hat_ref[...]
    cot = cot_ref[...].astype(F32)
    middle_back = cot + norm_back(back, gain_ref[...], hat, inverse_ref[...])
    rounded = middle_back.astype(BF16)
    middle_ref[...] = middle_back
    attended = nt(rounded, mixing_ref[...]).astype(BF16)
    for j in range(attended_ref.shape[0]):
        attended_ref[j] = attended[:, j * PAIR : (j + 1) * PAIR]
    accumulate(wide_ref, nn(rounded.T, mixed_ref[...]))

    @pl.when(step == 0)
    def _():
        sums_ref[...] = jnp.zeros_like(sums_ref)

    for i, value in enumerate((back * hat, back, middle_back, cot)):
        sums_ref[i : i + 1, :] += jnp.sum(value, axis=0, keepdims=True)

    @pl.when(step == pl.num_programs(0) - 1)
    def _():
        runs, parts, lanes, rows, cols = grad_ref.shape
        for k in range(parts):
            for j in range(lanes):
                left = (k * lanes + j) * cols
                value = wide_ref[:, left : left + cols].astype(BF16)
                grad_ref[:, (parts - k) % parts, j] = value.reshape(runs, rows, cols)


def back_norm(own, came, cot, hat, inverse, gain, mixing, mixed, grads):
    rows, width = own.shape
    blocks = mixing.shape[0] // PAIR
    runs, parts, lanes, lines, cols = grads.shape
    extra = blocks // parts
    tile = rows // 2
    row = pl.BlockSpec((tile, width), lambda i: (i, 0))
    return pl.pallas_call(
        back_norm_kernel,
        grid=(2,),
        in_specs=[
            row, row, row, row,
            pl.BlockSpec((tile, 1), lambda i: (i, 0)),
            pl.BlockSpec((1, width), lambda i: (0, 0)),
            pl.BlockSpec(mixing.shape, lambda i: (0, 0)),
            row,
            ANY,
        ],
        out_specs=[
            row,
            pl.BlockSpec((blocks, tile, PAIR), lambda i: (0, i, 0)),
            pl.BlockSpec((8, width), lambda i: (0, 0)),
            pl.BlockSpec((runs, parts, extra, lines, cols), lambda i: (0, 0, UNIT // PAIR // extra, 0, 0)),
        ],
        out_shape=[
            jax.ShapeDtypeStruct((rows, width), F32),
            jax.ShapeDtypeStruct((blocks, rows, PAIR), BF16),
            jax.ShapeDtypeStruct((8, width), F32),
            jax.ShapeDtypeStruct(grads.shape, BF16),
        ],
        input_output_aliases={8: 3},
        scratch_shapes=[pltpu.VMEM((width, width), F32)],
        cost_estimate=light(16 * rows * width, 4 * rows * width * width),
        name="back_norm",
    )(own, came, cot, hat, inverse, gain[None], mixing, mixed, grads)


def front_norm_kernel(parts, places_ref, *refs):
    pieces, (weight_ref, middle_ref, hat_ref, inverse_ref, gain_ref, out_ref) = refs[:-6], refs[-6:]
    cut = pieces[0].shape[1]
    back = jnp.zeros(out_ref.shape, F32)
    for k in range(parts):
        spot = lax.rem(places_ref[0] - k + parts, parts)
        back = back + nn(pieces[2 * k][...], weight_ref[spot, :cut, :])
        back = back + nn(pieces[2 * k + 1][...], weight_ref[spot, cut:, :])
    out_ref[...] = middle_ref[...] + norm_back(
        back, gain_ref[...], hat_ref[...], inverse_ref[...]
    )


def front_norm(places, pieces, weight, middle, hat, inverse, gain):
    rows, width = middle.shape
    parts = weight.shape[0]
    tile = rows // 4

    def row(cols):
        return pl.BlockSpec((tile, cols), lambda i, p: (i, 0))

    return pl.pallas_call(
        functools.partial(front_norm_kernel, parts),
        grid_spec=pltpu.PrefetchScalarGridSpec(
            num_scalar_prefetch=1,
            grid=(4,),
            in_specs=[row(piece.shape[1]) for piece in pieces]
            + [fixed(weight.shape), row(width), row(width), row(1), fixed((1, width))],
            out_specs=row(width),
        ),
        out_shape=jax.ShapeDtypeStruct((rows, width), F32),
        cost_estimate=light(16 * rows * width, 2 * rows * width * weight.shape[0] * weight.shape[1]),
        name="front_norm",
    )(places, *pieces, weight, middle, hat, inverse, gain[None])


def around(value, steps):
    count = lax.axis_size("tp")
    return lax.ppermute(value, "tp", [(i, (i + steps) % count) for i in range(count)])


def flipped(value, axis, bit):
    count = lax.axis_size(axis)
    return lax.ppermute(value, axis, [(i, i ^ bit) for i in range(count)])


def along(value, steps):
    count = lax.axis_size(SEQ)
    first, last = max(0, -steps), min(count, count - steps)
    return lax.ppermute(value, SEQ, [(i, i + steps) for i in range(first, last)])


def butterfly(value, axis):
    bit = 1
    while bit < lax.axis_size(axis):
        value = value + flipped(value, axis, bit)
        bit *= 2
    return value


def pick(value, index, dim):
    return lax.dynamic_index_in_dim(value, index, dim, keepdims=False)


def joined(a, b):
    return (a.astype(F32) + b.astype(F32)).astype(BF16)


def seq_bits():
    bits, bit = [], 1
    while bit < lax.axis_size(SEQ):
        bits.append(bit)
        bit *= 2
    return bits


def tied(*groups):
    return lax.optimization_barrier(groups)


class Scatter:
    def __init__(self, value, place):
        self.place = place
        self.bits = seq_bits()
        self.left = value.reshape((2,) * len(self.bits) + value.shape[1:])
        self.issue()

    def issue(self):
        bit = self.bits.pop(0)
        dim = len(self.bits)
        mine = (self.place // bit) % 2
        self.parts = (
            pick(self.left, mine, dim), flipped(pick(self.left, 1 - mine, dim), SEQ, bit)
        )

    def merge(self):
        self.left = joined(*self.parts)
        if self.bits:
            self.issue()
            return True
        return False

    def result(self):
        while self.merge():
            pass
        return self.left


def in_order(own, other, bit, place, dim):
    low = (place // bit) % 2 == 0
    return jnp.stack((jnp.where(low, own, other), jnp.where(low, other, own)), axis=dim)


def quarter(shard, place):
    size = shard.shape[0] // 4
    spot = 2 * ((place // 2) % 2) + place % 2
    return lax.dynamic_slice_in_dim(shard, spot * size, size, 0)


def from_shards(piece):
    return [around(piece, k) for k in range(1, lax.axis_size("tp"))]


def center(rows):
    average = jnp.mean(rows, axis=-1, keepdims=True)
    centered = rows - average
    inverse = lax.rsqrt(jnp.mean(centered * centered, axis=-1, keepdims=True) + EPSILON)
    return centered * inverse, inverse


def norm_back(grad, gain, xhat, inverse):
    e = grad * gain
    return inverse * (
        e
        - jnp.mean(e, axis=-1, keepdims=True)
        - xhat * jnp.mean(e * xhat, axis=-1, keepdims=True)
    )


def local(
    stream, segments, skip_values, first_gain, first_shift, query_weight, query_bias, key_weight,
    value_weight, value_bias, mixing_weight, mixing_bias, second_gain, second_shift, up_weight,
    up_bias, down_weight, down_bias, cotangent,
):
    rows, width = stream.shape
    tokens = skip_values.shape[0]
    own = query_weight.shape[1]
    tp = lax.axis_size("tp")
    seq = lax.axis_size(SEQ)
    seq_place = lax.axis_index(SEQ)
    tp_place = lax.axis_index("tp")
    core = lax.axis_index("core")
    places = jnp.stack((tp_place, core)).astype(jnp.int32)
    half = tokens - DOC_MAX
    part = width // seq
    kcol = own // PAIR

    stream_wide = stream.astype(F32)
    first_hat, first_inverse = center(stream_wide)
    piece = (first_hat * first_gain + first_shift).astype(BF16)
    piece, up_weight, down_weight, mixing_weight, segments, cotangent = lax.optimization_barrier(
        (piece, up_weight, down_weight, mixing_weight, segments, cotangent)
    )

    def own_rows(shard):
        size = shard.shape[0] // seq
        return lax.dynamic_slice_in_dim(shard, seq_place * size, size, 0)

    qkv_turned = jnp.concatenate(
        (
            query_weight[:, :PAIR], key_weight[:, :PAIR], value_weight,
            query_weight[:, PAIR:], key_weight[:, PAIR:],
        ),
        axis=1,
    ).T
    packet = jnp.concatenate([own_rows(w) for w in (up_weight, down_weight)], axis=0)
    qkv_packet = own_rows(qkv_turned)
    bias_pieces = jnp.stack([up_bias] + [around(up_bias, k) for k in range(1, tp)])[:, None]
    cot_got = flipped(cotangent, "core", 1)

    padded = jnp.concatenate((jnp.full((DOC_MAX,), -1, jnp.int32), segments))
    window = lax.dynamic_slice_in_dim(padded, seq_place * tokens, DOC_MAX + tokens, 0)
    start = jnp.sum(
        (window[:, None] < window[None, DOC_MAX:]).astype(jnp.int32), axis=0, keepdims=True
    )
    meta = jnp.concatenate((start[0, ::TILE] // TILE, places))
    halo_skip = along(skip_values[half:], 1)
    wqkv = jnp.concatenate((query_weight, key_weight, value_weight), axis=1)
    bias = jnp.concatenate((query_bias, jnp.zeros((own,), F32), value_bias))[None]
    made = None
    for k in range(tp):
        if k == tp - 1:
            piece, meta, start, bias_pieces, cot_got, mixing_piece = tied(
                piece, meta, start, bias_pieces, cot_got, quarter(mixing_weight, seq_place)
            )
        elif k > 0:
            piece, made = tied(piece, made)
        ahead = around(piece, 1) if k < tp - 1 else None
        made = project(k, tp, places, piece, wqkv, bias, made)
        piece = ahead
        if k == GATHER_STEP:
            piece, packet = tied(piece, packet)
            gathered = lax.all_gather(packet, ("tp",) + SEQ, axis=0, tiled=False)
    qkv, normed_turned = made
    halo = along(qkv[half:, own:], 1)
    qkv, mixing_piece = tied(qkv, mixing_piece)
    mixing_got = from_shards(mixing_piece)
    early = early_skip = None

    def values_of(pair):
        if pair == 0:
            return (qkv, 2 * kcol), (early, kcol)
        return (skip_values, 0), (early_skip, 0)

    steps = half // TILE
    attended = []
    for pair in range(2):
        (v, vcol), _ = values_of(pair)
        attended.append(
            attend(steps, DOC_MAX, meta, start, qkv, pair, qkv, kcol + pair, v, vcol, None, tokens, tp)
        )
    attended, halo, halo_skip, mixing_got = tied(attended, halo, halo_skip, mixing_got)
    early_skip = jnp.concatenate((halo_skip, skip_values[:half]), axis=0)
    early = jnp.concatenate((halo, qkv[:half, own:]), axis=0)
    mixing_got = jnp.stack(mixing_got)
    mixing_other = flipped(mixing_got, SEQ, 2)
    arrived = []
    for pair in range(2):
        _, (v, vcol) = values_of(pair)
        attended[pair] = attend(
            0, 0, meta, start, qkv, pair, early, pair, v, vcol, attended[pair], tokens, tp
        )
        blocks = attended[pair][0].reshape(tp, rows, PAIR)
        arrived.append([blocks[0]] + [around(blocks[k], k) for k in range(1, tp)])
    attended[1], mixing_got, mixing_other, cotangent, cot_got = tied(
        attended[1], mixing_got, mixing_other, cotangent, cot_got
    )
    mixing_got = in_order(mixing_got, mixing_other, 2, seq_place, 1)
    mixing_other = flipped(mixing_got, "core", 1)
    cot_turned = turn_rows(cotangent, cot_got)
    mixing_rot = in_order(mixing_got, mixing_other, 1, seq_place, 2).reshape(-1, width)
    mixing_rot = jnp.concatenate((mixing_weight, mixing_rot), axis=0)
    arrived, mixing_rot, cot_turned = tied(arrived, mixing_rot, cot_turned)

    mixed_in = jnp.concatenate([arrived[pair][k] for k in range(tp) for pair in range(2)], axis=1)
    middle = stream_wide + nn(mixed_in, mixing_rot) + mixing_bias
    second_hat, second_inverse = center(middle)
    second = (second_hat * second_gain + second_shift).astype(BF16)

    got = flipped(second, "core", 1)
    got, qkv_packet = tied(got, qkv_packet)
    qkv_full = lax.all_gather(qkv_packet, ("tp",) + SEQ, axis=0, tiled=False)
    qkv_full = qkv_full.reshape(tp, -1, width)
    lost, lost_other, slope, down_grads = feed_up(
        places, second, got, cot_turned, gathered, bias_pieces, seq, tp
    )

    def over_runs(grads):
        flat = grads.reshape(grads.shape[0], -1, PAIR)
        flat = lax.psum_scatter(flat, "run", scatter_dimension=0, tiled=True)
        return flat.reshape(grads.shape[1:])

    def over_shards(grads):
        return [grads[0]] + [around(grads[k], k) for k in range(1, tp)]

    down_grads = over_runs(down_grads)
    back_own, back_other, up_grads, up_bias_grad = feed_down(
        places, cotangent, cot_got, second, got, slope, gathered, seq, tp, UNIT // PAIR
    )
    back_came = flipped(back_other, "core", 1)
    middle_back, attended_back, norm_sums, up_grads = back_norm(
        back_own, back_came, cotangent, second_hat, second_inverse, second_gain, mixing_rot,
        mixed_in, up_grads,
    )
    up_grads = over_runs(up_grads)[:, : (UNIT + own) // PAIR]

    def send_back(pair):
        return [attended_back[pair]] + [
            around(attended_back[2 * k + pair], -k) for k in range(1, tp)
        ]

    moved = send_back(0)
    moved, attended_back, lost_other, qkv_full = tied(moved, attended_back, lost_other, qkv_full)
    returned = [jnp.concatenate(moved, axis=0)]
    moved = send_back(1)
    lost_came = flipped(lost_other, "core", 1)

    halves = []
    for pair in range(2):
        _, (v, vcol) = values_of(pair)
        _, turned, logs = attended[pair]
        dq, gone, dk, dv = back_early(
            meta, start, qkv, pair, early, pair, v, vcol, returned[pair], turned, logs, tokens, tp
        )
        halves.append((dq, dk, dv, along(gone, -1)))
        if pair == 0:
            dq, moved, lost_came = tied(dq, moved, lost_came)
            returned.append(jnp.concatenate(moved, axis=0))
    halves, norm_sums, up_bias_grad = tied(halves, norm_sums, up_bias_grad)
    halves = [list(group) for group in halves]
    made_here = [pick(up_bias_grad.reshape(tp, UNIT), (k - tp_place) % tp, 0) for k in range(tp)]
    made_here = jnp.stack(made_here).reshape(tp, 1, -1, PAIR)
    which = lax.broadcasted_iota(jnp.int32, (tp, 2) + made_here.shape[2:], 1)
    early_sums = jnp.concatenate(
        (
            norm_sums[:4].reshape(-1, PAIR),
            jnp.where(which == core, made_here, 0.0).reshape(-1, PAIR),
        ),
        axis=0,
    )
    packets, column_sums, pieces = [], [], []
    skip_gradient = None
    for pair in range(2):
        (v, vcol), _ = values_of(pair)
        _, turned, logs = attended[pair]
        packed, values, sums = back_late(
            meta, start, qkv, pair, qkv, kcol + pair, v, vcol, returned[pair], turned, logs,
            *halves[pair], pair == 0, tokens, tp,
        )
        blocks = packed.reshape(tp, rows, packed.shape[1])
        pieces.append([blocks[0]] + [around(blocks[k], k) for k in range(1, tp)])
        if pair == 0:
            halves[1], packed, down_grads = tied(halves[1], packed, down_grads)
            down_grads = over_shards(down_grads)
        else:
            skip_gradient = values
        packets.append(packed)
        column_sums.append(sums[0])
    packets, pieces[0], middle = tied(packets, pieces[0], middle)
    output = (middle + (lost + lost_came) + down_bias).astype(BF16)
    wide_grad = nn(normed_turned, jnp.concatenate(packets, axis=1))
    weight_sum = Scatter(wide_grad.astype(BF16).reshape(seq, part, -1), seq_place)
    column_sum = jnp.concatenate(column_sums)
    columns = qkv_turned.T.astype(F32)
    first_shift_part = jnp.sum(columns * column_sum, axis=1)
    hat_grad = (wide_grad - first_shift[:, None] * column_sum) / first_gain[:, None]
    first_gain_part = jnp.sum(columns * hat_grad, axis=1)

    def widen(value):
        size = value.shape[0]
        return lax.dynamic_update_slice_in_dim(
            jnp.zeros((size * tp,), F32), value, tp_place * size, 0
        )

    query_part = jnp.concatenate((column_sum[:PAIR], column_sum[3 * PAIR : 4 * PAIR]))
    late_sums = (
        first_gain_part, first_shift_part, widen(query_part),
        widen(column_sum[2 * PAIR : 3 * PAIR]),
    )
    late_sums = [value.reshape(-1, PAIR) for value in late_sums]
    sums = jnp.concatenate(late_sums + [early_sums], axis=0)
    pieces[1], weight_sum.parts, up_grads, sums = tied(
        pieces[1], weight_sum.parts, up_grads, sums
    )
    up_grads = over_shards(up_grads)
    weight_sum.merge()
    stream_gradient = front_norm(
        places, [pieces[pair][k] for k in range(tp) for pair in range(2)], qkv_full, middle_back,
        first_hat, first_inverse, first_gain,
    )
    for spot, bit in enumerate(seq_bits()):
        if spot + 1 < tp:
            sums, down_grads[spot + 1] = tied(sums, down_grads[spot + 1])
        sums = sums + flipped(sums, SEQ, bit)
    sums = butterfly(sums, "tp")
    weight_grad = weight_sum.result().astype(F32)

    def both_cores(blocks):
        cut = sum(block.astype(F32) for block in blocks)
        cut = cut.reshape(cut.shape[0], 2, part, PAIR)
        kept = pick(cut, core, 1)
        came = flipped(pick(cut, 1 - core, 1), "core", 1)
        lanes = UNIT // PAIR
        return jnp.concatenate(
            (
                jnp.where(core == 0, kept[:lanes], came[:lanes]),
                jnp.where(core == 0, came[:lanes], kept[:lanes]),
            ),
            axis=0,
        ), kept[lanes:] + came[lanes:]

    down_gradient = both_cores(down_grads)[0].transpose(0, 2, 1).reshape(-1, part)
    up_gradient, mixing_gradient = both_cores(up_grads)
    up_gradient = up_gradient.transpose(1, 0, 2).reshape(part, -1)
    mixing_gradient = mixing_gradient.transpose(0, 2, 1).reshape(-1, part)

    query_gradient = jnp.concatenate(
        (weight_grad[:, :PAIR], weight_grad[:, 3 * PAIR : 4 * PAIR]), axis=1
    )
    key_gradient = jnp.concatenate(
        (weight_grad[:, PAIR : 2 * PAIR], weight_grad[:, 4 * PAIR :]), axis=1
    )
    value_gradient = weight_grad[:, 2 * PAIR : 3 * PAIR]

    cuts = []
    for size in (width, width, width, width // 2) + (width,) * 4 + (tp * width,):
        cuts.append(sums[: size // PAIR].reshape(-1))
        sums = sums[size // PAIR :]
    (
        first_gain_grad, first_shift_grad, query_bias_grad, value_bias_grad, second_gain_grad,
        second_shift_grad, mixing_bias_grad, down_bias_grad, up_bias_grad,
    ) = cuts
    return (
        output,
        stream_gradient,
        skip_gradient,
        query_gradient,
        query_bias_grad,
        key_gradient,
        value_gradient,
        value_bias_grad,
        mixing_gradient,
        mixing_bias_grad,
        first_gain_grad,
        first_shift_grad,
        second_gain_grad,
        second_shift_grad,
        up_gradient,
        up_bias_grad,
        down_gradient,
        down_bias_grad,
    )


def solution(mesh):
    seq, tp = mesh.shape["seq"], mesh.shape["tp"]
    mesh = jax.sharding.Mesh(mesh.devices.reshape(seq // 2, 2, tp), SEQ + ("tp",))
    split = P(SEQ + ("tp",), None)
    column = P(None, "tp")
    tile = P(SEQ, "tp")
    turned = P("tp", SEQ)
    in_specs = (
        split, P(), tile, P(), P(), column, P("tp"), column, column, P("tp"),
        P("tp", None), P(), P(), P(), column, P("tp"), P("tp", None), P(), split,
    )
    out_specs = (
        split, split, tile, tile, P(), tile, tile, P(), turned, P(), P(), P(), P(), P(),
        tile, P(), turned, P(),
    )
    return jax.shard_map(local, mesh=mesh, in_specs=in_specs, out_specs=out_specs, check_vma=False)
```
